256 devices in a mesh: gx: 16 (over z, y_hi), gy: 4 (over y_lo, core), gz: 4 (over x).
Axes of the slice: x: 4, y: 4 (y_hi: 2, y_lo: 2; y = y_hi * 2 + y_lo), z: 8, core: 2. Of those that a mesh axis runs over, the one named last changes fastest.
Arguments:
- electric: float32 [3, 256, 128, 512], P(None, 'gz', 'gx', 'gy'), may hold values from -6 to 6
- magnetic: float32 [3, 256, 128, 512], P(None, 'gz', 'gx', 'gy'), may hold values from -6 to 6
- material: int32 [256, 128, 512], P('gz', 'gx', 'gy'), may hold values from 0 to 7
- layer_map: int32 [256], P('gz'), may hold values from 0 to 3
- permittivity: float32 [4, 8], replicated, may hold values from 1.5 to 5
- conductivity: float32 [4, 8], replicated, may hold values from 0.05 to 2
Outputs:
- electric_next: float32 [3, 256, 128, 512], P(None, 'gz', 'gx', 'gy')
- magnetic_next: float32 [3, 256, 128, 512], P(None, 'gz', 'gx', 'gy')
The draws below stay inside these ranges and needn't reach their ends.
All inputs are finite; a program needn't handle non-finite values.
Results may differ from the reference program's by a relative error of at most 0.0015.
Values sent between devices are 32-bit elements; how exact they have to be, the bound alone decides.
A program may use at most 64 MiB of HBM per device.

```python
import math
import jax
import jax.numpy as jnp
from jax import lax

LAYER_KINDS = 4
MATERIALS = 8
NX = 128
NY = 512
NZ = 256


def touch_ends(drawn, own_key, least, top_value):
    dims = drawn.shape
    index_at = [jax.random.randint(jax.random.fold_in(own_key, axis), (), 0, dims[axis]) for axis in range(len(dims))]
    drawn = drawn.at[tuple(index_at)].set(least)
    longest = dims.index(max(dims))
    index_at[longest] = (index_at[longest] + 1) % dims[longest]
    return drawn.at[tuple(index_at)].set(top_value)


def steps_of(stream_key, shape, split, least, largest):
    gain = 1.0
    for axis_at, parts in split:
        steps = jax.random.uniform(jax.random.fold_in(jax.random.fold_in(stream_key, 6), axis_at), (parts,), jnp.float32, least / len(split), largest / len(split))
        gain = gain * jnp.repeat(jnp.exp(steps), shape[axis_at] // parts).reshape((-1,) + (1,) * (len(shape) - 1 - axis_at))
    return gain


def bell_draw(key, dims, width, most, shards=(), dtype=jnp.bfloat16):
    values = jax.random.normal(key, dims, jnp.float32) * width
    if len(shards) > 0:
        values = steps_of(key, dims, shards, -0.22, 0.18) * values
    return jnp.clip(values, min=-most, max=most).astype(dtype)


def setup_inputs(seed: int = 0) -> dict:
    splits = jax.random.split(jax.random.key(seed), 7)
    return {
        "electric": bell_draw(splits[0], (3, NZ, NX, NY), 1.0, 6.0, ((1, 4), (2, 16), (3, 4)), jnp.float32),
        "magnetic": bell_draw(splits[1], (3, NZ, NX, NY), 1.0, 6.0, ((1, 4), (2, 16), (3, 4)), jnp.float32),
        "material": touch_ends(jax.random.randint(splits[2], (NZ, NX, NY), 0, MATERIALS), jax.random.fold_in(splits[2], 1), 0, MATERIALS - 1).astype(jnp.int32),
        "layer_map": touch_ends(jax.random.randint(splits[3], (NZ,), 0, LAYER_KINDS), jax.random.fold_in(splits[3], 1), 0, LAYER_KINDS - 1).astype(jnp.int32),
        "permittivity": jnp.clip(jnp.exp(jax.random.uniform(splits[4], (LAYER_KINDS, MATERIALS), jnp.float32, math.log(1.5), math.log(5.0))), 1.5, 5.0),
        "conductivity": jnp.clip(jnp.exp(jax.random.uniform(splits[5], (LAYER_KINDS, MATERIALS), jnp.float32, math.log(0.05), math.log(2.0))), 0.05, 2.0),
    }


time_step = 0.5
z_courant = 128.0


def forward_diff(values, along_axis):
    widths = [(0, 0), (0, 0), (0, 0)]
    widths[along_axis] = (0, 1)
    padded = jnp.pad(values, widths)
    return lax.slice_in_dim(padded, 1, values.shape[along_axis] + 1, axis=along_axis) - values


def backward_diff(values, along_axis):
    widths = [(0, 0), (0, 0), (0, 0)]
    widths[along_axis] = (1, 0)
    padded = jnp.pad(values, widths)
    return values - lax.slice_in_dim(padded, 0, values.shape[along_axis], axis=along_axis)


def second_z(values):
    return backward_diff(forward_diff(values, 0), 0)


def rates(epsilon_cell, sigma_cell):
    half_loss = 0.25 * sigma_cell / epsilon_cell
    drive_rate = 1.0 / (1.0 + half_loss)
    keep_rate = (1.0 - half_loss) * drive_rate
    curl_rate = 0.5 * drive_rate / epsilon_cell
    z_rate = z_courant * drive_rate / epsilon_cell
    stiffness = 4096.0 * drive_rate / epsilon_cell
    return keep_rate, curl_rate, z_rate, stiffness


def sweep_columns(stiffness, diagonal, sources):
    def downward(carried, inputs):
        prev_upper, prev_value = carried
        stiff_row, diag_row, source_row = inputs
        pivot_row = diag_row + stiff_row * prev_upper
        upper_ratio = -stiff_row / pivot_row
        value_row = (source_row + stiff_row[None] * prev_value) / pivot_row[None]
        return (upper_ratio, value_row), (upper_ratio, value_row)

    start_state = (jnp.zeros(stiffness.shape[1:], jnp.float32), jnp.zeros(sources.shape[1:], jnp.float32))
    unused, (uppers, values) = lax.scan(downward, start_state, (stiffness, diagonal, sources))

    def upward(following, inputs):
        upper_ratio, value_row = inputs
        result = value_row - upper_ratio[None] * following
        return result, result

    unused_last, solved = lax.scan(upward, jnp.zeros(sources.shape[1:], jnp.float32), (uppers, values), reverse=True)
    return solved


def reference(electric, magnetic, material, layer_map, permittivity, conductivity):
    epsilon_cell = permittivity[layer_map[:, None, None], material]
    sigma_cell = conductivity[layer_map[:, None, None], material]
    keep_rate, curl_rate, z_rate, stiffness = rates(epsilon_cell, sigma_cell)
    electric_x, electric_y, electric_z = electric[0], electric[1], electric[2]
    magnetic_x, magnetic_y, magnetic_z = magnetic[0], magnetic[1], magnetic[2]
    magnetic_z_new = magnetic_z - time_step * (forward_diff(electric_y, 1) - forward_diff(electric_x, 2))
    slope_zx = forward_diff(electric_z, 1)
    slope_zy = forward_diff(electric_z, 2)
    quarter_z = 0.25 * z_rate
    source_x = (keep_rate * electric_x + stiffness * second_z(electric_x)
                + curl_rate * backward_diff(magnetic_z_new, 2)
                - z_rate * backward_diff(magnetic_y, 0) - quarter_z * backward_diff(slope_zx, 0))
    source_y = (keep_rate * electric_y + stiffness * second_z(electric_y)
                + z_rate * backward_diff(magnetic_x, 0) - quarter_z * backward_diff(slope_zy, 0)
                - curl_rate * backward_diff(magnetic_z_new, 1))
    diagonal = 1.0 + 2.0 * stiffness
    diagonal = diagonal.at[0].set(1.0 + stiffness[0])
    solved = sweep_columns(stiffness, diagonal, jnp.stack([source_x, source_y], axis=1))
    electric_x_new = solved[:, 0]
    electric_y_new = solved[:, 1]
    magnetic_y_new = magnetic_y - 0.5 * z_courant * forward_diff(electric_x + electric_x_new, 0) + time_step * slope_zx
    magnetic_x_new = magnetic_x - time_step * slope_zy + 0.5 * z_courant * forward_diff(electric_y + electric_y_new, 0)
    electric_z_new = keep_rate * electric_z + curl_rate * (backward_diff(magnetic_y_new, 1) - backward_diff(magnetic_x_new, 2))
    return (jnp.stack([electric_x_new, electric_y_new, electric_z_new]),
            jnp.stack([magnetic_x_new, magnetic_y_new, magnetic_z_new]))
```

```python
import jax
import jax.numpy as jnp
from jax import lax
from jax.sharding import PartitionSpec as P

time_step = 0.5
z_courant = 128.0


def from_prev(block, axis):
    count = lax.axis_size(axis)
    return lax.ppermute(block, axis, [(i, i + 1) for i in range(count - 1)])


def from_next(block, axis):
    count = lax.axis_size(axis)
    return lax.ppermute(block, axis, [(i + 1, i) for i in range(count - 1)])


def from_diagonal(block, axes, step_a, step_b):
    size_a = lax.axis_size(axes[0])
    size_b = lax.axis_size(axes[1])
    pairs = []
    for a in range(size_a):
        for b in range(size_b):
            src_a, src_b = a - step_a, b - step_b
            if 0 <= src_a < size_a and 0 <= src_b < size_b:
                pairs.append((src_a * size_b + src_b, a * size_b + b))
    return lax.ppermute(block, axes, pairs)


def lookup(table_values, layer_map, material):
    kind_count, entry_count = table_values.shape
    layer_hot = layer_map[:, None] == lax.broadcasted_iota(jnp.int32, (1, kind_count), 1)
    table_rows = jnp.sum(jnp.where(layer_hot[:, :, None], table_values[None], 0.0), axis=1)
    result = jnp.zeros(material.shape, jnp.float32)
    for entry_index in range(entry_count):
        result = result + jnp.where(
            material == entry_index, table_rows[:, entry_index][:, None, None], 0.0
        )
    return result


def rates(epsilon_cell, sigma_cell):
    half_loss = 0.25 * sigma_cell / epsilon_cell
    drive_rate = 1.0 / (1.0 + half_loss)
    keep_rate = (1.0 - half_loss) * drive_rate
    curl_rate = 0.5 * drive_rate / epsilon_cell
    z_rate = z_courant * drive_rate / epsilon_cell
    stiffness = 4096.0 * drive_rate / epsilon_cell
    return (keep_rate, curl_rate, z_rate, stiffness)


def from_below(values, stride, fill):
    depth = values.shape[0]
    padding = jnp.full((stride,) + values.shape[1:], fill, jnp.float32)
    return jnp.concatenate([padding, values[: depth - stride]], axis=0)


def from_above(values, stride, fill):
    padding = jnp.full((stride,) + values.shape[1:], fill, jnp.float32)
    return jnp.concatenate([values[stride:], padding], axis=0)


def sweep_columns(stiffness, diagonal, sources):
    depth = stiffness.shape[0]
    level_index = lax.broadcasted_iota(jnp.int32, stiffness.shape, 0)
    lower = jnp.where(level_index == 0, 0.0, -stiffness)
    upper = jnp.where(level_index == depth - 1, 0.0, -stiffness)
    pivot = diagonal
    values = sources
    stride = 1
    while stride < depth:
        lower_below = from_below(lower, stride, 0.0)
        upper_below = from_below(upper, stride, 0.0)
        pivot_below = from_below(pivot, stride, 1.0)
        values_below = from_below(values, stride, 0.0)
        lower_above = from_above(lower, stride, 0.0)
        upper_above = from_above(upper, stride, 0.0)
        pivot_above = from_above(pivot, stride, 1.0)
        values_above = from_above(values, stride, 0.0)
        alpha = -lower / pivot_below
        gamma = -upper / pivot_above
        pivot = pivot + alpha * upper_below + gamma * lower_above
        values = values + alpha[:, None] * values_below + gamma[:, None] * values_above
        lower = alpha * lower_below
        upper = gamma * upper_above
        stride = stride * 2
    return values / pivot[:, None]


def advance(pieces, incoming, factor):
    rows_first, rows_last, low_first, low_last, high_first, high_last = pieces
    denominator = 1.0 - low_first * factor
    offset = (rows_first + low_first[None] * incoming) / denominator[None]
    coupling = high_first / denominator
    outgoing = rows_last + low_last[None] * (incoming + factor[None] * offset)
    factor_out = low_last * factor * coupling + high_last
    return (offset, coupling, outgoing, factor_out)


def body(electric, magnetic, material, layer_map, permittivity, conductivity):
    epsilon_cell = lookup(permittivity, layer_map, material)
    sigma_cell = lookup(conductivity, layer_map, material)
    keep_rate, curl_rate, z_rate, stiffness = rates(epsilon_cell, sigma_cell)
    depth_rows, span_x, span_y = material.shape
    slab = lax.axis_index("gz")
    bottom = slab == 0
    first_x = lax.axis_index("gx") == 0
    first_y = lax.axis_index("gy") == 0
    electric_x, electric_y, electric_z = (electric[0], electric[1], electric[2])
    magnetic_x, magnetic_y, magnetic_z = (magnetic[0], magnetic[1], magnetic[2])

    x_high = from_next(jnp.stack([electric_y[:, :1], electric_z[:, :1]]), "gx")
    x_low = from_prev(
        jnp.stack([electric_x[:, -1:], electric_y[:, -1:], magnetic_z[:, -1:]]), "gx"
    )
    y_high = from_next(jnp.stack([electric_x[:, :, :1], electric_z[:, :, :1]]), "gy")
    y_low = from_prev(
        jnp.stack([electric_x[:, :, -1:], electric_y[:, :, -1:], magnetic_z[:, :, -1:]]), "gy"
    )
    z_low = from_prev(
        jnp.stack(
            [electric_x[-1:], electric_y[-1:], electric_z[-1:], magnetic_x[-1:], magnetic_y[-1:]]
        ),
        "gz",
    )
    z_high = from_next(jnp.stack([electric_x[:1], electric_y[:1]]), "gz")
    corner_ex = from_diagonal(electric_x[:, -1:, :1], ("gx", "gy"), 1, -1)
    corner_ey = from_diagonal(electric_y[:, :1, -1:], ("gx", "gy"), -1, 1)
    corner_zx = from_diagonal(electric_z[-1:, :1, :], ("gx", "gz"), -1, 1)
    corner_zy = from_diagonal(electric_z[-1:, :, :1], ("gy", "gz"), -1, 1)

    ey_xh, ez_xh = x_high[0], x_high[1]
    ex_xl, ey_xl, hz_xl = x_low[0], x_low[1], x_low[2]
    ex_yh, ez_yh = y_high[0], y_high[1]
    ex_yl, ey_yl, hz_yl = y_low[0], y_low[1], y_low[2]
    ex_zl, ey_zl, ez_zl, hx_zl, hy_zl = z_low[0], z_low[1], z_low[2], z_low[3], z_low[4]
    ex_zh, ey_zh = z_high[0], z_high[1]

    ey_next_x = jnp.concatenate([electric_y[:, 1:], ey_xh], axis=1)
    ex_next_y = jnp.concatenate([electric_x[:, :, 1:], ex_yh], axis=2)
    face_term = (ey_next_x - electric_y) - (ex_next_y - electric_x)
    magnetic_z_new = magnetic_z - time_step * face_term
    ey_yl_next_x = jnp.concatenate([ey_yl[:, 1:], corner_ey], axis=1)
    face_yl = (ey_yl_next_x - ey_yl) - (electric_x[:, :, :1] - ex_yl)
    hz_new_yl = jnp.where(first_y, 0.0, hz_yl - time_step * face_yl)
    ex_xl_next_y = jnp.concatenate([ex_xl[:, :, 1:], corner_ex], axis=2)
    face_xl = (electric_y[:, :1] - ey_xl) - (ex_xl_next_y - ex_xl)
    hz_new_xl = jnp.where(first_x, 0.0, hz_xl - time_step * face_xl)
    hz_before_y = jnp.concatenate([hz_new_yl, magnetic_z_new[:, :, :-1]], axis=2)
    hz_before_x = jnp.concatenate([hz_new_xl, magnetic_z_new[:, :-1]], axis=1)

    ez_next_x = jnp.concatenate([electric_z[:, 1:], ez_xh], axis=1)
    ez_next_y = jnp.concatenate([electric_z[:, :, 1:], ez_yh], axis=2)
    slope_zx = ez_next_x - electric_z
    slope_zy = ez_next_y - electric_z
    slope_zx_below = jnp.concatenate([ez_zl[:, 1:], corner_zx], axis=1) - ez_zl
    slope_zy_below = jnp.concatenate([ez_zl[:, :, 1:], corner_zy], axis=2) - ez_zl

    def second_z(field, below, above):
        column = jnp.concatenate([below, field, above], axis=0)
        rise_steps = column[1:] - column[:-1]
        level_index = lax.broadcasted_iota(jnp.int32, rise_steps.shape, 0)
        rise_steps = jnp.where(jnp.logical_and(bottom, level_index == 0), 0.0, rise_steps)
        return rise_steps[1:] - rise_steps[:-1]

    def down_z(field, below):
        return field - jnp.concatenate([below, field[:-1]], axis=0)

    quarter_z = 0.25 * z_rate
    source_x = (
        keep_rate * electric_x
        + stiffness * second_z(electric_x, ex_zl, ex_zh)
        + curl_rate * (magnetic_z_new - hz_before_y)
        - z_rate * down_z(magnetic_y, hy_zl)
        - quarter_z * down_z(slope_zx, slope_zx_below)
    )
    source_y = (
        keep_rate * electric_y
        + stiffness * second_z(electric_y, ey_zl, ey_zh)
        + z_rate * down_z(magnetic_x, hx_zl)
        - quarter_z * down_z(slope_zy, slope_zy_below)
        - curl_rate * (magnetic_z_new - hz_before_x)
    )
    level_index = lax.broadcasted_iota(jnp.int32, stiffness.shape, 0)
    diagonal = 1.0 + 2.0 * stiffness
    diagonal = jnp.where(jnp.logical_and(bottom, level_index == 0), 1.0 + stiffness, diagonal)
    unit_low = jnp.where(level_index == 0, 1.0, 0.0)
    unit_high = jnp.where(level_index == depth_rows - 1, 1.0, 0.0)
    solved = sweep_columns(
        stiffness, diagonal, jnp.stack([source_x, source_y, unit_low, unit_high], axis=1)
    )
    partial_pair = solved[:, :2]
    low_weight = stiffness[0] * solved[:, 2]
    high_weight = stiffness[-1] * solved[:, 3]

    own = jnp.concatenate(
        [
            partial_pair[0],
            partial_pair[-1],
            jnp.stack([low_weight[0], low_weight[-1], high_weight[0], high_weight[-1]]),
        ],
        axis=0,
    )
    slab_count = lax.axis_size("gz")
    gathered = [own]
    for shift in range(1, slab_count):
        gathered.append(
            lax.ppermute(own, "gz", [(i, (i + shift) % slab_count) for i in range(slab_count)])
        )
    gathered = jnp.stack(gathered)
    slabs = []
    for index in range(slab_count):
        chosen = lax.dynamic_index_in_dim(
            gathered, (slab - index) % slab_count, axis=0, keepdims=False
        )
        slabs.append(
            (chosen[0:2], chosen[2:4], chosen[4], chosen[5], chosen[6], chosen[7])
        )

    incoming_all = []
    factor_all = []
    offset_all = []
    coupling_all = []
    incoming = jnp.zeros_like(partial_pair[0])
    factor = jnp.zeros_like(low_weight[0])
    for index in range(slab_count):
        if index > 0:
            incoming, factor = outgoing, factor_out
        offset, coupling, outgoing, factor_out = advance(slabs[index], incoming, factor)
        incoming_all.append(incoming)
        factor_all.append(factor)
        offset_all.append(offset)
        coupling_all.append(coupling)
    following_all = [None] * slab_count
    leading_all = [None] * slab_count
    following = jnp.zeros_like(partial_pair[0])
    for index in reversed(range(slab_count)):
        if index < slab_count - 1:
            following = leading_all[index + 1]
        following_all[index] = following
        leading_all[index] = offset_all[index] + coupling_all[index][None] * following

    def pick(values):
        return lax.dynamic_index_in_dim(jnp.stack(values), slab, axis=0, keepdims=False)

    incoming = pick(incoming_all)
    factor = pick(factor_all)
    following = pick(following_all)
    leading = pick(leading_all)

    previous_last = incoming + factor[None] * leading
    new_pair = (
        partial_pair
        + previous_last[None] * low_weight[:, None]
        + following[None] * high_weight[:, None]
    )
    electric_x_new = new_pair[:, 0]
    electric_y_new = new_pair[:, 1]
    sum_x = electric_x + electric_x_new
    sum_y = electric_y + electric_y_new
    top_x = ex_zh[0] + following[0]
    top_y = ey_zh[0] + following[1]
    rise_x = jnp.concatenate([sum_x[1:], top_x[None]], axis=0) - sum_x
    rise_y = jnp.concatenate([sum_y[1:], top_y[None]], axis=0) - sum_y
    magnetic_y_new = magnetic_y - 0.5 * z_courant * rise_x + time_step * slope_zx
    magnetic_x_new = magnetic_x - time_step * slope_zy + 0.5 * z_courant * rise_y
    before_hy = from_prev(magnetic_y_new[:, -1:, :], "gx")
    before_hx = from_prev(magnetic_x_new[:, :, -1:], "gy")
    change_hy = magnetic_y_new - jnp.concatenate([before_hy, magnetic_y_new[:, :-1]], axis=1)
    change_hx = magnetic_x_new - jnp.concatenate([before_hx, magnetic_x_new[:, :, :-1]], axis=2)
    electric_z_new = keep_rate * electric_z + curl_rate * (change_hy - change_hx)
    return (
        jnp.stack([electric_x_new, electric_y_new, electric_z_new]),
        jnp.stack([magnetic_x_new, magnetic_y_new, magnetic_z_new]),
    )


def solution(mesh):
    return jax.shard_map(
        body,
        mesh=mesh,
        in_specs=(
            P(None, "gz", "gx", "gy"),
            P(None, "gz", "gx", "gy"),
            P("gz", "gx", "gy"),
            P("gz"),
            P(),
            P(),
        ),
        out_specs=(P(None, "gz", "gx", "gy"), P(None, "gz", "gx", "gy")),
        check_vma=False,
    )
```

```python
import jax
import jax.numpy as jnp
from jax import lax
from jax.sharding import PartitionSpec as P
from jax.experimental import pallas as pl
from jax.experimental.pallas import tpu as pltpu

time_step = 0.5
z_courant = 128.0


def from_prev(block, axis):
    count = lax.axis_size(axis)
    return lax.ppermute(block, axis, [(i, i + 1) for i in range(count - 1)])


def from_next(block, axis):
    count = lax.axis_size(axis)
    return lax.ppermute(block, axis, [(i + 1, i) for i in range(count - 1)])


def from_diagonal(block, axes, step_a, step_b):
    size_a = lax.axis_size(axes[0])
    size_b = lax.axis_size(axes[1])
    pairs = []
    for a in range(size_a):
        for b in range(size_b):
            src_a, src_b = a - step_a, b - step_b
            if 0 <= src_a < size_a and 0 <= src_b < size_b:
                pairs.append((src_a * size_b + src_b, a * size_b + b))
    return lax.ppermute(block, axes, pairs)


def lookup(table_values, layer_map, material):
    kind_count, entry_count = table_values.shape
    layer_hot = layer_map[:, None] == lax.broadcasted_iota(jnp.int32, (1, kind_count), 1)
    table_rows = jnp.sum(jnp.where(layer_hot[:, :, None], table_values[None], 0.0), axis=1)
    result = jnp.zeros(material.shape, jnp.float32)
    for entry_index in range(entry_count):
        result = result + jnp.where(
            material == entry_index, table_rows[:, entry_index][:, None, None], 0.0
        )
    return result


def rates(epsilon_cell, sigma_cell):
    half_loss = 0.25 * sigma_cell / epsilon_cell
    drive_rate = 1.0 / (1.0 + half_loss)
    keep_rate = (1.0 - half_loss) * drive_rate
    curl_rate = 0.5 * drive_rate / epsilon_cell
    z_rate = z_courant * drive_rate / epsilon_cell
    stiffness = 4096.0 * drive_rate / epsilon_cell
    return (keep_rate, curl_rate, z_rate, stiffness)


def thomas_kernel(stiff_ref, diag_ref, sx_ref, sy_ref, px_ref, py_ref, lw_ref, hw_ref, ur_ref):
    depth = stiff_ref.shape[0]
    stiff = stiff_ref[0]
    inv = 1.0 / diag_ref[0]
    ur_ref[0] = -stiff * inv
    px_ref[0] = sx_ref[0] * inv
    py_ref[0] = sy_ref[0] * inv
    lw_ref[0] = inv

    def forward(z, carry):
        upper, value_x, value_y, value_low, unused = carry
        stiff = stiff_ref[z]
        inv = 1.0 / (diag_ref[z] + stiff * upper)
        upper = -stiff * inv
        value_x = (sx_ref[z] + stiff * value_x) * inv
        value_y = (sy_ref[z] + stiff * value_y) * inv
        value_low = (stiff * value_low) * inv
        ur_ref[z] = upper
        px_ref[z] = value_x
        py_ref[z] = value_y
        lw_ref[z] = value_low
        return upper, value_x, value_y, value_low, inv

    first = (ur_ref[0], px_ref[0], py_ref[0], lw_ref[0], inv)
    last_x, last_y, last_low, last_high = lax.fori_loop(1, depth, forward, first, unroll=8)[1:]
    low_scale = stiff_ref[0]
    high_scale = stiff_ref[depth - 1]
    lw_ref[depth - 1] = low_scale * last_low
    hw_ref[depth - 1] = high_scale * last_high

    def backward(step, carry):
        z = depth - 2 - step
        next_x, next_y, next_low, next_high = carry
        upper = ur_ref[z]
        next_x = px_ref[z] - upper * next_x
        next_y = py_ref[z] - upper * next_y
        next_low = lw_ref[z] - upper * next_low
        next_high = -upper * next_high
        px_ref[z] = next_x
        py_ref[z] = next_y
        lw_ref[z] = low_scale * next_low
        hw_ref[z] = high_scale * next_high
        return next_x, next_y, next_low, next_high

    lax.fori_loop(0, depth - 1, backward, (last_x, last_y, last_low, last_high), unroll=8)


def solve_slab(stiffness, diagonal, source_x, source_y):
    shape = jax.ShapeDtypeStruct(stiffness.shape, jnp.float32)
    return pl.pallas_call(
        thomas_kernel,
        out_shape=(shape, shape, shape, shape),
        scratch_shapes=[pltpu.VMEM(stiffness.shape, jnp.float32)],
    )(stiffness, diagonal, source_x, source_y)


def advance(pieces, incoming, factor):
    rows_first, rows_last, low_first, low_last, high_first, high_last = pieces
    denominator = 1.0 - low_first * factor
    offset = (rows_first + low_first[None] * incoming) / denominator[None]
    coupling = high_first / denominator
    outgoing = rows_last + low_last[None] * (incoming + factor[None] * offset)
    factor_out = low_last * factor * coupling + high_last
    return (offset, coupling, outgoing, factor_out)


def body(electric, magnetic, material, layer_map, permittivity, conductivity):
    epsilon_cell = lookup(permittivity, layer_map, material)
    sigma_cell = lookup(conductivity, layer_map, material)
    keep_rate, curl_rate, z_rate, stiffness = rates(epsilon_cell, sigma_cell)
    depth_rows, span_x, span_y = material.shape
    slab = lax.axis_index("gz")
    bottom = slab == 0
    first_x = lax.axis_index("gx") == 0
    first_y = lax.axis_index("gy") == 0
    electric_x, electric_y, electric_z = (electric[0], electric[1], electric[2])
    magnetic_x, magnetic_y, magnetic_z = (magnetic[0], magnetic[1], magnetic[2])

    x_high = from_next(jnp.stack([electric_y[:, :1], electric_z[:, :1]]), "gx")
    x_low = from_prev(
        jnp.stack([electric_x[:, -1:], electric_y[:, -1:], magnetic_z[:, -1:]]), "gx"
    )
    y_high = from_next(jnp.stack([electric_x[:, :, :1], electric_z[:, :, :1]]), "gy")
    y_low = from_prev(
        jnp.stack([electric_x[:, :, -1:], electric_y[:, :, -1:], magnetic_z[:, :, -1:]]), "gy"
    )
    z_low = from_prev(
        jnp.stack(
            [electric_x[-1:], electric_y[-1:], electric_z[-1:], magnetic_x[-1:], magnetic_y[-1:]]
        ),
        "gz",
    )
    z_high = from_next(jnp.stack([electric_x[:1], electric_y[:1]]), "gz")
    corner_ex = from_diagonal(electric_x[:, -1:, :1], ("gx", "gy"), 1, -1)
    corner_ey = from_diagonal(electric_y[:, :1, -1:], ("gx", "gy"), -1, 1)
    corner_zx = from_diagonal(electric_z[-1:, :1, :], ("gx", "gz"), -1, 1)
    corner_zy = from_diagonal(electric_z[-1:, :, :1], ("gy", "gz"), -1, 1)

    ey_xh, ez_xh = x_high[0], x_high[1]
    ex_xl, ey_xl, hz_xl = x_low[0], x_low[1], x_low[2]
    ex_yh, ez_yh = y_high[0], y_high[1]
    ex_yl, ey_yl, hz_yl = y_low[0], y_low[1], y_low[2]
    ex_zl, ey_zl, ez_zl, hx_zl, hy_zl = z_low[0], z_low[1], z_low[2], z_low[3], z_low[4]
    ex_zh, ey_zh = z_high[0], z_high[1]

    ey_next_x = jnp.concatenate([electric_y[:, 1:], ey_xh], axis=1)
    ex_next_y = jnp.concatenate([electric_x[:, :, 1:], ex_yh], axis=2)
    face_term = (ey_next_x - electric_y) - (ex_next_y - electric_x)
    magnetic_z_new = magnetic_z - time_step * face_term
    ey_yl_next_x = jnp.concatenate([ey_yl[:, 1:], corner_ey], axis=1)
    face_yl = (ey_yl_next_x - ey_yl) - (electric_x[:, :, :1] - ex_yl)
    hz_new_yl = jnp.where(first_y, 0.0, hz_yl - time_step * face_yl)
    ex_xl_next_y = jnp.concatenate([ex_xl[:, :, 1:], corner_ex], axis=2)
    face_xl = (electric_y[:, :1] - ey_xl) - (ex_xl_next_y - ex_xl)
    hz_new_xl = jnp.where(first_x, 0.0, hz_xl - time_step * face_xl)
    hz_before_y = jnp.concatenate([hz_new_yl, magnetic_z_new[:, :, :-1]], axis=2)
    hz_before_x = jnp.concatenate([hz_new_xl, magnetic_z_new[:, :-1]], axis=1)

    ez_next_x = jnp.concatenate([electric_z[:, 1:], ez_xh], axis=1)
    ez_next_y = jnp.concatenate([electric_z[:, :, 1:], ez_yh], axis=2)
    slope_zx = ez_next_x - electric_z
    slope_zy = ez_next_y - electric_z
    slope_zx_below = jnp.concatenate([ez_zl[:, 1:], corner_zx], axis=1) - ez_zl
    slope_zy_below = jnp.concatenate([ez_zl[:, :, 1:], corner_zy], axis=2) - ez_zl

    def second_z(field, below, above):
        column = jnp.concatenate([below, field, above], axis=0)
        rise_steps = column[1:] - column[:-1]
        level_index = lax.broadcasted_iota(jnp.int32, rise_steps.shape, 0)
        rise_steps = jnp.where(jnp.logical_and(bottom, level_index == 0), 0.0, rise_steps)
        return rise_steps[1:] - rise_steps[:-1]

    def down_z(field, below):
        return field - jnp.concatenate([below, field[:-1]], axis=0)

    quarter_z = 0.25 * z_rate
    source_x = (
        keep_rate * electric_x
        + stiffness * second_z(electric_x, ex_zl, ex_zh)
        + curl_rate * (magnetic_z_new - hz_before_y)
        - z_rate * down_z(magnetic_y, hy_zl)
        - quarter_z * down_z(slope_zx, slope_zx_below)
    )
    source_y = (
        keep_rate * electric_y
        + stiffness * second_z(electric_y, ey_zl, ey_zh)
        + z_rate * down_z(magnetic_x, hx_zl)
        - quarter_z * down_z(slope_zy, slope_zy_below)
        - curl_rate * (magnetic_z_new - hz_before_x)
    )
    level_index = lax.broadcasted_iota(jnp.int32, stiffness.shape, 0)
    diagonal = 1.0 + 2.0 * stiffness
    diagonal = jnp.where(jnp.logical_and(bottom, level_index == 0), 1.0 + stiffness, diagonal)
    partial_x, partial_y, low_weight, high_weight = solve_slab(
        stiffness, diagonal, source_x, source_y
    )

    own = jnp.concatenate(
        [
            jnp.stack([partial_x[0], partial_y[0], partial_x[-1], partial_y[-1]]),
            jnp.stack([low_weight[0], low_weight[-1], high_weight[0], high_weight[-1]]),
        ],
        axis=0,
    )
    slab_count = lax.axis_size("gz")
    gathered = [own]
    for shift in range(1, slab_count):
        gathered.append(
            lax.ppermute(own, "gz", [(i, (i + shift) % slab_count) for i in range(slab_count)])
        )
    gathered = jnp.stack(gathered)
    slabs = []
    for index in range(slab_count):
        chosen = lax.dynamic_index_in_dim(
            gathered, (slab - index) % slab_count, axis=0, keepdims=False
        )
        slabs.append(
            (chosen[0:2], chosen[2:4], chosen[4], chosen[5], chosen[6], chosen[7])
        )

    incoming_all = []
    factor_all = []
    offset_all = []
    coupling_all = []
    incoming = jnp.zeros((2,) + partial_x.shape[1:], jnp.float32)
    factor = jnp.zeros_like(low_weight[0])
    for index in range(slab_count):
        if index > 0:
            incoming, factor = outgoing, factor_out
        offset, coupling, outgoing, factor_out = advance(slabs[index], incoming, factor)
        incoming_all.append(incoming)
        factor_all.append(factor)
        offset_all.append(offset)
        coupling_all.append(coupling)
    following_all = [None] * slab_count
    leading_all = [None] * slab_count
    following = jnp.zeros((2,) + partial_x.shape[1:], jnp.float32)
    for index in reversed(range(slab_count)):
        if index < slab_count - 1:
            following = leading_all[index + 1]
        following_all[index] = following
        leading_all[index] = offset_all[index] + coupling_all[index][None] * following

    def pick(values):
        return lax.dynamic_index_in_dim(jnp.stack(values), slab, axis=0, keepdims=False)

    incoming = pick(incoming_all)
    factor = pick(factor_all)
    following = pick(following_all)
    leading = pick(leading_all)

    previous_last = incoming + factor[None] * leading
    electric_x_new = (
        partial_x + previous_last[0][None] * low_weight + following[0][None] * high_weight
    )
    electric_y_new = (
        partial_y + previous_last[1][None] * low_weight + following[1][None] * high_weight
    )
    sum_x = electric_x + electric_x_new
    sum_y = electric_y + electric_y_new
    top_x = ex_zh[0] + following[0]
    top_y = ey_zh[0] + following[1]
    rise_x = jnp.concatenate([sum_x[1:], top_x[None]], axis=0) - sum_x
    rise_y = jnp.concatenate([sum_y[1:], top_y[None]], axis=0) - sum_y
    magnetic_y_new = magnetic_y - 0.5 * z_courant * rise_x + time_step * slope_zx
    magnetic_x_new = magnetic_x - time_step * slope_zy + 0.5 * z_courant * rise_y
    before_hy = from_prev(magnetic_y_new[:, -1:, :], "gx")
    before_hx = from_prev(magnetic_x_new[:, :, -1:], "gy")
    change_hy = magnetic_y_new - jnp.concatenate([before_hy, magnetic_y_new[:, :-1]], axis=1)
    change_hx = magnetic_x_new - jnp.concatenate([before_hx, magnetic_x_new[:, :, :-1]], axis=2)
    electric_z_new = keep_rate * electric_z + curl_rate * (change_hy - change_hx)
    return (
        jnp.stack([electric_x_new, electric_y_new, electric_z_new]),
        jnp.stack([magnetic_x_new, magnetic_y_new, magnetic_z_new]),
    )


def solution(mesh):
    return jax.shard_map(
        body,
        mesh=mesh,
        in_specs=(
            P(None, "gz", "gx", "gy"),
            P(None, "gz", "gx", "gy"),
            P("gz", "gx", "gy"),
            P("gz"),
            P(),
            P(),
        ),
        out_specs=(P(None, "gz", "gx", "gy"), P(None, "gz", "gx", "gy")),
        check_vma=False,
    )
```

```python
import jax
import jax.numpy as jnp
from jax import lax
from jax.sharding import PartitionSpec as P
from jax.experimental import pallas as pl
from jax.experimental.pallas import tpu as pltpu

time_step = 0.5
z_courant = 128.0


def from_prev(block, axis):
    count = lax.axis_size(axis)
    return lax.ppermute(block, axis, [(i, i + 1) for i in range(count - 1)])


def from_next(block, axis):
    count = lax.axis_size(axis)
    return lax.ppermute(block, axis, [(i + 1, i) for i in range(count - 1)])


def from_diagonal(block, axes, step_a, step_b):
    size_a = lax.axis_size(axes[0])
    size_b = lax.axis_size(axes[1])
    pairs = []
    for a in range(size_a):
        for b in range(size_b):
            src_a, src_b = a - step_a, b - step_b
            if 0 <= src_a < size_a and 0 <= src_b < size_b:
                pairs.append((src_a * size_b + src_b, a * size_b + b))
    return lax.ppermute(block, axes, pairs)


def lookup(table_values, layer_map, material):
    kind_count, entry_count = table_values.shape
    layer_hot = layer_map[:, None] == lax.broadcasted_iota(jnp.int32, (1, kind_count), 1)
    table_rows = jnp.sum(jnp.where(layer_hot[:, :, None], table_values[None], 0.0), axis=1)
    result = jnp.zeros(material.shape, jnp.float32)
    for entry_index in range(entry_count):
        result = result + jnp.where(
            material == entry_index, table_rows[:, entry_index][:, None, None], 0.0
        )
    return result


def rates(epsilon_cell, sigma_cell):
    half_loss = 0.25 * sigma_cell / epsilon_cell
    drive_rate = 1.0 / (1.0 + half_loss)
    keep_rate = (1.0 - half_loss) * drive_rate
    curl_rate = 0.5 * drive_rate / epsilon_cell
    z_rate = z_courant * drive_rate / epsilon_cell
    stiffness = 4096.0 * drive_rate / epsilon_cell
    return (keep_rate, curl_rate, z_rate, stiffness)


def thomas_kernel(
    stiff_ref, diag_ref, sx_ref, sy_ref, px_ref, py_ref, lw_ref, hw_ref, edge_ref, ur_ref
):
    depth = stiff_ref.shape[0]
    stiff = stiff_ref[0]
    inv = 1.0 / diag_ref[0]
    ur_ref[0] = -stiff * inv
    px_ref[0] = sx_ref[0] * inv
    py_ref[0] = sy_ref[0] * inv
    lw_ref[0] = inv

    def forward(z, carry):
        upper, value_x, value_y, value_low, unused = carry
        stiff = stiff_ref[z]
        inv = 1.0 / (diag_ref[z] + stiff * upper)
        upper = -stiff * inv
        value_x = (sx_ref[z] + stiff * value_x) * inv
        value_y = (sy_ref[z] + stiff * value_y) * inv
        value_low = (stiff * value_low) * inv
        ur_ref[z] = upper
        px_ref[z] = value_x
        py_ref[z] = value_y
        lw_ref[z] = value_low
        return upper, value_x, value_y, value_low, inv

    first = (ur_ref[0], px_ref[0], py_ref[0], lw_ref[0], inv)
    last_x, last_y, last_low, last_high = lax.fori_loop(1, depth, forward, first, unroll=8)[1:]
    low_scale = stiff_ref[0]
    high_scale = stiff_ref[depth - 1]
    lw_ref[depth - 1] = low_scale * last_low
    hw_ref[depth - 1] = high_scale * last_high

    def backward(step, carry):
        z = depth - 2 - step
        next_x, next_y, next_low, next_high = carry
        upper = ur_ref[z]
        next_x = px_ref[z] - upper * next_x
        next_y = py_ref[z] - upper * next_y
        next_low = lw_ref[z] - upper * next_low
        next_high = -upper * next_high
        px_ref[z] = next_x
        py_ref[z] = next_y
        lw_ref[z] = low_scale * next_low
        hw_ref[z] = high_scale * next_high
        return next_x, next_y, next_low, next_high

    lax.fori_loop(0, depth - 1, backward, (last_x, last_y, last_low, last_high), unroll=8)
    edge_ref[0] = px_ref[0]
    edge_ref[1] = py_ref[0]
    edge_ref[2] = px_ref[depth - 1]
    edge_ref[3] = py_ref[depth - 1]
    edge_ref[4] = lw_ref[0]
    edge_ref[5] = lw_ref[depth - 1]
    edge_ref[6] = hw_ref[0]
    edge_ref[7] = hw_ref[depth - 1]


def solve_slab(stiffness, diagonal, source_x, source_y):
    shape = jax.ShapeDtypeStruct(stiffness.shape, jnp.float32)
    edges = jax.ShapeDtypeStruct((8,) + stiffness.shape[1:], jnp.float32)
    return pl.pallas_call(
        thomas_kernel,
        out_shape=(shape, shape, shape, shape, edges),
        scratch_shapes=[pltpu.VMEM(stiffness.shape, jnp.float32)],
    )(stiffness, diagonal, source_x, source_y)


def advance(pieces, incoming, factor):
    rows_first, rows_last, low_first, low_last, high_first, high_last = pieces
    denominator = 1.0 - low_first * factor
    offset = (rows_first + low_first[None] * incoming) / denominator[None]
    coupling = high_first / denominator
    outgoing = rows_last + low_last[None] * (incoming + factor[None] * offset)
    factor_out = low_last * factor * coupling + high_last
    return (offset, coupling, outgoing, factor_out)


def body(electric, magnetic, material, layer_map, permittivity, conductivity):
    epsilon_cell = lookup(permittivity, layer_map, material)
    sigma_cell = lookup(conductivity, layer_map, material)
    keep_rate, curl_rate, z_rate, stiffness = rates(epsilon_cell, sigma_cell)
    depth_rows, span_x, span_y = material.shape
    slab = lax.axis_index("gz")
    bottom = slab == 0
    first_x = lax.axis_index("gx") == 0
    first_y = lax.axis_index("gy") == 0
    electric_x, electric_y, electric_z = (electric[0], electric[1], electric[2])
    magnetic_x, magnetic_y, magnetic_z = (magnetic[0], magnetic[1], magnetic[2])

    x_high = from_next(jnp.stack([electric_y[:, :1], electric_z[:, :1]]), "gx")
    x_low = from_prev(
        jnp.stack([electric_x[:, -1:], electric_y[:, -1:], magnetic_z[:, -1:]]), "gx"
    )
    y_high = from_next(jnp.stack([electric_x[:, :, :1], electric_z[:, :, :1]]), "gy")
    y_low = from_prev(
        jnp.stack([electric_x[:, :, -1:], electric_y[:, :, -1:], magnetic_z[:, :, -1:]]), "gy"
    )
    z_low = from_prev(
        jnp.stack(
            [electric_x[-1:], electric_y[-1:], electric_z[-1:], magnetic_x[-1:], magnetic_y[-1:]]
        ),
        "gz",
    )
    z_high = from_next(jnp.stack([electric_x[:1], electric_y[:1]]), "gz")
    corner_ex = from_diagonal(electric_x[:, -1:, :1], ("gx", "gy"), 1, -1)
    corner_ey = from_diagonal(electric_y[:, :1, -1:], ("gx", "gy"), -1, 1)
    corner_zx = from_diagonal(electric_z[-1:, :1, :], ("gx", "gz"), -1, 1)
    corner_zy = from_diagonal(electric_z[-1:, :, :1], ("gy", "gz"), -1, 1)

    ey_xh, ez_xh = x_high[0], x_high[1]
    ex_xl, ey_xl, hz_xl = x_low[0], x_low[1], x_low[2]
    ex_yh, ez_yh = y_high[0], y_high[1]
    ex_yl, ey_yl, hz_yl = y_low[0], y_low[1], y_low[2]
    ex_zl, ey_zl, ez_zl, hx_zl, hy_zl = z_low[0], z_low[1], z_low[2], z_low[3], z_low[4]
    ex_zh, ey_zh = z_high[0], z_high[1]

    ey_next_x = jnp.concatenate([electric_y[:, 1:], ey_xh], axis=1)
    ex_next_y = jnp.concatenate([electric_x[:, :, 1:], ex_yh], axis=2)
    face_term = (ey_next_x - electric_y) - (ex_next_y - electric_x)
    magnetic_z_new = magnetic_z - time_step * face_term
    ey_yl_next_x = jnp.concatenate([ey_yl[:, 1:], corner_ey], axis=1)
    face_yl = (ey_yl_next_x - ey_yl) - (electric_x[:, :, :1] - ex_yl)
    hz_new_yl = jnp.where(first_y, 0.0, hz_yl - time_step * face_yl)
    ex_xl_next_y = jnp.concatenate([ex_xl[:, :, 1:], corner_ex], axis=2)
    face_xl = (electric_y[:, :1] - ey_xl) - (ex_xl_next_y - ex_xl)
    hz_new_xl = jnp.where(first_x, 0.0, hz_xl - time_step * face_xl)
    hz_before_y = jnp.concatenate([hz_new_yl, magnetic_z_new[:, :, :-1]], axis=2)
    hz_before_x = jnp.concatenate([hz_new_xl, magnetic_z_new[:, :-1]], axis=1)

    ez_next_x = jnp.concatenate([electric_z[:, 1:], ez_xh], axis=1)
    ez_next_y = jnp.concatenate([electric_z[:, :, 1:], ez_yh], axis=2)
    slope_zx = ez_next_x - electric_z
    slope_zy = ez_next_y - electric_z
    slope_zx_below = jnp.concatenate([ez_zl[:, 1:], corner_zx], axis=1) - ez_zl
    slope_zy_below = jnp.concatenate([ez_zl[:, :, 1:], corner_zy], axis=2) - ez_zl

    def second_z(field, below, above):
        column = jnp.concatenate([below, field, above], axis=0)
        rise_steps = column[1:] - column[:-1]
        level_index = lax.broadcasted_iota(jnp.int32, rise_steps.shape, 0)
        rise_steps = jnp.where(jnp.logical_and(bottom, level_index == 0), 0.0, rise_steps)
        return rise_steps[1:] - rise_steps[:-1]

    def down_z(field, below):
        return field - jnp.concatenate([below, field[:-1]], axis=0)

    quarter_z = 0.25 * z_rate
    source_x = (
        keep_rate * electric_x
        + stiffness * second_z(electric_x, ex_zl, ex_zh)
        + curl_rate * (magnetic_z_new - hz_before_y)
        - z_rate * down_z(magnetic_y, hy_zl)
        - quarter_z * down_z(slope_zx, slope_zx_below)
    )
    source_y = (
        keep_rate * electric_y
        + stiffness * second_z(electric_y, ey_zl, ey_zh)
        + z_rate * down_z(magnetic_x, hx_zl)
        - quarter_z * down_z(slope_zy, slope_zy_below)
        - curl_rate * (magnetic_z_new - hz_before_x)
    )
    level_index = lax.broadcasted_iota(jnp.int32, stiffness.shape, 0)
    diagonal = 1.0 + 2.0 * stiffness
    diagonal = jnp.where(jnp.logical_and(bottom, level_index == 0), 1.0 + stiffness, diagonal)
    partial_x, partial_y, low_weight, high_weight, own = solve_slab(
        stiffness, diagonal, source_x, source_y
    )

    slab_count = lax.axis_size("gz")
    gathered = [own]
    for shift in range(1, slab_count):
        gathered.append(
            lax.ppermute(own, "gz", [(i, (i + shift) % slab_count) for i in range(slab_count)])
        )
    gathered = jnp.stack(gathered)
    slabs = []
    for index in range(slab_count):
        chosen = lax.dynamic_index_in_dim(
            gathered, (slab - index) % slab_count, axis=0, keepdims=False
        )
        slabs.append(
            (chosen[0:2], chosen[2:4], chosen[4], chosen[5], chosen[6], chosen[7])
        )

    incoming_all = []
    factor_all = []
    offset_all = []
    coupling_all = []
    incoming = jnp.zeros((2,) + partial_x.shape[1:], jnp.float32)
    factor = jnp.zeros_like(low_weight[0])
    for index in range(slab_count):
        if index > 0:
            incoming, factor = outgoing, factor_out
        offset, coupling, outgoing, factor_out = advance(slabs[index], incoming, factor)
        incoming_all.append(incoming)
        factor_all.append(factor)
        offset_all.append(offset)
        coupling_all.append(coupling)
    following_all = [None] * slab_count
    leading_all = [None] * slab_count
    following = jnp.zeros((2,) + partial_x.shape[1:], jnp.float32)
    for index in reversed(range(slab_count)):
        if index < slab_count - 1:
            following = leading_all[index + 1]
        following_all[index] = following
        leading_all[index] = offset_all[index] + coupling_all[index][None] * following

    def pick(values):
        return lax.dynamic_index_in_dim(jnp.stack(values), slab, axis=0, keepdims=False)

    incoming = pick(incoming_all)
    factor = pick(factor_all)
    following = pick(following_all)
    leading = pick(leading_all)

    previous_last = incoming + factor[None] * leading
    electric_x_new = (
        partial_x + previous_last[0][None] * low_weight + following[0][None] * high_weight
    )
    electric_y_new = (
        partial_y + previous_last[1][None] * low_weight + following[1][None] * high_weight
    )
    sum_x = electric_x + electric_x_new
    sum_y = electric_y + electric_y_new
    top_x = ex_zh[0] + following[0]
    top_y = ey_zh[0] + following[1]
    rise_x = jnp.concatenate([sum_x[1:], top_x[None]], axis=0) - sum_x
    rise_y = jnp.concatenate([sum_y[1:], top_y[None]], axis=0) - sum_y
    magnetic_y_new = magnetic_y - 0.5 * z_courant * rise_x + time_step * slope_zx
    magnetic_x_new = magnetic_x - time_step * slope_zy + 0.5 * z_courant * rise_y
    before_hy = from_prev(magnetic_y_new[:, -1:, :], "gx")
    before_hx = from_prev(magnetic_x_new[:, :, -1:], "gy")
    change_hy = magnetic_y_new - jnp.concatenate([before_hy, magnetic_y_new[:, :-1]], axis=1)
    change_hx = magnetic_x_new - jnp.concatenate([before_hx, magnetic_x_new[:, :, :-1]], axis=2)
    electric_z_new = keep_rate * electric_z + curl_rate * (change_hy - change_hx)
    return (
        jnp.stack([electric_x_new, electric_y_new, electric_z_new]),
        jnp.stack([magnetic_x_new, magnetic_y_new, magnetic_z_new]),
    )


def solution(mesh):
    return jax.shard_map(
        body,
        mesh=mesh,
        in_specs=(
            P(None, "gz", "gx", "gy"),
            P(None, "gz", "gx", "gy"),
            P("gz", "gx", "gy"),
            P("gz"),
            P(),
            P(),
        ),
        out_specs=(P(None, "gz", "gx", "gy"), P(None, "gz", "gx", "gy")),
        check_vma=False,
    )
```

```python
import jax
import jax.numpy as jnp
from jax import lax
from jax.sharding import PartitionSpec as P
from jax.experimental import pallas as pl
from jax.experimental.pallas import tpu as pltpu

time_step = 0.5
z_courant = 128.0


def from_prev(block, axis):
    count = lax.axis_size(axis)
    return lax.ppermute(block, axis, [(i, i + 1) for i in range(count - 1)])


def from_next(block, axis):
    count = lax.axis_size(axis)
    return lax.ppermute(block, axis, [(i + 1, i) for i in range(count - 1)])


def from_diagonal(block, axes, step_a, step_b):
    size_a = lax.axis_size(axes[0])
    size_b = lax.axis_size(axes[1])
    pairs = []
    for a in range(size_a):
        for b in range(size_b):
            src_a, src_b = a - step_a, b - step_b
            if 0 <= src_a < size_a and 0 <= src_b < size_b:
                pairs.append((src_a * size_b + src_b, a * size_b + b))
    return lax.ppermute(block, axes, pairs)


def lookup(table_values, layer_map, material):
    kind_count, entry_count = table_values.shape
    layer_hot = layer_map[:, None] == lax.broadcasted_iota(jnp.int32, (1, kind_count), 1)
    table_rows = jnp.sum(jnp.where(layer_hot[:, :, None], table_values[None], 0.0), axis=1)
    result = jnp.zeros(material.shape, jnp.float32)
    for entry_index in range(entry_count):
        result = result + jnp.where(
            material == entry_index, table_rows[:, entry_index][:, None, None], 0.0
        )
    return result


def rates(epsilon_cell, sigma_cell):
    half_loss = 0.25 * sigma_cell / epsilon_cell
    drive_rate = 1.0 / (1.0 + half_loss)
    keep_rate = (1.0 - half_loss) * drive_rate
    curl_rate = 0.5 * drive_rate / epsilon_cell
    z_rate = z_courant * drive_rate / epsilon_cell
    stiffness = 4096.0 * drive_rate / epsilon_cell
    return (keep_rate, curl_rate, z_rate, stiffness)


def thomas_kernel(
    stiff_ref, diag_ref, sx_ref, sy_ref, px_ref, py_ref, lw_ref, hw_ref, edge_ref, ur_ref
):
    depth = stiff_ref.shape[0]
    stiff = stiff_ref[0]
    inv = 1.0 / diag_ref[0]
    ur_ref[0] = -stiff * inv
    px_ref[0] = sx_ref[0] * inv
    py_ref[0] = sy_ref[0] * inv
    lw_ref[0] = inv

    def forward(z, carry):
        upper, value_x, value_y, value_low, unused = carry
        stiff = stiff_ref[z]
        inv = 1.0 / (diag_ref[z] + stiff * upper)
        upper = -stiff * inv
        value_x = (sx_ref[z] + stiff * value_x) * inv
        value_y = (sy_ref[z] + stiff * value_y) * inv
        value_low = (stiff * value_low) * inv
        ur_ref[z] = upper
        px_ref[z] = value_x
        py_ref[z] = value_y
        lw_ref[z] = value_low
        return upper, value_x, value_y, value_low, inv

    first = (ur_ref[0], px_ref[0], py_ref[0], lw_ref[0], inv)
    last_x, last_y, last_low, last_high = lax.fori_loop(1, depth, forward, first, unroll=8)[1:]
    low_scale = stiff_ref[0]
    high_scale = stiff_ref[depth - 1]
    lw_ref[depth - 1] = low_scale * last_low
    hw_ref[depth - 1] = high_scale * last_high

    def backward(step, carry):
        z = depth - 2 - step
        next_x, next_y, next_low, next_high = carry
        upper = ur_ref[z]
        next_x = px_ref[z] - upper * next_x
        next_y = py_ref[z] - upper * next_y
        next_low = lw_ref[z] - upper * next_low
        next_high = -upper * next_high
        px_ref[z] = next_x
        py_ref[z] = next_y
        lw_ref[z] = low_scale * next_low
        hw_ref[z] = high_scale * next_high
        return next_x, next_y, next_low, next_high

    lax.fori_loop(0, depth - 1, backward, (last_x, last_y, last_low, last_high), unroll=8)
    edge_ref[0] = px_ref[0]
    edge_ref[1] = py_ref[0]
    edge_ref[2] = px_ref[depth - 1]
    edge_ref[3] = py_ref[depth - 1]
    edge_ref[4] = lw_ref[0]
    edge_ref[5] = lw_ref[depth - 1]
    edge_ref[6] = hw_ref[0]
    edge_ref[7] = hw_ref[depth - 1]


def solve_slab(stiffness, diagonal, source_x, source_y):
    shape = jax.ShapeDtypeStruct(stiffness.shape, jnp.float32)
    edges = jax.ShapeDtypeStruct((8,) + stiffness.shape[1:], jnp.float32)
    return pl.pallas_call(
        thomas_kernel,
        out_shape=(shape, shape, shape, shape, edges),
        scratch_shapes=[pltpu.VMEM(stiffness.shape, jnp.float32)],
    )(stiffness, diagonal, source_x, source_y)


def source_kernel(
    flag_ref, e_ref, h_ref, rate_ref, xh_ref, xl_ref, yh_ref, yl_ref, zl_ref, zh_ref,
    cex_ref, cey_ref, czx_ref, czy_ref, sx_ref, sy_ref, hzn_ref, szx_ref, szy_ref,
):
    depth, rows, lanes = sx_ref.shape
    bottom = flag_ref[0] == 1
    first_x = flag_ref[1] == 1
    first_y = flag_ref[2] == 1
    sub = lax.broadcasted_iota(jnp.int32, (rows, lanes), 0)
    lane = lax.broadcasted_iota(jnp.int32, (rows, lanes), 1)

    def full(value):
        return jnp.broadcast_to(value, (rows, lanes))

    def next_x(tile, edge):
        return jnp.where(sub == rows - 1, full(edge), pltpu.roll(tile, rows - 1, 0))

    def prev_x(tile, edge):
        return jnp.where(sub == 0, full(edge), pltpu.roll(tile, 1, 0))

    def next_y(tile, edge):
        return jnp.where(lane == lanes - 1, full(edge), pltpu.roll(tile, lanes - 1, 1))

    def prev_y(tile, edge):
        return jnp.where(lane == 0, full(edge), pltpu.roll(tile, 1, 1))

    def row(z, below, above, first_row):
        ex, ey, ez = e_ref[0, z], e_ref[1, z], e_ref[2, z]
        hx, hy, hz = h_ref[0, z], h_ref[1, z], h_ref[2, z]
        keep, curl, zrate, stiff = rate_ref[0, z], rate_ref[1, z], rate_ref[2, z], rate_ref[3, z]
        ey_xh, ez_xh = full(xh_ref[0, z]), full(xh_ref[1, z])
        ex_xl, ey_xl, hz_xl = full(xl_ref[0, z]), full(xl_ref[1, z]), full(xl_ref[2, z])
        ex_yh, ez_yh = full(yh_ref[0, z]), full(yh_ref[1, z])
        ex_yl, ey_yl, hz_yl = full(yl_ref[0, z]), full(yl_ref[1, z]), full(yl_ref[2, z])
        corner_ex = full(cex_ref[z])
        corner_ey = full(cey_ref[z])
        hz_new = hz - time_step * ((next_x(ey, ey_xh) - ey) - (next_y(ex, ex_yh) - ex))
        ex_py = prev_y(ex, ex_yl)
        ey_py = prev_y(ey, ey_yl)
        hz_py = prev_y(hz, hz_yl)
        face_py = (next_x(ey_py, prev_y(ey_xh, corner_ey)) - ey_py) - (ex - ex_py)
        hz_new_py = hz_py - time_step * face_py
        hz_new_py = jnp.where(jnp.logical_and(first_y, lane == 0), 0.0, hz_new_py)
        ex_px = prev_x(ex, ex_xl)
        ey_px = prev_x(ey, ey_xl)
        hz_px = prev_x(hz, hz_xl)
        face_px = (ey - ey_px) - (next_y(ex_px, prev_x(ex_yh, corner_ex)) - ex_px)
        hz_new_px = hz_px - time_step * face_px
        hz_new_px = jnp.where(jnp.logical_and(first_x, sub == 0), 0.0, hz_new_px)
        slope_zx = next_x(ez, ez_xh) - ez
        slope_zy = next_y(ez, ez_yh) - ez
        ex_b, ey_b, hx_b, hy_b, slope_zx_b, slope_zy_b = below
        ex_a, ey_a = above
        rise_x = ex - ex_b
        rise_y = ey - ey_b
        if first_row:
            rise_x = jnp.where(bottom, 0.0, rise_x)
            rise_y = jnp.where(bottom, 0.0, rise_y)
        quarter_z = 0.25 * zrate
        sx_ref[z] = (
            keep * ex
            + stiff * ((ex_a - ex) - rise_x)
            + curl * (hz_new - hz_new_py)
            - zrate * (hy - hy_b)
            - quarter_z * (slope_zx - slope_zx_b)
        )
        sy_ref[z] = (
            keep * ey
            + stiff * ((ey_a - ey) - rise_y)
            + zrate * (hx - hx_b)
            - quarter_z * (slope_zy - slope_zy_b)
            - curl * (hz_new - hz_new_px)
        )
        hzn_ref[z] = hz_new
        szx_ref[z] = slope_zx
        szy_ref[z] = slope_zy
        return (ex, ey, hx, hy, slope_zx, slope_zy)

    ez_b = zl_ref[2]
    slope_zx_b = next_x(ez_b, full(czx_ref[...])) - ez_b
    slope_zy_b = next_y(ez_b, full(czy_ref[...])) - ez_b
    below = (zl_ref[0], zl_ref[1], zl_ref[3], zl_ref[4], slope_zx_b, slope_zy_b)
    below = row(0, below, (e_ref[0, 1], e_ref[1, 1]), True)

    def middle(z, below):
        return row(z, below, (e_ref[0, z + 1], e_ref[1, z + 1]), False)

    below = lax.fori_loop(1, depth - 1, middle, below, unroll=2)
    row(depth - 1, below, (zh_ref[0], zh_ref[1]), False)


def make_sources(flags, electric, magnetic, rate_stack, x_high, x_low, y_high, y_low,
                 z_low, z_high, corner_ex, corner_ey, corner_zx, corner_zy):
    shape = jax.ShapeDtypeStruct(electric.shape[1:], jnp.float32)
    vmem = pl.BlockSpec(memory_space=pltpu.VMEM)
    smem = pl.BlockSpec(memory_space=pltpu.SMEM)
    return pl.pallas_call(
        source_kernel,
        out_shape=(shape,) * 5,
        in_specs=[smem] + [vmem] * 13,
        out_specs=(vmem,) * 5,
    )(flags, electric, magnetic, rate_stack, x_high, x_low, y_high, y_low,
      z_low, z_high, corner_ex, corner_ey, corner_zx, corner_zy)


def advance(pieces, incoming, factor):
    rows_first, rows_last, low_first, low_last, high_first, high_last = pieces
    denominator = 1.0 - low_first * factor
    offset = (rows_first + low_first[None] * incoming) / denominator[None]
    coupling = high_first / denominator
    outgoing = rows_last + low_last[None] * (incoming + factor[None] * offset)
    factor_out = low_last * factor * coupling + high_last
    return (offset, coupling, outgoing, factor_out)


def body(electric, magnetic, material, layer_map, permittivity, conductivity):
    epsilon_cell = lookup(permittivity, layer_map, material)
    sigma_cell = lookup(conductivity, layer_map, material)
    keep_rate, curl_rate, z_rate, stiffness = rates(epsilon_cell, sigma_cell)
    depth_rows, span_x, span_y = material.shape
    slab = lax.axis_index("gz")
    bottom = slab == 0
    first_x = lax.axis_index("gx") == 0
    first_y = lax.axis_index("gy") == 0
    electric_x, electric_y, electric_z = (electric[0], electric[1], electric[2])
    magnetic_x, magnetic_y, magnetic_z = (magnetic[0], magnetic[1], magnetic[2])

    x_high = from_next(jnp.stack([electric_y[:, :1], electric_z[:, :1]]), "gx")
    x_low = from_prev(
        jnp.stack([electric_x[:, -1:], electric_y[:, -1:], magnetic_z[:, -1:]]), "gx"
    )
    y_high = from_next(jnp.stack([electric_x[:, :, :1], electric_z[:, :, :1]]), "gy")
    y_low = from_prev(
        jnp.stack([electric_x[:, :, -1:], electric_y[:, :, -1:], magnetic_z[:, :, -1:]]), "gy"
    )
    z_low = from_prev(
        jnp.stack(
            [electric_x[-1:], electric_y[-1:], electric_z[-1:], magnetic_x[-1:], magnetic_y[-1:]]
        ),
        "gz",
    )
    z_high = from_next(jnp.stack([electric_x[:1], electric_y[:1]]), "gz")
    corner_ex = from_diagonal(electric_x[:, -1:, :1], ("gx", "gy"), 1, -1)
    corner_ey = from_diagonal(electric_y[:, :1, -1:], ("gx", "gy"), -1, 1)
    corner_zx = from_diagonal(electric_z[-1:, :1, :], ("gx", "gz"), -1, 1)
    corner_zy = from_diagonal(electric_z[-1:, :, :1], ("gy", "gz"), -1, 1)

    ex_zh, ey_zh = z_high[0], z_high[1]
    flags = jnp.stack([bottom, first_x, first_y]).astype(jnp.int32)
    rate_stack = jnp.stack([keep_rate, curl_rate, z_rate, stiffness])
    source_x, source_y, magnetic_z_new, slope_zx, slope_zy = make_sources(
        flags, electric, magnetic, rate_stack, x_high, x_low, y_high, y_low,
        z_low[:, 0], z_high[:, 0], corner_ex, corner_ey, corner_zx[0], corner_zy[0],
    )
    level_index = lax.broadcasted_iota(jnp.int32, stiffness.shape, 0)
    diagonal = 1.0 + 2.0 * stiffness
    diagonal = jnp.where(jnp.logical_and(bottom, level_index == 0), 1.0 + stiffness, diagonal)
    partial_x, partial_y, low_weight, high_weight, own = solve_slab(
        stiffness, diagonal, source_x, source_y
    )

    slab_count = lax.axis_size("gz")
    gathered = [own]
    for shift in range(1, slab_count):
        gathered.append(
            lax.ppermute(own, "gz", [(i, (i + shift) % slab_count) for i in range(slab_count)])
        )
    gathered = jnp.stack(gathered)
    slabs = []
    for index in range(slab_count):
        chosen = lax.dynamic_index_in_dim(
            gathered, (slab - index) % slab_count, axis=0, keepdims=False
        )
        slabs.append(
            (chosen[0:2], chosen[2:4], chosen[4], chosen[5], chosen[6], chosen[7])
        )

    incoming_all = []
    factor_all = []
    offset_all = []
    coupling_all = []
    incoming = jnp.zeros((2,) + partial_x.shape[1:], jnp.float32)
    factor = jnp.zeros_like(low_weight[0])
    for index in range(slab_count):
        if index > 0:
            incoming, factor = outgoing, factor_out
        offset, coupling, outgoing, factor_out = advance(slabs[index], incoming, factor)
        incoming_all.append(incoming)
        factor_all.append(factor)
        offset_all.append(offset)
        coupling_all.append(coupling)
    following_all = [None] * slab_count
    leading_all = [None] * slab_count
    following = jnp.zeros((2,) + partial_x.shape[1:], jnp.float32)
    for index in reversed(range(slab_count)):
        if index < slab_count - 1:
            following = leading_all[index + 1]
        following_all[index] = following
        leading_all[index] = offset_all[index] + coupling_all[index][None] * following

    def pick(values):
        return lax.dynamic_index_in_dim(jnp.stack(values), slab, axis=0, keepdims=False)

    incoming = pick(incoming_all)
    factor = pick(factor_all)
    following = pick(following_all)
    leading = pick(leading_all)

    previous_last = incoming + factor[None] * leading
    electric_x_new = (
        partial_x + previous_last[0][None] * low_weight + following[0][None] * high_weight
    )
    electric_y_new = (
        partial_y + previous_last[1][None] * low_weight + following[1][None] * high_weight
    )
    sum_x = electric_x + electric_x_new
    sum_y = electric_y + electric_y_new
    top_x = ex_zh[0] + following[0]
    top_y = ey_zh[0] + following[1]
    rise_x = jnp.concatenate([sum_x[1:], top_x[None]], axis=0) - sum_x
    rise_y = jnp.concatenate([sum_y[1:], top_y[None]], axis=0) - sum_y
    magnetic_y_new = magnetic_y - 0.5 * z_courant * rise_x + time_step * slope_zx
    magnetic_x_new = magnetic_x - time_step * slope_zy + 0.5 * z_courant * rise_y
    before_hy = from_prev(magnetic_y_new[:, -1:, :], "gx")
    before_hx = from_prev(magnetic_x_new[:, :, -1:], "gy")
    change_hy = magnetic_y_new - jnp.concatenate([before_hy, magnetic_y_new[:, :-1]], axis=1)
    change_hx = magnetic_x_new - jnp.concatenate([before_hx, magnetic_x_new[:, :, :-1]], axis=2)
    electric_z_new = keep_rate * electric_z + curl_rate * (change_hy - change_hx)
    return (
        jnp.stack([electric_x_new, electric_y_new, electric_z_new]),
        jnp.stack([magnetic_x_new, magnetic_y_new, magnetic_z_new]),
    )


def solution(mesh):
    return jax.shard_map(
        body,
        mesh=mesh,
        in_specs=(
            P(None, "gz", "gx", "gy"),
            P(None, "gz", "gx", "gy"),
            P("gz", "gx", "gy"),
            P("gz"),
            P(),
            P(),
        ),
        out_specs=(P(None, "gz", "gx", "gy"), P(None, "gz", "gx", "gy")),
        check_vma=False,
    )
```

```python
import jax
import jax.numpy as jnp
from jax import lax
from jax.sharding import PartitionSpec as P
from jax.experimental import pallas as pl
from jax.experimental.pallas import tpu as pltpu

time_step = 0.5
z_courant = 128.0


def from_prev(block, axis):
    count = lax.axis_size(axis)
    return lax.ppermute(block, axis, [(i, i + 1) for i in range(count - 1)])


def from_next(block, axis):
    count = lax.axis_size(axis)
    return lax.ppermute(block, axis, [(i + 1, i) for i in range(count - 1)])


def from_diagonal(block, axes, step_a, step_b):
    size_a = lax.axis_size(axes[0])
    size_b = lax.axis_size(axes[1])
    pairs = []
    for a in range(size_a):
        for b in range(size_b):
            src_a, src_b = a - step_a, b - step_b
            if 0 <= src_a < size_a and 0 <= src_b < size_b:
                pairs.append((src_a * size_b + src_b, a * size_b + b))
    return lax.ppermute(block, axes, pairs)


def lookup(table_values, layer_map, material):
    kind_count, entry_count = table_values.shape
    layer_hot = layer_map[:, None] == lax.broadcasted_iota(jnp.int32, (1, kind_count), 1)
    table_rows = jnp.sum(jnp.where(layer_hot[:, :, None], table_values[None], 0.0), axis=1)
    result = jnp.zeros(material.shape, jnp.float32)
    for entry_index in range(entry_count):
        result = result + jnp.where(
            material == entry_index, table_rows[:, entry_index][:, None, None], 0.0
        )
    return result


def rates(epsilon_cell, sigma_cell):
    half_loss = 0.25 * sigma_cell / epsilon_cell
    drive_rate = 1.0 / (1.0 + half_loss)
    keep_rate = (1.0 - half_loss) * drive_rate
    curl_rate = 0.5 * drive_rate / epsilon_cell
    z_rate = z_courant * drive_rate / epsilon_cell
    stiffness = 4096.0 * drive_rate / epsilon_cell
    return (keep_rate, curl_rate, z_rate, stiffness)


def thomas_kernel(
    stiff_ref, diag_ref, sx_ref, sy_ref, px_ref, py_ref, lw_ref, hw_ref, edge_ref, ur_ref
):
    depth = stiff_ref.shape[0]
    stiff = stiff_ref[0]
    inv = 1.0 / diag_ref[0]
    ur_ref[0] = -stiff * inv
    px_ref[0] = sx_ref[0] * inv
    py_ref[0] = sy_ref[0] * inv
    lw_ref[0] = inv

    def forward(z, carry):
        upper, value_x, value_y, value_low, unused = carry
        stiff = stiff_ref[z]
        inv = 1.0 / (diag_ref[z] + stiff * upper)
        upper = -stiff * inv
        value_x = (sx_ref[z] + stiff * value_x) * inv
        value_y = (sy_ref[z] + stiff * value_y) * inv
        value_low = (stiff * value_low) * inv
        ur_ref[z] = upper
        px_ref[z] = value_x
        py_ref[z] = value_y
        lw_ref[z] = value_low
        return upper, value_x, value_y, value_low, inv

    first = (ur_ref[0], px_ref[0], py_ref[0], lw_ref[0], inv)
    last_x, last_y, last_low, last_high = lax.fori_loop(1, depth, forward, first, unroll=8)[1:]
    low_scale = stiff_ref[0]
    high_scale = stiff_ref[depth - 1]
    lw_ref[depth - 1] = low_scale * last_low
    hw_ref[depth - 1] = high_scale * last_high

    def backward(step, carry):
        z = depth - 2 - step
        next_x, next_y, next_low, next_high = carry
        upper = ur_ref[z]
        next_x = px_ref[z] - upper * next_x
        next_y = py_ref[z] - upper * next_y
        next_low = lw_ref[z] - upper * next_low
        next_high = -upper * next_high
        px_ref[z] = next_x
        py_ref[z] = next_y
        lw_ref[z] = low_scale * next_low
        hw_ref[z] = high_scale * next_high
        return next_x, next_y, next_low, next_high

    lax.fori_loop(0, depth - 1, backward, (last_x, last_y, last_low, last_high), unroll=8)
    edge_ref[0] = px_ref[0]
    edge_ref[1] = py_ref[0]
    edge_ref[2] = px_ref[depth - 1]
    edge_ref[3] = py_ref[depth - 1]
    edge_ref[4] = lw_ref[0]
    edge_ref[5] = lw_ref[depth - 1]
    edge_ref[6] = hw_ref[0]
    edge_ref[7] = hw_ref[depth - 1]


def solve_slab(stiffness, diagonal, source_x, source_y):
    shape = jax.ShapeDtypeStruct(stiffness.shape, jnp.float32)
    edges = jax.ShapeDtypeStruct((8,) + stiffness.shape[1:], jnp.float32)
    return pl.pallas_call(
        thomas_kernel,
        out_shape=(shape, shape, shape, shape, edges),
        scratch_shapes=[pltpu.VMEM(stiffness.shape, jnp.float32)],
    )(stiffness, diagonal, source_x, source_y)


def source_kernel(
    flag_ref, e_ref, h_ref, rate_ref, xh_ref, xl_ref, yh_ref, yl_ref,
    cex_ref, cey_ref, sx_ref, sy_ref, hzn_ref, szx_ref, szy_ref,
):
    depth, rows, lanes = sx_ref.shape
    bottom = flag_ref[0] == 1
    first_x = flag_ref[1] == 1
    first_y = flag_ref[2] == 1
    sub = lax.broadcasted_iota(jnp.int32, (rows, lanes), 0)
    lane = lax.broadcasted_iota(jnp.int32, (rows, lanes), 1)

    def full(value):
        return jnp.broadcast_to(value, (rows, lanes))

    def next_x(tile, edge):
        return jnp.where(sub == rows - 1, full(edge), pltpu.roll(tile, rows - 1, 0))

    def prev_x(tile, edge):
        return jnp.where(sub == 0, full(edge), pltpu.roll(tile, 1, 0))

    def next_y(tile, edge):
        return jnp.where(lane == lanes - 1, full(edge), pltpu.roll(tile, lanes - 1, 1))

    def prev_y(tile, edge):
        return jnp.where(lane == 0, full(edge), pltpu.roll(tile, 1, 1))

    def row(z, below, above, first_row):
        ex, ey, ez = e_ref[0, z], e_ref[1, z], e_ref[2, z]
        hx, hy, hz = h_ref[0, z], h_ref[1, z], h_ref[2, z]
        keep, curl, zrate, stiff = rate_ref[0, z], rate_ref[1, z], rate_ref[2, z], rate_ref[3, z]
        ey_xh, ez_xh = full(xh_ref[0, z]), full(xh_ref[1, z])
        ex_xl, ey_xl, hz_xl = full(xl_ref[0, z]), full(xl_ref[1, z]), full(xl_ref[2, z])
        ex_yh, ez_yh = full(yh_ref[0, z]), full(yh_ref[1, z])
        ex_yl, ey_yl, hz_yl = full(yl_ref[0, z]), full(yl_ref[1, z]), full(yl_ref[2, z])
        corner_ex = full(cex_ref[z])
        corner_ey = full(cey_ref[z])
        hz_new = hz - time_step * ((next_x(ey, ey_xh) - ey) - (next_y(ex, ex_yh) - ex))
        ex_py = prev_y(ex, ex_yl)
        ey_py = prev_y(ey, ey_yl)
        hz_py = prev_y(hz, hz_yl)
        face_py = (next_x(ey_py, prev_y(ey_xh, corner_ey)) - ey_py) - (ex - ex_py)
        hz_new_py = hz_py - time_step * face_py
        hz_new_py = jnp.where(jnp.logical_and(first_y, lane == 0), 0.0, hz_new_py)
        ex_px = prev_x(ex, ex_xl)
        ey_px = prev_x(ey, ey_xl)
        hz_px = prev_x(hz, hz_xl)
        face_px = (ey - ey_px) - (next_y(ex_px, prev_x(ex_yh, corner_ex)) - ex_px)
        hz_new_px = hz_px - time_step * face_px
        hz_new_px = jnp.where(jnp.logical_and(first_x, sub == 0), 0.0, hz_new_px)
        slope_zx = next_x(ez, ez_xh) - ez
        slope_zy = next_y(ez, ez_yh) - ez
        ex_b, ey_b, hx_b, hy_b, slope_zx_b, slope_zy_b = below
        ex_a, ey_a = above
        rise_x = ex - ex_b
        rise_y = ey - ey_b
        if first_row:
            rise_x = jnp.where(bottom, 0.0, rise_x)
            rise_y = jnp.where(bottom, 0.0, rise_y)
        quarter_z = 0.25 * zrate
        sx_ref[z] = (
            keep * ex
            + stiff * ((ex_a - ex) - rise_x)
            + curl * (hz_new - hz_new_py)
            - zrate * (hy - hy_b)
            - quarter_z * (slope_zx - slope_zx_b)
        )
        sy_ref[z] = (
            keep * ey
            + stiff * ((ey_a - ey) - rise_y)
            + zrate * (hx - hx_b)
            - quarter_z * (slope_zy - slope_zy_b)
            - curl * (hz_new - hz_new_px)
        )
        hzn_ref[z] = hz_new
        szx_ref[z] = slope_zx
        szy_ref[z] = slope_zy
        return (ex, ey, hx, hy, slope_zx, slope_zy)

    zero = jnp.zeros((rows, lanes), jnp.float32)
    below = row(0, (zero,) * 6, (e_ref[0, 1], e_ref[1, 1]), True)

    def middle(z, below):
        return row(z, below, (e_ref[0, z + 1], e_ref[1, z + 1]), False)

    below = lax.fori_loop(1, depth - 1, middle, below, unroll=2)
    row(depth - 1, below, (zero, zero), False)


def make_sources(flags, electric, magnetic, rate_stack, x_high, x_low, y_high, y_low,
                 corner_ex, corner_ey):
    shape = jax.ShapeDtypeStruct(electric.shape[1:], jnp.float32)
    vmem = pl.BlockSpec(memory_space=pltpu.VMEM)
    smem = pl.BlockSpec(memory_space=pltpu.SMEM)
    return pl.pallas_call(
        source_kernel,
        out_shape=(shape,) * 5,
        in_specs=[smem] + [vmem] * 9,
        out_specs=(vmem,) * 5,
    )(flags, electric, magnetic, rate_stack, x_high, x_low, y_high, y_low,
      corner_ex, corner_ey)


def advance(pieces, incoming, factor):
    rows_first, rows_last, low_first, low_last, high_first, high_last = pieces
    denominator = 1.0 - low_first * factor
    offset = (rows_first + low_first[None] * incoming) / denominator[None]
    coupling = high_first / denominator
    outgoing = rows_last + low_last[None] * (incoming + factor[None] * offset)
    factor_out = low_last * factor * coupling + high_last
    return (offset, coupling, outgoing, factor_out)


def body(electric, magnetic, material, layer_map, permittivity, conductivity):
    epsilon_cell = lookup(permittivity, layer_map, material)
    sigma_cell = lookup(conductivity, layer_map, material)
    keep_rate, curl_rate, z_rate, stiffness = rates(epsilon_cell, sigma_cell)
    depth_rows, span_x, span_y = material.shape
    slab = lax.axis_index("gz")
    bottom = slab == 0
    first_x = lax.axis_index("gx") == 0
    first_y = lax.axis_index("gy") == 0
    electric_x, electric_y, electric_z = (electric[0], electric[1], electric[2])
    magnetic_x, magnetic_y, magnetic_z = (magnetic[0], magnetic[1], magnetic[2])

    x_high = from_next(jnp.stack([electric_y[:, :1], electric_z[:, :1]]), "gx")
    x_low = from_prev(
        jnp.stack([electric_x[:, -1:], electric_y[:, -1:], magnetic_z[:, -1:]]), "gx"
    )
    y_high = from_next(jnp.stack([electric_x[:, :, :1], electric_z[:, :, :1]]), "gy")
    y_low = from_prev(
        jnp.stack([electric_x[:, :, -1:], electric_y[:, :, -1:], magnetic_z[:, :, -1:]]), "gy"
    )
    corner_ex = from_diagonal(electric_x[:, -1:, :1], ("gx", "gy"), 1, -1)
    corner_ey = from_diagonal(electric_y[:, :1, -1:], ("gx", "gy"), -1, 1)

    flags = jnp.stack([bottom, first_x, first_y]).astype(jnp.int32)
    rate_stack = jnp.stack([keep_rate, curl_rate, z_rate, stiffness])
    source_x, source_y, magnetic_z_new, slope_zx, slope_zy = make_sources(
        flags, electric, magnetic, rate_stack, x_high, x_low, y_high, y_low,
        corner_ex, corner_ey,
    )
    level_index = lax.broadcasted_iota(jnp.int32, stiffness.shape, 0)
    diagonal = 1.0 + 2.0 * stiffness
    diagonal = jnp.where(jnp.logical_and(bottom, level_index == 0), 1.0 + stiffness, diagonal)
    partial_x, partial_y, low_weight, high_weight, edges = solve_slab(
        stiffness, diagonal, source_x, source_y
    )
    below_x = electric_x[-1] + (magnetic_y[-1] + 0.25 * slope_zx[-1]) / 32.0
    below_y = electric_y[-1] + (0.25 * slope_zy[-1] - magnetic_x[-1]) / 32.0
    own = jnp.concatenate(
        [edges, jnp.stack([below_x, below_y, electric_x[0], electric_y[0]])], axis=0
    )

    slab_count = lax.axis_size("gz")
    gathered = [own]
    for shift in range(1, slab_count):
        gathered.append(
            lax.ppermute(own, "gz", [(i, (i + shift) % slab_count) for i in range(slab_count)])
        )
    gathered = jnp.stack(gathered)
    slabs = []
    for index in range(slab_count):
        chosen = lax.dynamic_index_in_dim(
            gathered, (slab - index) % slab_count, axis=0, keepdims=False
        )
        slabs.append(chosen)
    zero_pair = jnp.zeros((2,) + partial_x.shape[1:], jnp.float32)
    below_all = [zero_pair] + [slabs[index][8:10] for index in range(slab_count - 1)]
    above_all = [slabs[index][10:12] for index in range(1, slab_count)] + [zero_pair]
    for index in range(slab_count):
        chosen = slabs[index]
        low_first, low_last, high_first, high_last = chosen[4], chosen[5], chosen[6], chosen[7]
        rows_first = (
            chosen[0:2] + below_all[index] * low_first[None] + above_all[index] * high_first[None]
        )
        rows_last = (
            chosen[2:4] + below_all[index] * low_last[None] + above_all[index] * high_last[None]
        )
        slabs[index] = (rows_first, rows_last, low_first, low_last, high_first, high_last)

    incoming_all = []
    factor_all = []
    offset_all = []
    coupling_all = []
    incoming = jnp.zeros((2,) + partial_x.shape[1:], jnp.float32)
    factor = jnp.zeros_like(low_weight[0])
    for index in range(slab_count):
        if index > 0:
            incoming, factor = outgoing, factor_out
        offset, coupling, outgoing, factor_out = advance(slabs[index], incoming, factor)
        incoming_all.append(incoming)
        factor_all.append(factor)
        offset_all.append(offset)
        coupling_all.append(coupling)
    following_all = [None] * slab_count
    leading_all = [None] * slab_count
    following = jnp.zeros((2,) + partial_x.shape[1:], jnp.float32)
    for index in reversed(range(slab_count)):
        if index < slab_count - 1:
            following = leading_all[index + 1]
        following_all[index] = following
        leading_all[index] = offset_all[index] + coupling_all[index][None] * following

    def pick(values):
        return lax.dynamic_index_in_dim(jnp.stack(values), slab, axis=0, keepdims=False)

    incoming = pick(incoming_all)
    factor = pick(factor_all)
    following = pick(following_all)
    leading = pick(leading_all)
    below = pick(below_all)
    above = pick(above_all)

    previous_last = incoming + factor[None] * leading + below
    following = following + above
    electric_x_new = (
        partial_x + previous_last[0][None] * low_weight + following[0][None] * high_weight
    )
    electric_y_new = (
        partial_y + previous_last[1][None] * low_weight + following[1][None] * high_weight
    )
    sum_x = electric_x + electric_x_new
    sum_y = electric_y + electric_y_new
    top_x = following[0]
    top_y = following[1]
    rise_x = jnp.concatenate([sum_x[1:], top_x[None]], axis=0) - sum_x
    rise_y = jnp.concatenate([sum_y[1:], top_y[None]], axis=0) - sum_y
    magnetic_y_new = magnetic_y - 0.5 * z_courant * rise_x + time_step * slope_zx
    magnetic_x_new = magnetic_x - time_step * slope_zy + 0.5 * z_courant * rise_y
    before_hy = from_prev(magnetic_y_new[:, -1:, :], "gx")
    before_hx = from_prev(magnetic_x_new[:, :, -1:], "gy")
    change_hy = magnetic_y_new - jnp.concatenate([before_hy, magnetic_y_new[:, :-1]], axis=1)
    change_hx = magnetic_x_new - jnp.concatenate([before_hx, magnetic_x_new[:, :, :-1]], axis=2)
    electric_z_new = keep_rate * electric_z + curl_rate * (change_hy - change_hx)
    return (
        jnp.stack([electric_x_new, electric_y_new, electric_z_new]),
        jnp.stack([magnetic_x_new, magnetic_y_new, magnetic_z_new]),
    )


def solution(mesh):
    return jax.shard_map(
        body,
        mesh=mesh,
        in_specs=(
            P(None, "gz", "gx", "gy"),
            P(None, "gz", "gx", "gy"),
            P("gz", "gx", "gy"),
            P("gz"),
            P(),
            P(),
        ),
        out_specs=(P(None, "gz", "gx", "gy"), P(None, "gz", "gx", "gy")),
        check_vma=False,
    )
```

```python
import jax
import jax.numpy as jnp
from jax import lax
from jax.sharding import PartitionSpec as P
from jax.experimental import pallas as pl
from jax.experimental.pallas import tpu as pltpu

time_step = 0.5
z_courant = 128.0


def from_prev(block, axis):
    count = lax.axis_size(axis)
    return lax.ppermute(block, axis, [(i, i + 1) for i in range(count - 1)])


def from_next(block, axis):
    count = lax.axis_size(axis)
    return lax.ppermute(block, axis, [(i + 1, i) for i in range(count - 1)])


def from_diagonal(block, axes, step_a, step_b):
    size_a = lax.axis_size(axes[0])
    size_b = lax.axis_size(axes[1])
    pairs = []
    for a in range(size_a):
        for b in range(size_b):
            src_a, src_b = a - step_a, b - step_b
            if 0 <= src_a < size_a and 0 <= src_b < size_b:
                pairs.append((src_a * size_b + src_b, a * size_b + b))
    return lax.ppermute(block, axes, pairs)


def lookup(table_values, layer_map, material):
    kind_count, entry_count = table_values.shape
    layer_hot = layer_map[:, None] == lax.broadcasted_iota(jnp.int32, (1, kind_count), 1)
    table_rows = jnp.sum(jnp.where(layer_hot[:, :, None], table_values[None], 0.0), axis=1)
    result = jnp.zeros(material.shape, jnp.float32)
    for entry_index in range(entry_count):
        result = result + jnp.where(
            material == entry_index, table_rows[:, entry_index][:, None, None], 0.0
        )
    return result


def rates(epsilon_cell, sigma_cell):
    half_loss = 0.25 * sigma_cell / epsilon_cell
    drive_rate = 1.0 / (1.0 + half_loss)
    keep_rate = (1.0 - half_loss) * drive_rate
    curl_rate = 0.5 * drive_rate / epsilon_cell
    z_rate = z_courant * drive_rate / epsilon_cell
    stiffness = 4096.0 * drive_rate / epsilon_cell
    return (keep_rate, curl_rate, z_rate, stiffness)


def thomas_kernel(
    stiff_ref, diag_ref, sx_ref, sy_ref, px_ref, py_ref, lw_ref, hw_ref, edge_ref, ur_ref
):
    depth = stiff_ref.shape[0]
    stiff = stiff_ref[0]
    inv = 1.0 / diag_ref[0]
    ur_ref[0] = -stiff * inv
    px_ref[0] = sx_ref[0] * inv
    py_ref[0] = sy_ref[0] * inv
    lw_ref[0] = inv

    def forward(z, carry):
        upper, value_x, value_y, value_low, unused = carry
        stiff = stiff_ref[z]
        inv = 1.0 / (diag_ref[z] + stiff * upper)
        upper = -stiff * inv
        value_x = (sx_ref[z] + stiff * value_x) * inv
        value_y = (sy_ref[z] + stiff * value_y) * inv
        value_low = (stiff * value_low) * inv
        ur_ref[z] = upper
        px_ref[z] = value_x
        py_ref[z] = value_y
        lw_ref[z] = value_low
        return upper, value_x, value_y, value_low, inv

    first = (ur_ref[0], px_ref[0], py_ref[0], lw_ref[0], inv)
    last_x, last_y, last_low, last_high = lax.fori_loop(1, depth, forward, first, unroll=8)[1:]
    low_scale = stiff_ref[0]
    high_scale = stiff_ref[depth - 1]
    lw_ref[depth - 1] = low_scale * last_low
    hw_ref[depth - 1] = high_scale * last_high

    def backward(step, carry):
        z = depth - 2 - step
        next_x, next_y, next_low, next_high = carry
        upper = ur_ref[z]
        next_x = px_ref[z] - upper * next_x
        next_y = py_ref[z] - upper * next_y
        next_low = lw_ref[z] - upper * next_low
        next_high = -upper * next_high
        px_ref[z] = next_x
        py_ref[z] = next_y
        lw_ref[z] = low_scale * next_low
        hw_ref[z] = high_scale * next_high
        return next_x, next_y, next_low, next_high

    lax.fori_loop(0, depth - 1, backward, (last_x, last_y, last_low, last_high), unroll=8)
    edge_ref[0] = px_ref[0]
    edge_ref[1] = py_ref[0]
    edge_ref[2] = px_ref[depth - 1]
    edge_ref[3] = py_ref[depth - 1]
    edge_ref[4] = lw_ref[0]
    edge_ref[5] = lw_ref[depth - 1]
    edge_ref[6] = hw_ref[0]
    edge_ref[7] = hw_ref[depth - 1]


def solve_slab(stiffness, diagonal, source_x, source_y):
    shape = jax.ShapeDtypeStruct(stiffness.shape, jnp.float32)
    edges = jax.ShapeDtypeStruct((8,) + stiffness.shape[1:], jnp.float32)
    return pl.pallas_call(
        thomas_kernel,
        out_shape=(shape, shape, shape, shape, edges),
        scratch_shapes=[pltpu.VMEM(stiffness.shape, jnp.float32)],
    )(stiffness, diagonal, source_x, source_y)


def source_kernel(
    flag_ref, e_ref, h_ref, rate_ref, xh_ref, xl_ref, yh_ref, yl_ref,
    cex_ref, cey_ref, hzn_ref, szx_ref, szy_ref, px_ref, py_ref, lw_ref, hw_ref, edge_ref,
    sx_ref, sy_ref, diag_ref, ur_ref,
):
    depth, rows, lanes = sx_ref.shape
    bottom = flag_ref[0] == 1
    first_x = flag_ref[1] == 1
    first_y = flag_ref[2] == 1
    sub = lax.broadcasted_iota(jnp.int32, (rows, lanes), 0)
    lane = lax.broadcasted_iota(jnp.int32, (rows, lanes), 1)

    def full(value):
        return jnp.broadcast_to(value, (rows, lanes))

    def next_x(tile, edge):
        return jnp.where(sub == rows - 1, full(edge), pltpu.roll(tile, rows - 1, 0))

    def prev_x(tile, edge):
        return jnp.where(sub == 0, full(edge), pltpu.roll(tile, 1, 0))

    def next_y(tile, edge):
        return jnp.where(lane == lanes - 1, full(edge), pltpu.roll(tile, lanes - 1, 1))

    def prev_y(tile, edge):
        return jnp.where(lane == 0, full(edge), pltpu.roll(tile, 1, 1))

    def row(z, below, above, first_row):
        ex, ey, ez = e_ref[0, z], e_ref[1, z], e_ref[2, z]
        hx, hy, hz = h_ref[0, z], h_ref[1, z], h_ref[2, z]
        keep, curl, zrate, stiff = rate_ref[0, z], rate_ref[1, z], rate_ref[2, z], rate_ref[3, z]
        ey_xh, ez_xh = full(xh_ref[0, z]), full(xh_ref[1, z])
        ex_xl, ey_xl, hz_xl = full(xl_ref[0, z]), full(xl_ref[1, z]), full(xl_ref[2, z])
        ex_yh, ez_yh = full(yh_ref[0, z]), full(yh_ref[1, z])
        ex_yl, ey_yl, hz_yl = full(yl_ref[0, z]), full(yl_ref[1, z]), full(yl_ref[2, z])
        corner_ex = full(cex_ref[z])
        corner_ey = full(cey_ref[z])
        hz_new = hz - time_step * ((next_x(ey, ey_xh) - ey) - (next_y(ex, ex_yh) - ex))
        ex_py = prev_y(ex, ex_yl)
        ey_py = prev_y(ey, ey_yl)
        hz_py = prev_y(hz, hz_yl)
        face_py = (next_x(ey_py, prev_y(ey_xh, corner_ey)) - ey_py) - (ex - ex_py)
        hz_new_py = hz_py - time_step * face_py
        hz_new_py = jnp.where(jnp.logical_and(first_y, lane == 0), 0.0, hz_new_py)
        ex_px = prev_x(ex, ex_xl)
        ey_px = prev_x(ey, ey_xl)
        hz_px = prev_x(hz, hz_xl)
        face_px = (ey - ey_px) - (next_y(ex_px, prev_x(ex_yh, corner_ex)) - ex_px)
        hz_new_px = hz_px - time_step * face_px
        hz_new_px = jnp.where(jnp.logical_and(first_x, sub == 0), 0.0, hz_new_px)
        slope_zx = next_x(ez, ez_xh) - ez
        slope_zy = next_y(ez, ez_yh) - ez
        ex_b, ey_b, hx_b, hy_b, slope_zx_b, slope_zy_b = below
        ex_a, ey_a = above
        rise_x = ex - ex_b
        rise_y = ey - ey_b
        diag_ref[z] = 1.0 + 2.0 * stiff
        if first_row:
            rise_x = jnp.where(bottom, 0.0, rise_x)
            rise_y = jnp.where(bottom, 0.0, rise_y)
            diag_ref[z] = jnp.where(bottom, 1.0 + stiff, 1.0 + 2.0 * stiff)
        quarter_z = 0.25 * zrate
        sx_ref[z] = (
            keep * ex
            + stiff * ((ex_a - ex) - rise_x)
            + curl * (hz_new - hz_new_py)
            - zrate * (hy - hy_b)
            - quarter_z * (slope_zx - slope_zx_b)
        )
        sy_ref[z] = (
            keep * ey
            + stiff * ((ey_a - ey) - rise_y)
            + zrate * (hx - hx_b)
            - quarter_z * (slope_zy - slope_zy_b)
            - curl * (hz_new - hz_new_px)
        )
        hzn_ref[z] = hz_new
        szx_ref[z] = slope_zx
        szy_ref[z] = slope_zy
        return (ex, ey, hx, hy, slope_zx, slope_zy)

    zero = jnp.zeros((rows, lanes), jnp.float32)
    below = row(0, (zero,) * 6, (e_ref[0, 1], e_ref[1, 1]), True)

    def middle(z, below):
        return row(z, below, (e_ref[0, z + 1], e_ref[1, z + 1]), False)

    below = lax.fori_loop(1, depth - 1, middle, below, unroll=2)
    row(depth - 1, below, (zero, zero), False)
    thomas_kernel(
        rate_ref.at[3], diag_ref, sx_ref, sy_ref, px_ref, py_ref, lw_ref, hw_ref, edge_ref, ur_ref
    )
    edge_ref[8] = e_ref[0, depth - 1] + (h_ref[1, depth - 1] + 0.25 * szx_ref[depth - 1]) / 32.0
    edge_ref[9] = e_ref[1, depth - 1] + (0.25 * szy_ref[depth - 1] - h_ref[0, depth - 1]) / 32.0
    edge_ref[10] = e_ref[0, 0]
    edge_ref[11] = e_ref[1, 0]


def make_sources(flags, electric, magnetic, rate_stack, x_high, x_low, y_high, y_low,
                 corner_ex, corner_ey):
    shape = jax.ShapeDtypeStruct(electric.shape[1:], jnp.float32)
    edges = jax.ShapeDtypeStruct((12,) + electric.shape[2:], jnp.float32)
    vmem = pl.BlockSpec(memory_space=pltpu.VMEM)
    smem = pl.BlockSpec(memory_space=pltpu.SMEM)
    return pl.pallas_call(
        source_kernel,
        out_shape=(shape,) * 7 + (edges,),
        in_specs=[smem] + [vmem] * 9,
        out_specs=(vmem,) * 8,
        scratch_shapes=[pltpu.VMEM(electric.shape[1:], jnp.float32)] * 4,
    )(flags, electric, magnetic, rate_stack, x_high, x_low, y_high, y_low,
      corner_ex, corner_ey)


def advance(pieces, incoming, factor):
    rows_first, rows_last, low_first, low_last, high_first, high_last = pieces
    denominator = 1.0 - low_first * factor
    offset = (rows_first + low_first[None] * incoming) / denominator[None]
    coupling = high_first / denominator
    outgoing = rows_last + low_last[None] * (incoming + factor[None] * offset)
    factor_out = low_last * factor * coupling + high_last
    return (offset, coupling, outgoing, factor_out)


def body(electric, magnetic, material, layer_map, permittivity, conductivity):
    epsilon_cell = lookup(permittivity, layer_map, material)
    sigma_cell = lookup(conductivity, layer_map, material)
    keep_rate, curl_rate, z_rate, stiffness = rates(epsilon_cell, sigma_cell)
    depth_rows, span_x, span_y = material.shape
    slab = lax.axis_index("gz")
    bottom = slab == 0
    first_x = lax.axis_index("gx") == 0
    first_y = lax.axis_index("gy") == 0
    electric_x, electric_y, electric_z = (electric[0], electric[1], electric[2])
    magnetic_x, magnetic_y, magnetic_z = (magnetic[0], magnetic[1], magnetic[2])

    x_high = from_next(jnp.stack([electric_y[:, :1], electric_z[:, :1]]), "gx")
    x_low = from_prev(
        jnp.stack([electric_x[:, -1:], electric_y[:, -1:], magnetic_z[:, -1:]]), "gx"
    )
    y_high = from_next(jnp.stack([electric_x[:, :, :1], electric_z[:, :, :1]]), "gy")
    y_low = from_prev(
        jnp.stack([electric_x[:, :, -1:], electric_y[:, :, -1:], magnetic_z[:, :, -1:]]), "gy"
    )
    corner_ex = from_diagonal(electric_x[:, -1:, :1], ("gx", "gy"), 1, -1)
    corner_ey = from_diagonal(electric_y[:, :1, -1:], ("gx", "gy"), -1, 1)

    flags = jnp.stack([bottom, first_x, first_y]).astype(jnp.int32)
    rate_stack = jnp.stack([keep_rate, curl_rate, z_rate, stiffness])
    (magnetic_z_new, slope_zx, slope_zy, partial_x, partial_y, low_weight, high_weight,
     own) = make_sources(
        flags, electric, magnetic, rate_stack, x_high, x_low, y_high, y_low,
        corner_ex, corner_ey,
    )
    slab_count = lax.axis_size("gz")
    gathered = [own]
    for shift in range(1, slab_count):
        gathered.append(
            lax.ppermute(own, "gz", [(i, (i + shift) % slab_count) for i in range(slab_count)])
        )
    gathered = jnp.stack(gathered)
    slabs = []
    for index in range(slab_count):
        chosen = lax.dynamic_index_in_dim(
            gathered, (slab - index) % slab_count, axis=0, keepdims=False
        )
        slabs.append(chosen)
    zero_pair = jnp.zeros((2,) + partial_x.shape[1:], jnp.float32)
    below_all = [zero_pair] + [slabs[index][8:10] for index in range(slab_count - 1)]
    above_all = [slabs[index][10:12] for index in range(1, slab_count)] + [zero_pair]
    for index in range(slab_count):
        chosen = slabs[index]
        low_first, low_last, high_first, high_last = chosen[4], chosen[5], chosen[6], chosen[7]
        rows_first = (
            chosen[0:2] + below_all[index] * low_first[None] + above_all[index] * high_first[None]
        )
        rows_last = (
            chosen[2:4] + below_all[index] * low_last[None] + above_all[index] * high_last[None]
        )
        slabs[index] = (rows_first, rows_last, low_first, low_last, high_first, high_last)

    incoming_all = []
    factor_all = []
    offset_all = []
    coupling_all = []
    incoming = jnp.zeros((2,) + partial_x.shape[1:], jnp.float32)
    factor = jnp.zeros_like(low_weight[0])
    for index in range(slab_count):
        if index > 0:
            incoming, factor = outgoing, factor_out
        offset, coupling, outgoing, factor_out = advance(slabs[index], incoming, factor)
        incoming_all.append(incoming)
        factor_all.append(factor)
        offset_all.append(offset)
        coupling_all.append(coupling)
    following_all = [None] * slab_count
    leading_all = [None] * slab_count
    following = jnp.zeros((2,) + partial_x.shape[1:], jnp.float32)
    for index in reversed(range(slab_count)):
        if index < slab_count - 1:
            following = leading_all[index + 1]
        following_all[index] = following
        leading_all[index] = offset_all[index] + coupling_all[index][None] * following

    def pick(values):
        return lax.dynamic_index_in_dim(jnp.stack(values), slab, axis=0, keepdims=False)

    incoming = pick(incoming_all)
    factor = pick(factor_all)
    following = pick(following_all)
    leading = pick(leading_all)
    below = pick(below_all)
    above = pick(above_all)

    previous_last = incoming + factor[None] * leading + below
    following = following + above
    electric_x_new = (
        partial_x + previous_last[0][None] * low_weight + following[0][None] * high_weight
    )
    electric_y_new = (
        partial_y + previous_last[1][None] * low_weight + following[1][None] * high_weight
    )
    sum_x = electric_x + electric_x_new
    sum_y = electric_y + electric_y_new
    top_x = following[0]
    top_y = following[1]
    rise_x = jnp.concatenate([sum_x[1:], top_x[None]], axis=0) - sum_x
    rise_y = jnp.concatenate([sum_y[1:], top_y[None]], axis=0) - sum_y
    magnetic_y_new = magnetic_y - 0.5 * z_courant * rise_x + time_step * slope_zx
    magnetic_x_new = magnetic_x - time_step * slope_zy + 0.5 * z_courant * rise_y
    before_hy = from_prev(magnetic_y_new[:, -1:, :], "gx")
    before_hx = from_prev(magnetic_x_new[:, :, -1:], "gy")
    change_hy = magnetic_y_new - jnp.concatenate([before_hy, magnetic_y_new[:, :-1]], axis=1)
    change_hx = magnetic_x_new - jnp.concatenate([before_hx, magnetic_x_new[:, :, :-1]], axis=2)
    electric_z_new = keep_rate * electric_z + curl_rate * (change_hy - change_hx)
    return (
        jnp.stack([electric_x_new, electric_y_new, electric_z_new]),
        jnp.stack([magnetic_x_new, magnetic_y_new, magnetic_z_new]),
    )


def solution(mesh):
    return jax.shard_map(
        body,
        mesh=mesh,
        in_specs=(
            P(None, "gz", "gx", "gy"),
            P(None, "gz", "gx", "gy"),
            P("gz", "gx", "gy"),
            P("gz"),
            P(),
            P(),
        ),
        out_specs=(P(None, "gz", "gx", "gy"), P(None, "gz", "gx", "gy")),
        check_vma=False,
    )
```

```python
import jax
import jax.numpy as jnp
from jax import lax
from jax.sharding import PartitionSpec as P
from jax.experimental import pallas as pl
from jax.experimental.pallas import tpu as pltpu

time_step = 0.5
z_courant = 128.0


def from_prev(block, axis):
    count = lax.axis_size(axis)
    return lax.ppermute(block, axis, [(i, i + 1) for i in range(count - 1)])


def from_next(block, axis):
    count = lax.axis_size(axis)
    return lax.ppermute(block, axis, [(i + 1, i) for i in range(count - 1)])


def from_diagonal(block, axes, step_a, step_b):
    size_a = lax.axis_size(axes[0])
    size_b = lax.axis_size(axes[1])
    pairs = []
    for a in range(size_a):
        for b in range(size_b):
            src_a, src_b = a - step_a, b - step_b
            if 0 <= src_a < size_a and 0 <= src_b < size_b:
                pairs.append((src_a * size_b + src_b, a * size_b + b))
    return lax.ppermute(block, axes, pairs)


def lookup(table_values, layer_map, material):
    kind_count, entry_count = table_values.shape
    layer_hot = layer_map[:, None] == lax.broadcasted_iota(jnp.int32, (1, kind_count), 1)
    table_rows = jnp.sum(jnp.where(layer_hot[:, :, None], table_values[None], 0.0), axis=1)
    result = jnp.zeros(material.shape, jnp.float32)
    for entry_index in range(entry_count):
        result = result + jnp.where(
            material == entry_index, table_rows[:, entry_index][:, None, None], 0.0
        )
    return result


def rates(epsilon_cell, sigma_cell):
    half_loss = 0.25 * sigma_cell / epsilon_cell
    drive_rate = 1.0 / (1.0 + half_loss)
    keep_rate = (1.0 - half_loss) * drive_rate
    curl_rate = 0.5 * drive_rate / epsilon_cell
    z_rate = z_courant * drive_rate / epsilon_cell
    stiffness = 4096.0 * drive_rate / epsilon_cell
    return (keep_rate, curl_rate, z_rate, stiffness)


def thomas_kernel(
    stiff_ref, diag_ref, sx_ref, sy_ref, px_ref, py_ref, lw_ref, hw_ref, edge_ref, ur_ref
):
    depth = stiff_ref.shape[0]
    stiff = stiff_ref[0]
    inv = 1.0 / diag_ref[0]
    ur_ref[0] = -stiff * inv
    px_ref[0] = sx_ref[0] * inv
    py_ref[0] = sy_ref[0] * inv
    lw_ref[0] = inv

    def forward(z, carry):
        upper, value_x, value_y, value_low, unused = carry
        stiff = stiff_ref[z]
        inv = 1.0 / (diag_ref[z] + stiff * upper)
        upper = -stiff * inv
        value_x = (sx_ref[z] + stiff * value_x) * inv
        value_y = (sy_ref[z] + stiff * value_y) * inv
        value_low = (stiff * value_low) * inv
        ur_ref[z] = upper
        px_ref[z] = value_x
        py_ref[z] = value_y
        lw_ref[z] = value_low
        return upper, value_x, value_y, value_low, inv

    first = (ur_ref[0], px_ref[0], py_ref[0], lw_ref[0], inv)
    last_x, last_y, last_low, last_high = lax.fori_loop(1, depth, forward, first, unroll=8)[1:]
    low_scale = stiff_ref[0]
    high_scale = stiff_ref[depth - 1]
    lw_ref[depth - 1] = low_scale * last_low
    hw_ref[depth - 1] = high_scale * last_high

    def backward(step, carry):
        z = depth - 2 - step
        next_x, next_y, next_low, next_high = carry
        upper = ur_ref[z]
        next_x = px_ref[z] - upper * next_x
        next_y = py_ref[z] - upper * next_y
        next_low = lw_ref[z] - upper * next_low
        next_high = -upper * next_high
        px_ref[z] = next_x
        py_ref[z] = next_y
        lw_ref[z] = low_scale * next_low
        hw_ref[z] = high_scale * next_high
        return next_x, next_y, next_low, next_high

    lax.fori_loop(0, depth - 1, backward, (last_x, last_y, last_low, last_high), unroll=8)
    edge_ref[0] = px_ref[0]
    edge_ref[1] = py_ref[0]
    edge_ref[2] = px_ref[depth - 1]
    edge_ref[3] = py_ref[depth - 1]
    edge_ref[4] = lw_ref[0]
    edge_ref[5] = lw_ref[depth - 1]
    edge_ref[6] = hw_ref[0]
    edge_ref[7] = hw_ref[depth - 1]


def solve_slab(stiffness, diagonal, source_x, source_y):
    shape = jax.ShapeDtypeStruct(stiffness.shape, jnp.float32)
    edges = jax.ShapeDtypeStruct((8,) + stiffness.shape[1:], jnp.float32)
    return pl.pallas_call(
        thomas_kernel,
        out_shape=(shape, shape, shape, shape, edges),
        scratch_shapes=[pltpu.VMEM(stiffness.shape, jnp.float32)],
    )(stiffness, diagonal, source_x, source_y)


def source_kernel(
    flag_ref, e_ref, h_ref, rate_ref, xh_ref, xl_ref, yh_ref, yl_ref,
    cex_ref, cey_ref, hzn_ref, szx_ref, szy_ref, px_ref, py_ref, lw_ref, hw_ref, edge_ref,
    sx_ref, sy_ref, diag_ref, ur_ref,
):
    depth, rows, lanes = sx_ref.shape
    bottom = flag_ref[0] == 1
    first_x = flag_ref[1] == 1
    first_y = flag_ref[2] == 1
    sub = lax.broadcasted_iota(jnp.int32, (rows, lanes), 0)
    lane = lax.broadcasted_iota(jnp.int32, (rows, lanes), 1)

    def full(value):
        return jnp.broadcast_to(value, (rows, lanes))

    def next_x(tile, edge):
        return jnp.where(sub == rows - 1, full(edge), pltpu.roll(tile, rows - 1, 0))

    def prev_x(tile, edge):
        return jnp.where(sub == 0, full(edge), pltpu.roll(tile, 1, 0))

    def next_y(tile, edge):
        return jnp.where(lane == lanes - 1, full(edge), pltpu.roll(tile, lanes - 1, 1))

    def prev_y(tile, edge):
        return jnp.where(lane == 0, full(edge), pltpu.roll(tile, 1, 1))

    def row(z, below, above, first_row):
        ex, ey, ez = e_ref[0, z], e_ref[1, z], e_ref[2, z]
        hx, hy, hz = h_ref[0, z], h_ref[1, z], h_ref[2, z]
        keep, curl, zrate, stiff = rate_ref[0, z], rate_ref[1, z], rate_ref[2, z], rate_ref[3, z]
        ey_xh, ez_xh = full(xh_ref[0, z]), full(xh_ref[1, z])
        ex_xl, ey_xl, hz_xl = full(xl_ref[0, z]), full(xl_ref[1, z]), full(xl_ref[2, z])
        ex_yh, ez_yh = full(yh_ref[0, z]), full(yh_ref[1, z])
        ex_yl, ey_yl, hz_yl = full(yl_ref[0, z]), full(yl_ref[1, z]), full(yl_ref[2, z])
        corner_ex = full(cex_ref[z])
        corner_ey = full(cey_ref[z])
        hz_new = hz - time_step * ((next_x(ey, ey_xh) - ey) - (next_y(ex, ex_yh) - ex))
        ex_py = prev_y(ex, ex_yl)
        ey_py = prev_y(ey, ey_yl)
        hz_py = prev_y(hz, hz_yl)
        face_py = (next_x(ey_py, prev_y(ey_xh, corner_ey)) - ey_py) - (ex - ex_py)
        hz_new_py = hz_py - time_step * face_py
        hz_new_py = jnp.where(jnp.logical_and(first_y, lane == 0), 0.0, hz_new_py)
        ex_px = prev_x(ex, ex_xl)
        ey_px = prev_x(ey, ey_xl)
        hz_px = prev_x(hz, hz_xl)
        face_px = (ey - ey_px) - (next_y(ex_px, prev_x(ex_yh, corner_ex)) - ex_px)
        hz_new_px = hz_px - time_step * face_px
        hz_new_px = jnp.where(jnp.logical_and(first_x, sub == 0), 0.0, hz_new_px)
        slope_zx = next_x(ez, ez_xh) - ez
        slope_zy = next_y(ez, ez_yh) - ez
        ex_b, ey_b, hx_b, hy_b, slope_zx_b, slope_zy_b = below
        ex_a, ey_a = above
        rise_x = ex - ex_b
        rise_y = ey - ey_b
        diag_ref[z] = 1.0 + 2.0 * stiff
        if first_row:
            rise_x = jnp.where(bottom, 0.0, rise_x)
            rise_y = jnp.where(bottom, 0.0, rise_y)
            diag_ref[z] = jnp.where(bottom, 1.0 + stiff, 1.0 + 2.0 * stiff)
        quarter_z = 0.25 * zrate
        sx_ref[z] = (
            keep * ex
            + stiff * ((ex_a - ex) - rise_x)
            + curl * (hz_new - hz_new_py)
            - zrate * (hy - hy_b)
            - quarter_z * (slope_zx - slope_zx_b)
        )
        sy_ref[z] = (
            keep * ey
            + stiff * ((ey_a - ey) - rise_y)
            + zrate * (hx - hx_b)
            - quarter_z * (slope_zy - slope_zy_b)
            - curl * (hz_new - hz_new_px)
        )
        hzn_ref[z] = hz_new
        szx_ref[z] = slope_zx
        szy_ref[z] = slope_zy
        return (ex, ey, hx, hy, slope_zx, slope_zy)

    zero = jnp.zeros((rows, lanes), jnp.float32)
    below = row(0, (zero,) * 6, (e_ref[0, 1], e_ref[1, 1]), True)

    def middle(z, below):
        return row(z, below, (e_ref[0, z + 1], e_ref[1, z + 1]), False)

    below = lax.fori_loop(1, depth - 1, middle, below, unroll=2)
    row(depth - 1, below, (zero, zero), False)
    thomas_kernel(
        rate_ref.at[3], diag_ref, sx_ref, sy_ref, px_ref, py_ref, lw_ref, hw_ref, edge_ref, ur_ref
    )
    edge_ref[8] = e_ref[0, depth - 1] + (h_ref[1, depth - 1] + 0.25 * szx_ref[depth - 1]) / 32.0
    edge_ref[9] = e_ref[1, depth - 1] + (0.25 * szy_ref[depth - 1] - h_ref[0, depth - 1]) / 32.0
    edge_ref[10] = e_ref[0, 0]
    edge_ref[11] = e_ref[1, 0]


def make_sources(flags, electric, magnetic, rate_stack, x_high, x_low, y_high, y_low,
                 corner_ex, corner_ey):
    shape = jax.ShapeDtypeStruct(electric.shape[1:], jnp.float32)
    edges = jax.ShapeDtypeStruct((12,) + electric.shape[2:], jnp.float32)
    vmem = pl.BlockSpec(memory_space=pltpu.VMEM)
    smem = pl.BlockSpec(memory_space=pltpu.SMEM)
    return pl.pallas_call(
        source_kernel,
        out_shape=(shape,) * 7 + (edges,),
        in_specs=[smem] + [vmem] * 9,
        out_specs=(vmem,) * 8,
        scratch_shapes=[pltpu.VMEM(electric.shape[1:], jnp.float32)] * 4,
    )(flags, electric, magnetic, rate_stack, x_high, x_low, y_high, y_low,
      corner_ex, corner_ey)


def advance(pieces, incoming, factor):
    rows_first, rows_last, low_first, low_last, high_first, high_last = pieces
    denominator = 1.0 - low_first * factor
    offset = (rows_first + low_first[None] * incoming) / denominator[None]
    coupling = high_first / denominator
    outgoing = rows_last + low_last[None] * (incoming + factor[None] * offset)
    factor_out = low_last * factor * coupling + high_last
    return (offset, coupling, outgoing, factor_out)


def body(electric, magnetic, material, layer_map, permittivity, conductivity):
    epsilon_cell = lookup(permittivity, layer_map, material)
    sigma_cell = lookup(conductivity, layer_map, material)
    keep_rate, curl_rate, z_rate, stiffness = rates(epsilon_cell, sigma_cell)
    depth_rows, span_x, span_y = material.shape
    slab = lax.axis_index("gz")
    bottom = slab == 0
    first_x = lax.axis_index("gx") == 0
    first_y = lax.axis_index("gy") == 0
    electric_x, electric_y, electric_z = (electric[0], electric[1], electric[2])
    magnetic_x, magnetic_y, magnetic_z = (magnetic[0], magnetic[1], magnetic[2])

    x_high = from_next(jnp.stack([electric_y[:, :1], electric_z[:, :1]]), "gx")
    x_low = from_prev(
        jnp.stack([electric_x[:, -1:], electric_y[:, -1:], magnetic_z[:, -1:]]), "gx"
    )
    y_high = from_next(jnp.stack([electric_x[:, :, :1], electric_z[:, :, :1]]), "gy")
    y_low = from_prev(
        jnp.stack([electric_x[:, :, -1:], electric_y[:, :, -1:], magnetic_z[:, :, -1:]]), "gy"
    )
    corner_ex = from_diagonal(electric_x[:, -1:, :1], ("gx", "gy"), 1, -1)
    corner_ey = from_diagonal(electric_y[:, :1, -1:], ("gx", "gy"), -1, 1)

    flags = jnp.stack([bottom, first_x, first_y]).astype(jnp.int32)
    rate_stack = jnp.stack([keep_rate, curl_rate, z_rate, stiffness])
    (magnetic_z_new, slope_zx, slope_zy, partial_x, partial_y, low_weight, high_weight,
     own) = make_sources(
        flags, electric, magnetic, rate_stack, x_high, x_low, y_high, y_low,
        corner_ex, corner_ey,
    )
    slab_count = lax.axis_size("gz")
    gathered = lax.all_to_all(
        jnp.broadcast_to(own[None], (slab_count,) + own.shape), "gz", 0, 0
    )
    slabs = [gathered[index] for index in range(slab_count)]
    zero_pair = jnp.zeros((2,) + partial_x.shape[1:], jnp.float32)
    below_all = [zero_pair] + [slabs[index][8:10] for index in range(slab_count - 1)]
    above_all = [slabs[index][10:12] for index in range(1, slab_count)] + [zero_pair]
    for index in range(slab_count):
        chosen = slabs[index]
        low_first, low_last, high_first, high_last = chosen[4], chosen[5], chosen[6], chosen[7]
        rows_first = (
            chosen[0:2] + below_all[index] * low_first[None] + above_all[index] * high_first[None]
        )
        rows_last = (
            chosen[2:4] + below_all[index] * low_last[None] + above_all[index] * high_last[None]
        )
        slabs[index] = (rows_first, rows_last, low_first, low_last, high_first, high_last)

    incoming_all = []
    factor_all = []
    offset_all = []
    coupling_all = []
    incoming = jnp.zeros((2,) + partial_x.shape[1:], jnp.float32)
    factor = jnp.zeros_like(low_weight[0])
    for index in range(slab_count):
        if index > 0:
            incoming, factor = outgoing, factor_out
        offset, coupling, outgoing, factor_out = advance(slabs[index], incoming, factor)
        incoming_all.append(incoming)
        factor_all.append(factor)
        offset_all.append(offset)
        coupling_all.append(coupling)
    following_all = [None] * slab_count
    leading_all = [None] * slab_count
    following = jnp.zeros((2,) + partial_x.shape[1:], jnp.float32)
    for index in reversed(range(slab_count)):
        if index < slab_count - 1:
            following = leading_all[index + 1]
        following_all[index] = following
        leading_all[index] = offset_all[index] + coupling_all[index][None] * following

    def pick(values):
        return lax.dynamic_index_in_dim(jnp.stack(values), slab, axis=0, keepdims=False)

    incoming = pick(incoming_all)
    factor = pick(factor_all)
    following = pick(following_all)
    leading = pick(leading_all)
    below = pick(below_all)
    above = pick(above_all)

    previous_last = incoming + factor[None] * leading + below
    following = following + above
    electric_x_new = (
        partial_x + previous_last[0][None] * low_weight + following[0][None] * high_weight
    )
    electric_y_new = (
        partial_y + previous_last[1][None] * low_weight + following[1][None] * high_weight
    )
    sum_x = electric_x + electric_x_new
    sum_y = electric_y + electric_y_new
    top_x = following[0]
    top_y = following[1]
    rise_x = jnp.concatenate([sum_x[1:], top_x[None]], axis=0) - sum_x
    rise_y = jnp.concatenate([sum_y[1:], top_y[None]], axis=0) - sum_y
    magnetic_y_new = magnetic_y - 0.5 * z_courant * rise_x + time_step * slope_zx
    magnetic_x_new = magnetic_x - time_step * slope_zy + 0.5 * z_courant * rise_y
    before_hy = from_prev(magnetic_y_new[:, -1:, :], "gx")
    before_hx = from_prev(magnetic_x_new[:, :, -1:], "gy")
    change_hy = magnetic_y_new - jnp.concatenate([before_hy, magnetic_y_new[:, :-1]], axis=1)
    change_hx = magnetic_x_new - jnp.concatenate([before_hx, magnetic_x_new[:, :, :-1]], axis=2)
    electric_z_new = keep_rate * electric_z + curl_rate * (change_hy - change_hx)
    return (
        jnp.stack([electric_x_new, electric_y_new, electric_z_new]),
        jnp.stack([magnetic_x_new, magnetic_y_new, magnetic_z_new]),
    )


def solution(mesh):
    return jax.shard_map(
        body,
        mesh=mesh,
        in_specs=(
            P(None, "gz", "gx", "gy"),
            P(None, "gz", "gx", "gy"),
            P("gz", "gx", "gy"),
            P("gz"),
            P(),
            P(),
        ),
        out_specs=(P(None, "gz", "gx", "gy"), P(None, "gz", "gx", "gy")),
        check_vma=False,
    )
```

```python
import jax
import jax.numpy as jnp
from jax import lax
from jax.sharding import PartitionSpec as P
from jax.experimental import pallas as pl
from jax.experimental.pallas import tpu as pltpu

time_step = 0.5
z_courant = 128.0


def from_prev(block, axis):
    count = lax.axis_size(axis)
    return lax.ppermute(block, axis, [(i, i + 1) for i in range(count - 1)])


def from_next(block, axis):
    count = lax.axis_size(axis)
    return lax.ppermute(block, axis, [(i + 1, i) for i in range(count - 1)])


def from_diagonal(block, axes, step_a, step_b):
    size_a = lax.axis_size(axes[0])
    size_b = lax.axis_size(axes[1])
    pairs = []
    for a in range(size_a):
        for b in range(size_b):
            src_a, src_b = a - step_a, b - step_b
            if 0 <= src_a < size_a and 0 <= src_b < size_b:
                pairs.append((src_a * size_b + src_b, a * size_b + b))
    return lax.ppermute(block, axes, pairs)


def lookup(table_values, layer_map, material):
    kind_count, entry_count = table_values.shape
    layer_hot = layer_map[:, None] == lax.broadcasted_iota(jnp.int32, (1, kind_count), 1)
    table_rows = jnp.sum(jnp.where(layer_hot[:, :, None], table_values[None], 0.0), axis=1)
    result = jnp.zeros(material.shape, jnp.float32)
    for entry_index in range(entry_count):
        result = result + jnp.where(
            material == entry_index, table_rows[:, entry_index][:, None, None], 0.0
        )
    return result


def rates(epsilon_cell, sigma_cell):
    half_loss = 0.25 * sigma_cell / epsilon_cell
    drive_rate = 1.0 / (1.0 + half_loss)
    keep_rate = (1.0 - half_loss) * drive_rate
    curl_rate = 0.5 * drive_rate / epsilon_cell
    z_rate = z_courant * drive_rate / epsilon_cell
    stiffness = 4096.0 * drive_rate / epsilon_cell
    return (keep_rate, curl_rate, z_rate, stiffness)


def thomas_kernel(
    stiff_ref, diag_ref, sx_ref, sy_ref, px_ref, py_ref, lw_ref, hw_ref, edge_ref, ur_ref
):
    depth = stiff_ref.shape[0]
    stiff = stiff_ref[0]
    inv = 1.0 / diag_ref[0]
    ur_ref[0] = -stiff * inv
    px_ref[0] = sx_ref[0] * inv
    py_ref[0] = sy_ref[0] * inv
    lw_ref[0] = inv

    def forward(z, carry):
        upper, value_x, value_y, value_low, unused = carry
        stiff = stiff_ref[z]
        inv = 1.0 / (diag_ref[z] + stiff * upper)
        upper = -stiff * inv
        value_x = (sx_ref[z] + stiff * value_x) * inv
        value_y = (sy_ref[z] + stiff * value_y) * inv
        value_low = (stiff * value_low) * inv
        ur_ref[z] = upper
        px_ref[z] = value_x
        py_ref[z] = value_y
        lw_ref[z] = value_low
        return upper, value_x, value_y, value_low, inv

    first = (ur_ref[0], px_ref[0], py_ref[0], lw_ref[0], inv)
    last_x, last_y, last_low, last_high = lax.fori_loop(1, depth, forward, first, unroll=8)[1:]
    low_scale = stiff_ref[0]
    high_scale = stiff_ref[depth - 1]
    lw_ref[depth - 1] = low_scale * last_low
    hw_ref[depth - 1] = high_scale * last_high

    def backward(step, carry):
        z = depth - 2 - step
        next_x, next_y, next_low, next_high = carry
        upper = ur_ref[z]
        next_x = px_ref[z] - upper * next_x
        next_y = py_ref[z] - upper * next_y
        next_low = lw_ref[z] - upper * next_low
        next_high = -upper * next_high
        px_ref[z] = next_x
        py_ref[z] = next_y
        lw_ref[z] = low_scale * next_low
        hw_ref[z] = high_scale * next_high
        return next_x, next_y, next_low, next_high

    lax.fori_loop(0, depth - 1, backward, (last_x, last_y, last_low, last_high), unroll=8)
    edge_ref[0] = px_ref[0]
    edge_ref[1] = py_ref[0]
    edge_ref[2] = px_ref[depth - 1]
    edge_ref[3] = py_ref[depth - 1]
    edge_ref[4] = lw_ref[0]
    edge_ref[5] = lw_ref[depth - 1]
    edge_ref[6] = hw_ref[0]
    edge_ref[7] = hw_ref[depth - 1]


def solve_slab(stiffness, diagonal, source_x, source_y):
    shape = jax.ShapeDtypeStruct(stiffness.shape, jnp.float32)
    edges = jax.ShapeDtypeStruct((8,) + stiffness.shape[1:], jnp.float32)
    return pl.pallas_call(
        thomas_kernel,
        out_shape=(shape, shape, shape, shape, edges),
        scratch_shapes=[pltpu.VMEM(stiffness.shape, jnp.float32)],
    )(stiffness, diagonal, source_x, source_y)


def source_kernel(
    flag_ref, e_ref, h_ref, rate_ref, xh_ref, xl_ref, yh_ref, yl_ref,
    cex_ref, cey_ref, hzn_ref, szx_ref, szy_ref, px_ref, py_ref, lw_ref, hw_ref, edge_ref,
    sx_ref, sy_ref, diag_ref, ur_ref,
):
    depth, rows, lanes = sx_ref.shape
    bottom = flag_ref[0] == 1
    first_x = flag_ref[1] == 1
    first_y = flag_ref[2] == 1
    sub = lax.broadcasted_iota(jnp.int32, (rows, lanes), 0)
    lane = lax.broadcasted_iota(jnp.int32, (rows, lanes), 1)

    def full(value):
        return jnp.broadcast_to(value, (rows, lanes))

    def next_x(tile, edge):
        return jnp.where(sub == rows - 1, full(edge), pltpu.roll(tile, rows - 1, 0))

    def prev_x(tile, edge):
        return jnp.where(sub == 0, full(edge), pltpu.roll(tile, 1, 0))

    def next_y(tile, edge):
        return jnp.where(lane == lanes - 1, full(edge), pltpu.roll(tile, lanes - 1, 1))

    def prev_y(tile, edge):
        return jnp.where(lane == 0, full(edge), pltpu.roll(tile, 1, 1))

    def row(z, below, above, first_row):
        ex, ey, ez = e_ref[0, z], e_ref[1, z], e_ref[2, z]
        hx, hy, hz = h_ref[0, z], h_ref[1, z], h_ref[2, z]
        keep, curl, zrate, stiff = rate_ref[0, z], rate_ref[1, z], rate_ref[2, z], rate_ref[3, z]
        ey_xh, ez_xh = full(xh_ref[0, z]), full(xh_ref[1, z])
        ex_xl, ey_xl, hz_xl = full(xl_ref[0, z]), full(xl_ref[1, z]), full(xl_ref[2, z])
        ex_yh, ez_yh = full(yh_ref[0, z]), full(yh_ref[1, z])
        ex_yl, ey_yl, hz_yl = full(yl_ref[0, z]), full(yl_ref[1, z]), full(yl_ref[2, z])
        corner_ex = full(cex_ref[z])
        corner_ey = full(cey_ref[z])
        hz_new = hz - time_step * ((next_x(ey, ey_xh) - ey) - (next_y(ex, ex_yh) - ex))
        ex_py = prev_y(ex, ex_yl)
        ey_py = prev_y(ey, ey_yl)
        hz_py = prev_y(hz, hz_yl)
        face_py = (next_x(ey_py, prev_y(ey_xh, corner_ey)) - ey_py) - (ex - ex_py)
        hz_new_py = hz_py - time_step * face_py
        hz_new_py = jnp.where(jnp.logical_and(first_y, lane == 0), 0.0, hz_new_py)
        ex_px = prev_x(ex, ex_xl)
        ey_px = prev_x(ey, ey_xl)
        hz_px = prev_x(hz, hz_xl)
        face_px = (ey - ey_px) - (next_y(ex_px, prev_x(ex_yh, corner_ex)) - ex_px)
        hz_new_px = hz_px - time_step * face_px
        hz_new_px = jnp.where(jnp.logical_and(first_x, sub == 0), 0.0, hz_new_px)
        slope_zx = next_x(ez, ez_xh) - ez
        slope_zy = next_y(ez, ez_yh) - ez
        ex_b, ey_b, hx_b, hy_b, slope_zx_b, slope_zy_b = below
        ex_a, ey_a = above
        rise_x = ex - ex_b
        rise_y = ey - ey_b
        diag_ref[z] = 1.0 + 2.0 * stiff
        if first_row:
            rise_x = jnp.where(bottom, 0.0, rise_x)
            rise_y = jnp.where(bottom, 0.0, rise_y)
            diag_ref[z] = jnp.where(bottom, 1.0 + stiff, 1.0 + 2.0 * stiff)
        quarter_z = 0.25 * zrate
        sx_ref[z] = (
            keep * ex
            + stiff * ((ex_a - ex) - rise_x)
            + curl * (hz_new - hz_new_py)
            - zrate * (hy - hy_b)
            - quarter_z * (slope_zx - slope_zx_b)
        )
        sy_ref[z] = (
            keep * ey
            + stiff * ((ey_a - ey) - rise_y)
            + zrate * (hx - hx_b)
            - quarter_z * (slope_zy - slope_zy_b)
            - curl * (hz_new - hz_new_px)
        )
        hzn_ref[z] = hz_new
        szx_ref[z] = slope_zx
        szy_ref[z] = slope_zy
        return (ex, ey, hx, hy, slope_zx, slope_zy)

    zero = jnp.zeros((rows, lanes), jnp.float32)
    below = row(0, (zero,) * 6, (e_ref[0, 1], e_ref[1, 1]), True)

    def middle(z, below):
        return row(z, below, (e_ref[0, z + 1], e_ref[1, z + 1]), False)

    below = lax.fori_loop(1, depth - 1, middle, below, unroll=2)
    row(depth - 1, below, (zero, zero), False)
    thomas_kernel(
        rate_ref.at[3], diag_ref, sx_ref, sy_ref, px_ref, py_ref, lw_ref, hw_ref, edge_ref, ur_ref
    )
    edge_ref[8] = e_ref[0, depth - 1] + (h_ref[1, depth - 1] + 0.25 * szx_ref[depth - 1]) / 32.0
    edge_ref[9] = e_ref[1, depth - 1] + (0.25 * szy_ref[depth - 1] - h_ref[0, depth - 1]) / 32.0
    edge_ref[10] = e_ref[0, 0]
    edge_ref[11] = e_ref[1, 0]


def make_sources(flags, electric, magnetic, rate_stack, x_high, x_low, y_high, y_low,
                 corner_ex, corner_ey):
    shape = jax.ShapeDtypeStruct(electric.shape[1:], jnp.float32)
    edges = jax.ShapeDtypeStruct((12,) + electric.shape[2:], jnp.float32)
    vmem = pl.BlockSpec(memory_space=pltpu.VMEM)
    smem = pl.BlockSpec(memory_space=pltpu.SMEM)
    return pl.pallas_call(
        source_kernel,
        out_shape=(shape,) * 7 + (edges,),
        in_specs=[smem] + [vmem] * 9,
        out_specs=(vmem,) * 8,
        scratch_shapes=[pltpu.VMEM(electric.shape[1:], jnp.float32)] * 4,
    )(flags, electric, magnetic, rate_stack, x_high, x_low, y_high, y_low,
      corner_ex, corner_ey)


def finish_kernel(
    e_ref, h_ref, px_ref, py_ref, lw_ref, hw_ref, szx_ref, szy_ref, coef_ref,
    exn_ref, eyn_ref, hxn_ref, hyn_ref,
):
    depth = px_ref.shape[0]
    last_x, last_y, next_x, next_y = coef_ref[0], coef_ref[1], coef_ref[2], coef_ref[3]

    def sums(z):
        new_x = px_ref[z] + last_x * lw_ref[z] + next_x * hw_ref[z]
        new_y = py_ref[z] + last_y * lw_ref[z] + next_y * hw_ref[z]
        exn_ref[z] = new_x
        eyn_ref[z] = new_y
        return e_ref[0, z] + new_x, e_ref[1, z] + new_y

    def write(z, sum_x, sum_y, up_x, up_y):
        rise_x = up_x - sum_x
        rise_y = up_y - sum_y
        hyn_ref[z] = h_ref[1, z] - 0.5 * z_courant * rise_x + time_step * szx_ref[z]
        hxn_ref[z] = h_ref[0, z] - time_step * szy_ref[z] + 0.5 * z_courant * rise_y

    def step(z, carry):
        sum_x, sum_y = carry
        up_x, up_y = sums(z + 1)
        write(z, sum_x, sum_y, up_x, up_y)
        return up_x, up_y

    sum_x, sum_y = lax.fori_loop(0, depth - 1, step, sums(0), unroll=4)
    write(depth - 1, sum_x, sum_y, next_x, next_y)


def finish(electric, magnetic, px, py, lw, hw, slope_zx, slope_zy, coef):
    shape = jax.ShapeDtypeStruct(px.shape, jnp.float32)
    return pl.pallas_call(finish_kernel, out_shape=(shape,) * 4)(
        electric, magnetic, px, py, lw, hw, slope_zx, slope_zy, coef
    )


def advance(pieces, incoming, factor):
    rows_first, rows_last, low_first, low_last, high_first, high_last = pieces
    denominator = 1.0 - low_first * factor
    offset = (rows_first + low_first[None] * incoming) / denominator[None]
    coupling = high_first / denominator
    outgoing = rows_last + low_last[None] * (incoming + factor[None] * offset)
    factor_out = low_last * factor * coupling + high_last
    return (offset, coupling, outgoing, factor_out)


def body(electric, magnetic, material, layer_map, permittivity, conductivity):
    epsilon_cell = lookup(permittivity, layer_map, material)
    sigma_cell = lookup(conductivity, layer_map, material)
    keep_rate, curl_rate, z_rate, stiffness = rates(epsilon_cell, sigma_cell)
    depth_rows, span_x, span_y = material.shape
    slab = lax.axis_index("gz")
    bottom = slab == 0
    first_x = lax.axis_index("gx") == 0
    first_y = lax.axis_index("gy") == 0
    electric_x, electric_y, electric_z = (electric[0], electric[1], electric[2])
    magnetic_x, magnetic_y, magnetic_z = (magnetic[0], magnetic[1], magnetic[2])

    x_high = from_next(jnp.stack([electric_y[:, :1], electric_z[:, :1]]), "gx")
    x_low = from_prev(
        jnp.stack([electric_x[:, -1:], electric_y[:, -1:], magnetic_z[:, -1:]]), "gx"
    )
    y_high = from_next(jnp.stack([electric_x[:, :, :1], electric_z[:, :, :1]]), "gy")
    y_low = from_prev(
        jnp.stack([electric_x[:, :, -1:], electric_y[:, :, -1:], magnetic_z[:, :, -1:]]), "gy"
    )
    corner_ex = from_diagonal(electric_x[:, -1:, :1], ("gx", "gy"), 1, -1)
    corner_ey = from_diagonal(electric_y[:, :1, -1:], ("gx", "gy"), -1, 1)

    flags = jnp.stack([bottom, first_x, first_y]).astype(jnp.int32)
    rate_stack = jnp.stack([keep_rate, curl_rate, z_rate, stiffness])
    (magnetic_z_new, slope_zx, slope_zy, partial_x, partial_y, low_weight, high_weight,
     own) = make_sources(
        flags, electric, magnetic, rate_stack, x_high, x_low, y_high, y_low,
        corner_ex, corner_ey,
    )
    slab_count = lax.axis_size("gz")
    gathered = [own]
    for shift in range(1, slab_count):
        gathered.append(
            lax.ppermute(own, "gz", [(i, (i + shift) % slab_count) for i in range(slab_count)])
        )
    gathered = jnp.stack(gathered)
    slabs = []
    for index in range(slab_count):
        chosen = lax.dynamic_index_in_dim(
            gathered, (slab - index) % slab_count, axis=0, keepdims=False
        )
        slabs.append(chosen)
    zero_pair = jnp.zeros((2,) + partial_x.shape[1:], jnp.float32)
    below_all = [zero_pair] + [slabs[index][8:10] for index in range(slab_count - 1)]
    above_all = [slabs[index][10:12] for index in range(1, slab_count)] + [zero_pair]
    for index in range(slab_count):
        chosen = slabs[index]
        low_first, low_last, high_first, high_last = chosen[4], chosen[5], chosen[6], chosen[7]
        rows_first = (
            chosen[0:2] + below_all[index] * low_first[None] + above_all[index] * high_first[None]
        )
        rows_last = (
            chosen[2:4] + below_all[index] * low_last[None] + above_all[index] * high_last[None]
        )
        slabs[index] = (rows_first, rows_last, low_first, low_last, high_first, high_last)

    incoming_all = []
    factor_all = []
    offset_all = []
    coupling_all = []
    incoming = jnp.zeros((2,) + partial_x.shape[1:], jnp.float32)
    factor = jnp.zeros_like(low_weight[0])
    for index in range(slab_count):
        if index > 0:
            incoming, factor = outgoing, factor_out
        offset, coupling, outgoing, factor_out = advance(slabs[index], incoming, factor)
        incoming_all.append(incoming)
        factor_all.append(factor)
        offset_all.append(offset)
        coupling_all.append(coupling)
    following_all = [None] * slab_count
    leading_all = [None] * slab_count
    following = jnp.zeros((2,) + partial_x.shape[1:], jnp.float32)
    for index in reversed(range(slab_count)):
        if index < slab_count - 1:
            following = leading_all[index + 1]
        following_all[index] = following
        leading_all[index] = offset_all[index] + coupling_all[index][None] * following

    def pick(values):
        return lax.dynamic_index_in_dim(jnp.stack(values), slab, axis=0, keepdims=False)

    incoming = pick(incoming_all)
    factor = pick(factor_all)
    following = pick(following_all)
    leading = pick(leading_all)
    below = pick(below_all)
    above = pick(above_all)

    previous_last = incoming + factor[None] * leading + below
    following = following + above
    coef = jnp.concatenate([previous_last, following], axis=0)
    electric_x_new, electric_y_new, magnetic_x_new, magnetic_y_new = finish(
        electric, magnetic, partial_x, partial_y, low_weight, high_weight, slope_zx, slope_zy, coef
    )
    before_hy = from_prev(magnetic_y_new[:, -1:, :], "gx")
    before_hx = from_prev(magnetic_x_new[:, :, -1:], "gy")
    change_hy = magnetic_y_new - jnp.concatenate([before_hy, magnetic_y_new[:, :-1]], axis=1)
    change_hx = magnetic_x_new - jnp.concatenate([before_hx, magnetic_x_new[:, :, :-1]], axis=2)
    electric_z_new = keep_rate * electric_z + curl_rate * (change_hy - change_hx)
    return (
        jnp.stack([electric_x_new, electric_y_new, electric_z_new]),
        jnp.stack([magnetic_x_new, magnetic_y_new, magnetic_z_new]),
    )


def solution(mesh):
    return jax.shard_map(
        body,
        mesh=mesh,
        in_specs=(
            P(None, "gz", "gx", "gy"),
            P(None, "gz", "gx", "gy"),
            P("gz", "gx", "gy"),
            P("gz"),
            P(),
            P(),
        ),
        out_specs=(P(None, "gz", "gx", "gy"), P(None, "gz", "gx", "gy")),
        check_vma=False,
    )
```

```python
import jax
import jax.numpy as jnp
from jax import lax
from jax.sharding import PartitionSpec as P
from jax.experimental import pallas as pl
from jax.experimental.pallas import tpu as pltpu

time_step = 0.5
z_courant = 128.0


def from_prev(block, axis):
    count = lax.axis_size(axis)
    return lax.ppermute(block, axis, [(i, i + 1) for i in range(count - 1)])


def from_next(block, axis):
    count = lax.axis_size(axis)
    return lax.ppermute(block, axis, [(i + 1, i) for i in range(count - 1)])


def from_diagonal(block, axes, step_a, step_b):
    size_a = lax.axis_size(axes[0])
    size_b = lax.axis_size(axes[1])
    pairs = []
    for a in range(size_a):
        for b in range(size_b):
            src_a, src_b = a - step_a, b - step_b
            if 0 <= src_a < size_a and 0 <= src_b < size_b:
                pairs.append((src_a * size_b + src_b, a * size_b + b))
    return lax.ppermute(block, axes, pairs)


def lookup(table_values, layer_map, material):
    kind_count, entry_count = table_values.shape
    layer_hot = layer_map[:, None] == lax.broadcasted_iota(jnp.int32, (1, kind_count), 1)
    table_rows = jnp.sum(jnp.where(layer_hot[:, :, None], table_values[None], 0.0), axis=1)
    result = jnp.zeros(material.shape, jnp.float32)
    for entry_index in range(entry_count):
        result = result + jnp.where(
            material == entry_index, table_rows[:, entry_index][:, None, None], 0.0
        )
    return result


def rates(epsilon_cell, sigma_cell):
    half_loss = 0.25 * sigma_cell / epsilon_cell
    drive_rate = 1.0 / (1.0 + half_loss)
    keep_rate = (1.0 - half_loss) * drive_rate
    curl_rate = 0.5 * drive_rate / epsilon_cell
    z_rate = z_courant * drive_rate / epsilon_cell
    stiffness = 4096.0 * drive_rate / epsilon_cell
    return (keep_rate, curl_rate, z_rate, stiffness)


def thomas_kernel(
    stiff_ref, diag_ref, sx_ref, sy_ref, px_ref, py_ref, lw_ref, hw_ref, edge_ref, ur_ref
):
    depth = stiff_ref.shape[0]
    stiff = stiff_ref[0]
    inv = 1.0 / diag_ref[0]
    ur_ref[0] = -stiff * inv
    px_ref[0] = sx_ref[0] * inv
    py_ref[0] = sy_ref[0] * inv
    lw_ref[0] = inv

    def forward(z, carry):
        upper, value_x, value_y, value_low, unused = carry
        stiff = stiff_ref[z]
        inv = 1.0 / (diag_ref[z] + stiff * upper)
        upper = -stiff * inv
        value_x = (sx_ref[z] + stiff * value_x) * inv
        value_y = (sy_ref[z] + stiff * value_y) * inv
        value_low = (stiff * value_low) * inv
        ur_ref[z] = upper
        px_ref[z] = value_x
        py_ref[z] = value_y
        lw_ref[z] = value_low
        return upper, value_x, value_y, value_low, inv

    first = (ur_ref[0], px_ref[0], py_ref[0], lw_ref[0], inv)
    last_x, last_y, last_low, last_high = lax.fori_loop(1, depth, forward, first, unroll=8)[1:]
    low_scale = stiff_ref[0]
    high_scale = stiff_ref[depth - 1]
    lw_ref[depth - 1] = low_scale * last_low
    hw_ref[depth - 1] = high_scale * last_high

    def backward(step, carry):
        z = depth - 2 - step
        next_x, next_y, next_low, next_high = carry
        upper = ur_ref[z]
        next_x = px_ref[z] - upper * next_x
        next_y = py_ref[z] - upper * next_y
        next_low = lw_ref[z] - upper * next_low
        next_high = -upper * next_high
        px_ref[z] = next_x
        py_ref[z] = next_y
        lw_ref[z] = low_scale * next_low
        hw_ref[z] = high_scale * next_high
        return next_x, next_y, next_low, next_high

    lax.fori_loop(0, depth - 1, backward, (last_x, last_y, last_low, last_high), unroll=8)
    edge_ref[0] = px_ref[0]
    edge_ref[1] = py_ref[0]
    edge_ref[2] = px_ref[depth - 1]
    edge_ref[3] = py_ref[depth - 1]
    edge_ref[4] = lw_ref[0]
    edge_ref[5] = lw_ref[depth - 1]
    edge_ref[6] = hw_ref[0]
    edge_ref[7] = hw_ref[depth - 1]


def solve_slab(stiffness, diagonal, source_x, source_y):
    shape = jax.ShapeDtypeStruct(stiffness.shape, jnp.float32)
    edges = jax.ShapeDtypeStruct((8,) + stiffness.shape[1:], jnp.float32)
    return pl.pallas_call(
        thomas_kernel,
        out_shape=(shape, shape, shape, shape, edges),
        scratch_shapes=[pltpu.VMEM(stiffness.shape, jnp.float32)],
    )(stiffness, diagonal, source_x, source_y)


def source_kernel(
    flag_ref, e_ref, h_ref, rate_ref, xh_ref, xl_ref, yh_ref, yl_ref,
    cex_ref, cey_ref, hzn_ref, szx_ref, szy_ref, px_ref, py_ref, lw_ref, hw_ref, edge_ref,
    sx_ref, sy_ref, diag_ref, ur_ref,
):
    depth, rows, lanes = sx_ref.shape
    bottom = flag_ref[0] == 1
    first_x = flag_ref[1] == 1
    first_y = flag_ref[2] == 1
    sub = lax.broadcasted_iota(jnp.int32, (rows, lanes), 0)
    lane = lax.broadcasted_iota(jnp.int32, (rows, lanes), 1)

    def full(value):
        return jnp.broadcast_to(value, (rows, lanes))

    def next_x(tile, edge):
        return jnp.where(sub == rows - 1, full(edge), pltpu.roll(tile, rows - 1, 0))

    def prev_x(tile, edge):
        return jnp.where(sub == 0, full(edge), pltpu.roll(tile, 1, 0))

    def next_y(tile, edge):
        return jnp.where(lane == lanes - 1, full(edge), pltpu.roll(tile, lanes - 1, 1))

    def prev_y(tile, edge):
        return jnp.where(lane == 0, full(edge), pltpu.roll(tile, 1, 1))

    def row(z, below, above, first_row):
        ex, ey, ez = e_ref[0, z], e_ref[1, z], e_ref[2, z]
        hx, hy, hz = h_ref[0, z], h_ref[1, z], h_ref[2, z]
        keep, curl, zrate, stiff = rate_ref[0, z], rate_ref[1, z], rate_ref[2, z], rate_ref[3, z]
        ey_xh, ez_xh = full(xh_ref[0, z]), full(xh_ref[1, z])
        ex_xl, ey_xl, hz_xl = full(xl_ref[0, z]), full(xl_ref[1, z]), full(xl_ref[2, z])
        ex_yh, ez_yh = full(yh_ref[0, z]), full(yh_ref[1, z])
        ex_yl, ey_yl, hz_yl = full(yl_ref[0, z]), full(yl_ref[1, z]), full(yl_ref[2, z])
        corner_ex = full(cex_ref[z])
        corner_ey = full(cey_ref[z])
        hz_new = hz - time_step * ((next_x(ey, ey_xh) - ey) - (next_y(ex, ex_yh) - ex))
        ex_py = prev_y(ex, ex_yl)
        ey_py = prev_y(ey, ey_yl)
        hz_py = prev_y(hz, hz_yl)
        face_py = (next_x(ey_py, prev_y(ey_xh, corner_ey)) - ey_py) - (ex - ex_py)
        hz_new_py = hz_py - time_step * face_py
        hz_new_py = jnp.where(jnp.logical_and(first_y, lane == 0), 0.0, hz_new_py)
        ex_px = prev_x(ex, ex_xl)
        ey_px = prev_x(ey, ey_xl)
        hz_px = prev_x(hz, hz_xl)
        face_px = (ey - ey_px) - (next_y(ex_px, prev_x(ex_yh, corner_ex)) - ex_px)
        hz_new_px = hz_px - time_step * face_px
        hz_new_px = jnp.where(jnp.logical_and(first_x, sub == 0), 0.0, hz_new_px)
        slope_zx = next_x(ez, ez_xh) - ez
        slope_zy = next_y(ez, ez_yh) - ez
        ex_b, ey_b, hx_b, hy_b, slope_zx_b, slope_zy_b = below
        ex_a, ey_a = above
        rise_x = ex - ex_b
        rise_y = ey - ey_b
        diag_ref[z] = 1.0 + 2.0 * stiff
        if first_row:
            rise_x = jnp.where(bottom, 0.0, rise_x)
            rise_y = jnp.where(bottom, 0.0, rise_y)
            diag_ref[z] = jnp.where(bottom, 1.0 + stiff, 1.0 + 2.0 * stiff)
        quarter_z = 0.25 * zrate
        sx_ref[z] = (
            keep * ex
            + stiff * ((ex_a - ex) - rise_x)
            + curl * (hz_new - hz_new_py)
            - zrate * (hy - hy_b)
            - quarter_z * (slope_zx - slope_zx_b)
        )
        sy_ref[z] = (
            keep * ey
            + stiff * ((ey_a - ey) - rise_y)
            + zrate * (hx - hx_b)
            - quarter_z * (slope_zy - slope_zy_b)
            - curl * (hz_new - hz_new_px)
        )
        hzn_ref[z] = hz_new
        szx_ref[z] = slope_zx
        szy_ref[z] = slope_zy
        return (ex, ey, hx, hy, slope_zx, slope_zy)

    zero = jnp.zeros((rows, lanes), jnp.float32)
    below = row(0, (zero,) * 6, (e_ref[0, 1], e_ref[1, 1]), True)

    def middle(z, below):
        return row(z, below, (e_ref[0, z + 1], e_ref[1, z + 1]), False)

    below = lax.fori_loop(1, depth - 1, middle, below, unroll=8)
    row(depth - 1, below, (zero, zero), False)
    thomas_kernel(
        rate_ref.at[3], diag_ref, sx_ref, sy_ref, px_ref, py_ref, lw_ref, hw_ref, edge_ref, ur_ref
    )
    edge_ref[8] = e_ref[0, depth - 1] + (h_ref[1, depth - 1] + 0.25 * szx_ref[depth - 1]) / 32.0
    edge_ref[9] = e_ref[1, depth - 1] + (0.25 * szy_ref[depth - 1] - h_ref[0, depth - 1]) / 32.0
    edge_ref[10] = e_ref[0, 0]
    edge_ref[11] = e_ref[1, 0]


def make_sources(flags, electric, magnetic, rate_stack, x_high, x_low, y_high, y_low,
                 corner_ex, corner_ey):
    shape = jax.ShapeDtypeStruct(electric.shape[1:], jnp.float32)
    edges = jax.ShapeDtypeStruct((12,) + electric.shape[2:], jnp.float32)
    vmem = pl.BlockSpec(memory_space=pltpu.VMEM)
    smem = pl.BlockSpec(memory_space=pltpu.SMEM)
    return pl.pallas_call(
        source_kernel,
        out_shape=(shape,) * 7 + (edges,),
        in_specs=[smem] + [vmem] * 9,
        out_specs=(vmem,) * 8,
        scratch_shapes=[pltpu.VMEM(electric.shape[1:], jnp.float32)] * 4,
    )(flags, electric, magnetic, rate_stack, x_high, x_low, y_high, y_low,
      corner_ex, corner_ey)


def advance(pieces, incoming, factor):
    rows_first, rows_last, low_first, low_last, high_first, high_last = pieces
    denominator = 1.0 - low_first * factor
    offset = (rows_first + low_first[None] * incoming) / denominator[None]
    coupling = high_first / denominator
    outgoing = rows_last + low_last[None] * (incoming + factor[None] * offset)
    factor_out = low_last * factor * coupling + high_last
    return (offset, coupling, outgoing, factor_out)


def body(electric, magnetic, material, layer_map, permittivity, conductivity):
    epsilon_cell = lookup(permittivity, layer_map, material)
    sigma_cell = lookup(conductivity, layer_map, material)
    keep_rate, curl_rate, z_rate, stiffness = rates(epsilon_cell, sigma_cell)
    depth_rows, span_x, span_y = material.shape
    slab = lax.axis_index("gz")
    bottom = slab == 0
    first_x = lax.axis_index("gx") == 0
    first_y = lax.axis_index("gy") == 0
    electric_x, electric_y, electric_z = (electric[0], electric[1], electric[2])
    magnetic_x, magnetic_y, magnetic_z = (magnetic[0], magnetic[1], magnetic[2])

    x_high = from_next(jnp.stack([electric_y[:, :1], electric_z[:, :1]]), "gx")
    x_low = from_prev(
        jnp.stack([electric_x[:, -1:], electric_y[:, -1:], magnetic_z[:, -1:]]), "gx"
    )
    y_high = from_next(jnp.stack([electric_x[:, :, :1], electric_z[:, :, :1]]), "gy")
    y_low = from_prev(
        jnp.stack([electric_x[:, :, -1:], electric_y[:, :, -1:], magnetic_z[:, :, -1:]]), "gy"
    )
    corner_ex = from_diagonal(electric_x[:, -1:, :1], ("gx", "gy"), 1, -1)
    corner_ey = from_diagonal(electric_y[:, :1, -1:], ("gx", "gy"), -1, 1)

    flags = jnp.stack([bottom, first_x, first_y]).astype(jnp.int32)
    rate_stack = jnp.stack([keep_rate, curl_rate, z_rate, stiffness])
    (magnetic_z_new, slope_zx, slope_zy, partial_x, partial_y, low_weight, high_weight,
     own) = make_sources(
        flags, electric, magnetic, rate_stack, x_high, x_low, y_high, y_low,
        corner_ex, corner_ey,
    )
    slab_count = lax.axis_size("gz")
    gathered = [own]
    for shift in range(1, slab_count):
        gathered.append(
            lax.ppermute(own, "gz", [(i, (i + shift) % slab_count) for i in range(slab_count)])
        )
    gathered = jnp.stack(gathered)
    slabs = []
    for index in range(slab_count):
        chosen = lax.dynamic_index_in_dim(
            gathered, (slab - index) % slab_count, axis=0, keepdims=False
        )
        slabs.append(chosen)
    zero_pair = jnp.zeros((2,) + partial_x.shape[1:], jnp.float32)
    below_all = [zero_pair] + [slabs[index][8:10] for index in range(slab_count - 1)]
    above_all = [slabs[index][10:12] for index in range(1, slab_count)] + [zero_pair]
    for index in range(slab_count):
        chosen = slabs[index]
        low_first, low_last, high_first, high_last = chosen[4], chosen[5], chosen[6], chosen[7]
        rows_first = (
            chosen[0:2] + below_all[index] * low_first[None] + above_all[index] * high_first[None]
        )
        rows_last = (
            chosen[2:4] + below_all[index] * low_last[None] + above_all[index] * high_last[None]
        )
        slabs[index] = (rows_first, rows_last, low_first, low_last, high_first, high_last)

    incoming_all = []
    factor_all = []
    offset_all = []
    coupling_all = []
    incoming = jnp.zeros((2,) + partial_x.shape[1:], jnp.float32)
    factor = jnp.zeros_like(low_weight[0])
    for index in range(slab_count):
        if index > 0:
            incoming, factor = outgoing, factor_out
        offset, coupling, outgoing, factor_out = advance(slabs[index], incoming, factor)
        incoming_all.append(incoming)
        factor_all.append(factor)
        offset_all.append(offset)
        coupling_all.append(coupling)
    following_all = [None] * slab_count
    leading_all = [None] * slab_count
    following = jnp.zeros((2,) + partial_x.shape[1:], jnp.float32)
    for index in reversed(range(slab_count)):
        if index < slab_count - 1:
            following = leading_all[index + 1]
        following_all[index] = following
        leading_all[index] = offset_all[index] + coupling_all[index][None] * following

    def pick(values):
        return lax.dynamic_index_in_dim(jnp.stack(values), slab, axis=0, keepdims=False)

    incoming = pick(incoming_all)
    factor = pick(factor_all)
    following = pick(following_all)
    leading = pick(leading_all)
    below = pick(below_all)
    above = pick(above_all)

    previous_last = incoming + factor[None] * leading + below
    following = following + above
    electric_x_new = (
        partial_x + previous_last[0][None] * low_weight + following[0][None] * high_weight
    )
    electric_y_new = (
        partial_y + previous_last[1][None] * low_weight + following[1][None] * high_weight
    )
    sum_x = electric_x + electric_x_new
    sum_y = electric_y + electric_y_new
    top_x = following[0]
    top_y = following[1]
    rise_x = jnp.concatenate([sum_x[1:], top_x[None]], axis=0) - sum_x
    rise_y = jnp.concatenate([sum_y[1:], top_y[None]], axis=0) - sum_y
    magnetic_y_new = magnetic_y - 0.5 * z_courant * rise_x + time_step * slope_zx
    magnetic_x_new = magnetic_x - time_step * slope_zy + 0.5 * z_courant * rise_y
    before_hy = from_prev(magnetic_y_new[:, -1:, :], "gx")
    before_hx = from_prev(magnetic_x_new[:, :, -1:], "gy")
    change_hy = magnetic_y_new - jnp.concatenate([before_hy, magnetic_y_new[:, :-1]], axis=1)
    change_hx = magnetic_x_new - jnp.concatenate([before_hx, magnetic_x_new[:, :, :-1]], axis=2)
    electric_z_new = keep_rate * electric_z + curl_rate * (change_hy - change_hx)
    return (
        jnp.stack([electric_x_new, electric_y_new, electric_z_new]),
        jnp.stack([magnetic_x_new, magnetic_y_new, magnetic_z_new]),
    )


def solution(mesh):
    return jax.shard_map(
        body,
        mesh=mesh,
        in_specs=(
            P(None, "gz", "gx", "gy"),
            P(None, "gz", "gx", "gy"),
            P("gz", "gx", "gy"),
            P("gz"),
            P(),
            P(),
        ),
        out_specs=(P(None, "gz", "gx", "gy"), P(None, "gz", "gx", "gy")),
        check_vma=False,
    )
```

```python
import jax
import jax.numpy as jnp
from jax import lax
from jax.sharding import PartitionSpec as P
from jax.experimental import pallas as pl
from jax.experimental.pallas import tpu as pltpu

time_step = 0.5
z_courant = 128.0


def from_prev(block, axis):
    count = lax.axis_size(axis)
    return lax.ppermute(block, axis, [(i, i + 1) for i in range(count - 1)])


def from_next(block, axis):
    count = lax.axis_size(axis)
    return lax.ppermute(block, axis, [(i + 1, i) for i in range(count - 1)])


def from_diagonal(block, axes, step_a, step_b):
    size_a = lax.axis_size(axes[0])
    size_b = lax.axis_size(axes[1])
    pairs = []
    for a in range(size_a):
        for b in range(size_b):
            src_a, src_b = a - step_a, b - step_b
            if 0 <= src_a < size_a and 0 <= src_b < size_b:
                pairs.append((src_a * size_b + src_b, a * size_b + b))
    return lax.ppermute(block, axes, pairs)


def lookup(table_values, layer_map, material):
    kind_count, entry_count = table_values.shape
    layer_hot = layer_map[:, None] == lax.broadcasted_iota(jnp.int32, (1, kind_count), 1)
    table_rows = jnp.sum(jnp.where(layer_hot[:, :, None], table_values[None], 0.0), axis=1)
    result = jnp.zeros(material.shape, jnp.float32)
    for entry_index in range(entry_count):
        result = result + jnp.where(
            material == entry_index, table_rows[:, entry_index][:, None, None], 0.0
        )
    return result


def rates(epsilon_cell, sigma_cell):
    half_loss = 0.25 * sigma_cell / epsilon_cell
    drive_rate = 1.0 / (1.0 + half_loss)
    keep_rate = (1.0 - half_loss) * drive_rate
    curl_rate = 0.5 * drive_rate / epsilon_cell
    z_rate = z_courant * drive_rate / epsilon_cell
    stiffness = 4096.0 * drive_rate / epsilon_cell
    return (keep_rate, curl_rate, z_rate, stiffness)


def thomas_kernel(
    stiff_ref, diag_ref, sx_ref, sy_ref, px_ref, py_ref, lw_ref, hw_ref, edge_ref, ur_ref
):
    depth = stiff_ref.shape[0]
    stiff = stiff_ref[0]
    inv = 1.0 / diag_ref[0]
    ur_ref[0] = -stiff * inv
    px_ref[0] = sx_ref[0] * inv
    py_ref[0] = sy_ref[0] * inv
    lw_ref[0] = inv

    def forward(z, carry):
        upper, value_x, value_y, value_low, unused = carry
        stiff = stiff_ref[z]
        inv = 1.0 / (diag_ref[z] + stiff * upper)
        upper = -stiff * inv
        value_x = (sx_ref[z] + stiff * value_x) * inv
        value_y = (sy_ref[z] + stiff * value_y) * inv
        value_low = (stiff * value_low) * inv
        ur_ref[z] = upper
        px_ref[z] = value_x
        py_ref[z] = value_y
        lw_ref[z] = value_low
        return upper, value_x, value_y, value_low, inv

    first = (ur_ref[0], px_ref[0], py_ref[0], lw_ref[0], inv)
    last_x, last_y, last_low, last_high = lax.fori_loop(1, depth, forward, first, unroll=16)[1:]
    low_scale = stiff_ref[0]
    high_scale = stiff_ref[depth - 1]
    lw_ref[depth - 1] = low_scale * last_low
    hw_ref[depth - 1] = high_scale * last_high

    def backward(step, carry):
        z = depth - 2 - step
        next_x, next_y, next_low, next_high = carry
        upper = ur_ref[z]
        next_x = px_ref[z] - upper * next_x
        next_y = py_ref[z] - upper * next_y
        next_low = lw_ref[z] - upper * next_low
        next_high = -upper * next_high
        px_ref[z] = next_x
        py_ref[z] = next_y
        lw_ref[z] = low_scale * next_low
        hw_ref[z] = high_scale * next_high
        return next_x, next_y, next_low, next_high

    lax.fori_loop(0, depth - 1, backward, (last_x, last_y, last_low, last_high), unroll=16)
    edge_ref[0] = px_ref[0]
    edge_ref[1] = py_ref[0]
    edge_ref[2] = px_ref[depth - 1]
    edge_ref[3] = py_ref[depth - 1]
    edge_ref[4] = lw_ref[0]
    edge_ref[5] = lw_ref[depth - 1]
    edge_ref[6] = hw_ref[0]
    edge_ref[7] = hw_ref[depth - 1]


def solve_slab(stiffness, diagonal, source_x, source_y):
    shape = jax.ShapeDtypeStruct(stiffness.shape, jnp.float32)
    edges = jax.ShapeDtypeStruct((8,) + stiffness.shape[1:], jnp.float32)
    return pl.pallas_call(
        thomas_kernel,
        out_shape=(shape, shape, shape, shape, edges),
        scratch_shapes=[pltpu.VMEM(stiffness.shape, jnp.float32)],
    )(stiffness, diagonal, source_x, source_y)


def source_kernel(
    flag_ref, e_ref, h_ref, rate_ref, xh_ref, xl_ref, yh_ref, yl_ref,
    cex_ref, cey_ref, hzn_ref, szx_ref, szy_ref, px_ref, py_ref, lw_ref, hw_ref, edge_ref,
    sx_ref, sy_ref, diag_ref, ur_ref,
):
    depth, rows, lanes = sx_ref.shape
    bottom = flag_ref[0] == 1
    first_x = flag_ref[1] == 1
    first_y = flag_ref[2] == 1
    sub = lax.broadcasted_iota(jnp.int32, (rows, lanes), 0)
    lane = lax.broadcasted_iota(jnp.int32, (rows, lanes), 1)

    def full(value):
        return jnp.broadcast_to(value, (rows, lanes))

    def next_x(tile, edge):
        return jnp.where(sub == rows - 1, full(edge), pltpu.roll(tile, rows - 1, 0))

    def prev_x(tile, edge):
        return jnp.where(sub == 0, full(edge), pltpu.roll(tile, 1, 0))

    def next_y(tile, edge):
        return jnp.where(lane == lanes - 1, full(edge), pltpu.roll(tile, lanes - 1, 1))

    def prev_y(tile, edge):
        return jnp.where(lane == 0, full(edge), pltpu.roll(tile, 1, 1))

    def row(z, below, above, first_row):
        ex, ey, ez = e_ref[0, z], e_ref[1, z], e_ref[2, z]
        hx, hy, hz = h_ref[0, z], h_ref[1, z], h_ref[2, z]
        keep, curl, zrate, stiff = rate_ref[0, z], rate_ref[1, z], rate_ref[2, z], rate_ref[3, z]
        ey_xh, ez_xh = full(xh_ref[0, z]), full(xh_ref[1, z])
        ex_xl, ey_xl, hz_xl = full(xl_ref[0, z]), full(xl_ref[1, z]), full(xl_ref[2, z])
        ex_yh, ez_yh = full(yh_ref[0, z]), full(yh_ref[1, z])
        ex_yl, ey_yl, hz_yl = full(yl_ref[0, z]), full(yl_ref[1, z]), full(yl_ref[2, z])
        corner_ex = full(cex_ref[z])
        corner_ey = full(cey_ref[z])
        hz_new = hz - time_step * ((next_x(ey, ey_xh) - ey) - (next_y(ex, ex_yh) - ex))
        ex_py = prev_y(ex, ex_yl)
        ey_py = prev_y(ey, ey_yl)
        hz_py = prev_y(hz, hz_yl)
        face_py = (next_x(ey_py, prev_y(ey_xh, corner_ey)) - ey_py) - (ex - ex_py)
        hz_new_py = hz_py - time_step * face_py
        hz_new_py = jnp.where(jnp.logical_and(first_y, lane == 0), 0.0, hz_new_py)
        ex_px = prev_x(ex, ex_xl)
        ey_px = prev_x(ey, ey_xl)
        hz_px = prev_x(hz, hz_xl)
        face_px = (ey - ey_px) - (next_y(ex_px, prev_x(ex_yh, corner_ex)) - ex_px)
        hz_new_px = hz_px - time_step * face_px
        hz_new_px = jnp.where(jnp.logical_and(first_x, sub == 0), 0.0, hz_new_px)
        slope_zx = next_x(ez, ez_xh) - ez
        slope_zy = next_y(ez, ez_yh) - ez
        ex_b, ey_b, hx_b, hy_b, slope_zx_b, slope_zy_b = below
        ex_a, ey_a = above
        rise_x = ex - ex_b
        rise_y = ey - ey_b
        diag_ref[z] = 1.0 + 2.0 * stiff
        if first_row:
            rise_x = jnp.where(bottom, 0.0, rise_x)
            rise_y = jnp.where(bottom, 0.0, rise_y)
            diag_ref[z] = jnp.where(bottom, 1.0 + stiff, 1.0 + 2.0 * stiff)
        quarter_z = 0.25 * zrate
        sx_ref[z] = (
            keep * ex
            + stiff * ((ex_a - ex) - rise_x)
            + curl * (hz_new - hz_new_py)
            - zrate * (hy - hy_b)
            - quarter_z * (slope_zx - slope_zx_b)
        )
        sy_ref[z] = (
            keep * ey
            + stiff * ((ey_a - ey) - rise_y)
            + zrate * (hx - hx_b)
            - quarter_z * (slope_zy - slope_zy_b)
            - curl * (hz_new - hz_new_px)
        )
        hzn_ref[z] = hz_new
        szx_ref[z] = slope_zx
        szy_ref[z] = slope_zy
        return (ex, ey, hx, hy, slope_zx, slope_zy)

    zero = jnp.zeros((rows, lanes), jnp.float32)
    below = row(0, (zero,) * 6, (e_ref[0, 1], e_ref[1, 1]), True)

    def middle(z, below):
        return row(z, below, (e_ref[0, z + 1], e_ref[1, z + 1]), False)

    below = lax.fori_loop(1, depth - 1, middle, below, unroll=True)
    row(depth - 1, below, (zero, zero), False)
    thomas_kernel(
        rate_ref.at[3], diag_ref, sx_ref, sy_ref, px_ref, py_ref, lw_ref, hw_ref, edge_ref, ur_ref
    )
    edge_ref[8] = e_ref[0, depth - 1] + (h_ref[1, depth - 1] + 0.25 * szx_ref[depth - 1]) / 32.0
    edge_ref[9] = e_ref[1, depth - 1] + (0.25 * szy_ref[depth - 1] - h_ref[0, depth - 1]) / 32.0
    edge_ref[10] = e_ref[0, 0]
    edge_ref[11] = e_ref[1, 0]


def make_sources(flags, electric, magnetic, rate_stack, x_high, x_low, y_high, y_low,
                 corner_ex, corner_ey):
    shape = jax.ShapeDtypeStruct(electric.shape[1:], jnp.float32)
    edges = jax.ShapeDtypeStruct((12,) + electric.shape[2:], jnp.float32)
    vmem = pl.BlockSpec(memory_space=pltpu.VMEM)
    smem = pl.BlockSpec(memory_space=pltpu.SMEM)
    return pl.pallas_call(
        source_kernel,
        out_shape=(shape,) * 7 + (edges,),
        in_specs=[smem] + [vmem] * 9,
        out_specs=(vmem,) * 8,
        scratch_shapes=[pltpu.VMEM(electric.shape[1:], jnp.float32)] * 4,
    )(flags, electric, magnetic, rate_stack, x_high, x_low, y_high, y_low,
      corner_ex, corner_ey)


def advance(pieces, incoming, factor):
    rows_first, rows_last, low_first, low_last, high_first, high_last = pieces
    denominator = 1.0 - low_first * factor
    offset = (rows_first + low_first[None] * incoming) / denominator[None]
    coupling = high_first / denominator
    outgoing = rows_last + low_last[None] * (incoming + factor[None] * offset)
    factor_out = low_last * factor * coupling + high_last
    return (offset, coupling, outgoing, factor_out)


def body(electric, magnetic, material, layer_map, permittivity, conductivity):
    epsilon_cell = lookup(permittivity, layer_map, material)
    sigma_cell = lookup(conductivity, layer_map, material)
    keep_rate, curl_rate, z_rate, stiffness = rates(epsilon_cell, sigma_cell)
    depth_rows, span_x, span_y = material.shape
    slab = lax.axis_index("gz")
    bottom = slab == 0
    first_x = lax.axis_index("gx") == 0
    first_y = lax.axis_index("gy") == 0
    electric_x, electric_y, electric_z = (electric[0], electric[1], electric[2])
    magnetic_x, magnetic_y, magnetic_z = (magnetic[0], magnetic[1], magnetic[2])

    x_high = from_next(jnp.stack([electric_y[:, :1], electric_z[:, :1]]), "gx")
    x_low = from_prev(
        jnp.stack([electric_x[:, -1:], electric_y[:, -1:], magnetic_z[:, -1:]]), "gx"
    )
    y_high = from_next(jnp.stack([electric_x[:, :, :1], electric_z[:, :, :1]]), "gy")
    y_low = from_prev(
        jnp.stack([electric_x[:, :, -1:], electric_y[:, :, -1:], magnetic_z[:, :, -1:]]), "gy"
    )
    corner_ex = from_diagonal(electric_x[:, -1:, :1], ("gx", "gy"), 1, -1)
    corner_ey = from_diagonal(electric_y[:, :1, -1:], ("gx", "gy"), -1, 1)

    flags = jnp.stack([bottom, first_x, first_y]).astype(jnp.int32)
    rate_stack = jnp.stack([keep_rate, curl_rate, z_rate, stiffness])
    (magnetic_z_new, slope_zx, slope_zy, partial_x, partial_y, low_weight, high_weight,
     own) = make_sources(
        flags, electric, magnetic, rate_stack, x_high, x_low, y_high, y_low,
        corner_ex, corner_ey,
    )
    slab_count = lax.axis_size("gz")
    gathered = [own]
    for shift in range(1, slab_count):
        gathered.append(
            lax.ppermute(own, "gz", [(i, (i + shift) % slab_count) for i in range(slab_count)])
        )
    gathered = jnp.stack(gathered)
    slabs = []
    for index in range(slab_count):
        chosen = lax.dynamic_index_in_dim(
            gathered, (slab - index) % slab_count, axis=0, keepdims=False
        )
        slabs.append(chosen)
    zero_pair = jnp.zeros((2,) + partial_x.shape[1:], jnp.float32)
    below_all = [zero_pair] + [slabs[index][8:10] for index in range(slab_count - 1)]
    above_all = [slabs[index][10:12] for index in range(1, slab_count)] + [zero_pair]
    for index in range(slab_count):
        chosen = slabs[index]
        low_first, low_last, high_first, high_last = chosen[4], chosen[5], chosen[6], chosen[7]
        rows_first = (
            chosen[0:2] + below_all[index] * low_first[None] + above_all[index] * high_first[None]
        )
        rows_last = (
            chosen[2:4] + below_all[index] * low_last[None] + above_all[index] * high_last[None]
        )
        slabs[index] = (rows_first, rows_last, low_first, low_last, high_first, high_last)

    incoming_all = []
    factor_all = []
    offset_all = []
    coupling_all = []
    incoming = jnp.zeros((2,) + partial_x.shape[1:], jnp.float32)
    factor = jnp.zeros_like(low_weight[0])
    for index in range(slab_count):
        if index > 0:
            incoming, factor = outgoing, factor_out
        offset, coupling, outgoing, factor_out = advance(slabs[index], incoming, factor)
        incoming_all.append(incoming)
        factor_all.append(factor)
        offset_all.append(offset)
        coupling_all.append(coupling)
    following_all = [None] * slab_count
    leading_all = [None] * slab_count
    following = jnp.zeros((2,) + partial_x.shape[1:], jnp.float32)
    for index in reversed(range(slab_count)):
        if index < slab_count - 1:
            following = leading_all[index + 1]
        following_all[index] = following
        leading_all[index] = offset_all[index] + coupling_all[index][None] * following

    def pick(values):
        return lax.dynamic_index_in_dim(jnp.stack(values), slab, axis=0, keepdims=False)

    incoming = pick(incoming_all)
    factor = pick(factor_all)
    following = pick(following_all)
    leading = pick(leading_all)
    below = pick(below_all)
    above = pick(above_all)

    previous_last = incoming + factor[None] * leading + below
    following = following + above
    electric_x_new = (
        partial_x + previous_last[0][None] * low_weight + following[0][None] * high_weight
    )
    electric_y_new = (
        partial_y + previous_last[1][None] * low_weight + following[1][None] * high_weight
    )
    sum_x = electric_x + electric_x_new
    sum_y = electric_y + electric_y_new
    top_x = following[0]
    top_y = following[1]
    rise_x = jnp.concatenate([sum_x[1:], top_x[None]], axis=0) - sum_x
    rise_y = jnp.concatenate([sum_y[1:], top_y[None]], axis=0) - sum_y
    magnetic_y_new = magnetic_y - 0.5 * z_courant * rise_x + time_step * slope_zx
    magnetic_x_new = magnetic_x - time_step * slope_zy + 0.5 * z_courant * rise_y
    before_hy = from_prev(magnetic_y_new[:, -1:, :], "gx")
    before_hx = from_prev(magnetic_x_new[:, :, -1:], "gy")
    change_hy = magnetic_y_new - jnp.concatenate([before_hy, magnetic_y_new[:, :-1]], axis=1)
    change_hx = magnetic_x_new - jnp.concatenate([before_hx, magnetic_x_new[:, :, :-1]], axis=2)
    electric_z_new = keep_rate * electric_z + curl_rate * (change_hy - change_hx)
    return (
        jnp.stack([electric_x_new, electric_y_new, electric_z_new]),
        jnp.stack([magnetic_x_new, magnetic_y_new, magnetic_z_new]),
    )


def solution(mesh):
    return jax.shard_map(
        body,
        mesh=mesh,
        in_specs=(
            P(None, "gz", "gx", "gy"),
            P(None, "gz", "gx", "gy"),
            P("gz", "gx", "gy"),
            P("gz"),
            P(),
            P(),
        ),
        out_specs=(P(None, "gz", "gx", "gy"), P(None, "gz", "gx", "gy")),
        check_vma=False,
    )
```

```python
import jax
import jax.numpy as jnp
from jax import lax
from jax.sharding import PartitionSpec as P
from jax.experimental import pallas as pl
from jax.experimental.pallas import tpu as pltpu

time_step = 0.5
z_courant = 128.0


def from_prev(block, axis):
    count = lax.axis_size(axis)
    return lax.ppermute(block, axis, [(i, i + 1) for i in range(count - 1)])


def from_next(block, axis):
    count = lax.axis_size(axis)
    return lax.ppermute(block, axis, [(i + 1, i) for i in range(count - 1)])


def from_diagonal(block, axes, step_a, step_b):
    size_a = lax.axis_size(axes[0])
    size_b = lax.axis_size(axes[1])
    pairs = []
    for a in range(size_a):
        for b in range(size_b):
            src_a, src_b = a - step_a, b - step_b
            if 0 <= src_a < size_a and 0 <= src_b < size_b:
                pairs.append((src_a * size_b + src_b, a * size_b + b))
    return lax.ppermute(block, axes, pairs)


def lookup(table_values, layer_map, material):
    kind_count, entry_count = table_values.shape
    layer_hot = layer_map[:, None] == lax.broadcasted_iota(jnp.int32, (1, kind_count), 1)
    table_rows = jnp.sum(jnp.where(layer_hot[:, :, None], table_values[None], 0.0), axis=1)
    result = jnp.zeros(material.shape, jnp.float32)
    for entry_index in range(entry_count):
        result = result + jnp.where(
            material == entry_index, table_rows[:, entry_index][:, None, None], 0.0
        )
    return result


def rates(epsilon_cell, sigma_cell):
    half_loss = 0.25 * sigma_cell / epsilon_cell
    drive_rate = 1.0 / (1.0 + half_loss)
    keep_rate = (1.0 - half_loss) * drive_rate
    curl_rate = 0.5 * drive_rate / epsilon_cell
    z_rate = z_courant * drive_rate / epsilon_cell
    stiffness = 4096.0 * drive_rate / epsilon_cell
    return (keep_rate, curl_rate, z_rate, stiffness)


def thomas_kernel(
    stiff_ref, diag_ref, sx_ref, sy_ref, px_ref, py_ref, lw_ref, hw_ref, edge_ref, ur_ref
):
    depth = stiff_ref.shape[0]
    stiff = stiff_ref[0]
    inv = 1.0 / diag_ref[0]
    ur_ref[0] = -stiff * inv
    px_ref[0] = sx_ref[0] * inv
    py_ref[0] = sy_ref[0] * inv
    lw_ref[0] = inv

    def forward(z, carry):
        upper, value_x, value_y, value_low, unused = carry
        stiff = stiff_ref[z]
        inv = 1.0 / (diag_ref[z] + stiff * upper)
        upper = -stiff * inv
        value_x = (sx_ref[z] + stiff * value_x) * inv
        value_y = (sy_ref[z] + stiff * value_y) * inv
        value_low = (stiff * value_low) * inv
        ur_ref[z] = upper
        px_ref[z] = value_x
        py_ref[z] = value_y
        lw_ref[z] = value_low
        return upper, value_x, value_y, value_low, inv

    first = (ur_ref[0], px_ref[0], py_ref[0], lw_ref[0], inv)
    last_x, last_y, last_low, last_high = lax.fori_loop(1, depth, forward, first, unroll=True)[1:]
    low_scale = stiff_ref[0]
    high_scale = stiff_ref[depth - 1]
    lw_ref[depth - 1] = low_scale * last_low
    hw_ref[depth - 1] = high_scale * last_high

    def backward(step, carry):
        z = depth - 2 - step
        next_x, next_y, next_low, next_high = carry
        upper = ur_ref[z]
        next_x = px_ref[z] - upper * next_x
        next_y = py_ref[z] - upper * next_y
        next_low = lw_ref[z] - upper * next_low
        next_high = -upper * next_high
        px_ref[z] = next_x
        py_ref[z] = next_y
        lw_ref[z] = low_scale * next_low
        hw_ref[z] = high_scale * next_high
        return next_x, next_y, next_low, next_high

    lax.fori_loop(0, depth - 1, backward, (last_x, last_y, last_low, last_high), unroll=True)
    edge_ref[0] = px_ref[0]
    edge_ref[1] = py_ref[0]
    edge_ref[2] = px_ref[depth - 1]
    edge_ref[3] = py_ref[depth - 1]
    edge_ref[4] = lw_ref[0]
    edge_ref[5] = lw_ref[depth - 1]
    edge_ref[6] = hw_ref[0]
    edge_ref[7] = hw_ref[depth - 1]


def solve_slab(stiffness, diagonal, source_x, source_y):
    shape = jax.ShapeDtypeStruct(stiffness.shape, jnp.float32)
    edges = jax.ShapeDtypeStruct((8,) + stiffness.shape[1:], jnp.float32)
    return pl.pallas_call(
        thomas_kernel,
        out_shape=(shape, shape, shape, shape, edges),
        scratch_shapes=[pltpu.VMEM(stiffness.shape, jnp.float32)],
    )(stiffness, diagonal, source_x, source_y)


def source_kernel(
    flag_ref, e_ref, h_ref, rate_ref, xh_ref, xl_ref, yh_ref, yl_ref,
    cex_ref, cey_ref, hzn_ref, szx_ref, szy_ref, px_ref, py_ref, lw_ref, hw_ref, edge_ref,
    sx_ref, sy_ref, diag_ref, ur_ref,
):
    depth, rows, lanes = sx_ref.shape
    bottom = flag_ref[0] == 1
    first_x = flag_ref[1] == 1
    first_y = flag_ref[2] == 1
    sub = lax.broadcasted_iota(jnp.int32, (rows, lanes), 0)
    lane = lax.broadcasted_iota(jnp.int32, (rows, lanes), 1)

    def full(value):
        return jnp.broadcast_to(value, (rows, lanes))

    def next_x(tile, edge):
        return jnp.where(sub == rows - 1, full(edge), pltpu.roll(tile, rows - 1, 0))

    def prev_x(tile, edge):
        return jnp.where(sub == 0, full(edge), pltpu.roll(tile, 1, 0))

    def next_y(tile, edge):
        return jnp.where(lane == lanes - 1, full(edge), pltpu.roll(tile, lanes - 1, 1))

    def prev_y(tile, edge):
        return jnp.where(lane == 0, full(edge), pltpu.roll(tile, 1, 1))

    def row(z, below, above, first_row):
        ex, ey, ez = e_ref[0, z], e_ref[1, z], e_ref[2, z]
        hx, hy, hz = h_ref[0, z], h_ref[1, z], h_ref[2, z]
        keep, curl, zrate, stiff = rate_ref[0, z], rate_ref[1, z], rate_ref[2, z], rate_ref[3, z]
        ey_xh, ez_xh = full(xh_ref[0, z]), full(xh_ref[1, z])
        ex_xl, ey_xl, hz_xl = full(xl_ref[0, z]), full(xl_ref[1, z]), full(xl_ref[2, z])
        ex_yh, ez_yh = full(yh_ref[0, z]), full(yh_ref[1, z])
        ex_yl, ey_yl, hz_yl = full(yl_ref[0, z]), full(yl_ref[1, z]), full(yl_ref[2, z])
        corner_ex = full(cex_ref[z])
        corner_ey = full(cey_ref[z])
        hz_new = hz - time_step * ((next_x(ey, ey_xh) - ey) - (next_y(ex, ex_yh) - ex))
        ex_py = prev_y(ex, ex_yl)
        ey_py = prev_y(ey, ey_yl)
        hz_py = prev_y(hz, hz_yl)
        face_py = (next_x(ey_py, prev_y(ey_xh, corner_ey)) - ey_py) - (ex - ex_py)
        hz_new_py = hz_py - time_step * face_py
        hz_new_py = jnp.where(jnp.logical_and(first_y, lane == 0), 0.0, hz_new_py)
        ex_px = prev_x(ex, ex_xl)
        ey_px = prev_x(ey, ey_xl)
        hz_px = prev_x(hz, hz_xl)
        face_px = (ey - ey_px) - (next_y(ex_px, prev_x(ex_yh, corner_ex)) - ex_px)
        hz_new_px = hz_px - time_step * face_px
        hz_new_px = jnp.where(jnp.logical_and(first_x, sub == 0), 0.0, hz_new_px)
        slope_zx = next_x(ez, ez_xh) - ez
        slope_zy = next_y(ez, ez_yh) - ez
        ex_b, ey_b, hx_b, hy_b, slope_zx_b, slope_zy_b = below
        ex_a, ey_a = above
        rise_x = ex - ex_b
        rise_y = ey - ey_b
        diag_ref[z] = 1.0 + 2.0 * stiff
        if first_row:
            rise_x = jnp.where(bottom, 0.0, rise_x)
            rise_y = jnp.where(bottom, 0.0, rise_y)
            diag_ref[z] = jnp.where(bottom, 1.0 + stiff, 1.0 + 2.0 * stiff)
        quarter_z = 0.25 * zrate
        sx_ref[z] = (
            keep * ex
            + stiff * ((ex_a - ex) - rise_x)
            + curl * (hz_new - hz_new_py)
            - zrate * (hy - hy_b)
            - quarter_z * (slope_zx - slope_zx_b)
        )
        sy_ref[z] = (
            keep * ey
            + stiff * ((ey_a - ey) - rise_y)
            + zrate * (hx - hx_b)
            - quarter_z * (slope_zy - slope_zy_b)
            - curl * (hz_new - hz_new_px)
        )
        hzn_ref[z] = hz_new
        szx_ref[z] = slope_zx
        szy_ref[z] = slope_zy
        return (ex, ey, hx, hy, slope_zx, slope_zy)

    zero = jnp.zeros((rows, lanes), jnp.float32)
    below = row(0, (zero,) * 6, (e_ref[0, 1], e_ref[1, 1]), True)

    def middle(z, below):
        return row(z, below, (e_ref[0, z + 1], e_ref[1, z + 1]), False)

    below = lax.fori_loop(1, depth - 1, middle, below, unroll=True)
    row(depth - 1, below, (zero, zero), False)
    thomas_kernel(
        rate_ref.at[3], diag_ref, sx_ref, sy_ref, px_ref, py_ref, lw_ref, hw_ref, edge_ref, ur_ref
    )
    edge_ref[8] = e_ref[0, depth - 1] + (h_ref[1, depth - 1] + 0.25 * szx_ref[depth - 1]) / 32.0
    edge_ref[9] = e_ref[1, depth - 1] + (0.25 * szy_ref[depth - 1] - h_ref[0, depth - 1]) / 32.0
    edge_ref[10] = e_ref[0, 0]
    edge_ref[11] = e_ref[1, 0]


def make_sources(flags, electric, magnetic, rate_stack, x_high, x_low, y_high, y_low,
                 corner_ex, corner_ey):
    shape = jax.ShapeDtypeStruct(electric.shape[1:], jnp.float32)
    edges = jax.ShapeDtypeStruct((12,) + electric.shape[2:], jnp.float32)
    vmem = pl.BlockSpec(memory_space=pltpu.VMEM)
    smem = pl.BlockSpec(memory_space=pltpu.SMEM)
    return pl.pallas_call(
        source_kernel,
        out_shape=(shape,) * 7 + (edges,),
        in_specs=[smem] + [vmem] * 9,
        out_specs=(vmem,) * 8,
        scratch_shapes=[pltpu.VMEM(electric.shape[1:], jnp.float32)] * 4,
    )(flags, electric, magnetic, rate_stack, x_high, x_low, y_high, y_low,
      corner_ex, corner_ey)


def advance(pieces, incoming, factor):
    rows_first, rows_last, low_first, low_last, high_first, high_last = pieces
    denominator = 1.0 - low_first * factor
    offset = (rows_first + low_first[None] * incoming) / denominator[None]
    coupling = high_first / denominator
    outgoing = rows_last + low_last[None] * (incoming + factor[None] * offset)
    factor_out = low_last * factor * coupling + high_last
    return (offset, coupling, outgoing, factor_out)


def body(electric, magnetic, material, layer_map, permittivity, conductivity):
    epsilon_cell = lookup(permittivity, layer_map, material)
    sigma_cell = lookup(conductivity, layer_map, material)
    keep_rate, curl_rate, z_rate, stiffness = rates(epsilon_cell, sigma_cell)
    depth_rows, span_x, span_y = material.shape
    slab = lax.axis_index("gz")
    bottom = slab == 0
    first_x = lax.axis_index("gx") == 0
    first_y = lax.axis_index("gy") == 0
    electric_x, electric_y, electric_z = (electric[0], electric[1], electric[2])
    magnetic_x, magnetic_y, magnetic_z = (magnetic[0], magnetic[1], magnetic[2])

    x_high = from_next(jnp.stack([electric_y[:, :1], electric_z[:, :1]]), "gx")
    x_low = from_prev(
        jnp.stack([electric_x[:, -1:], electric_y[:, -1:], magnetic_z[:, -1:]]), "gx"
    )
    y_high = from_next(jnp.stack([electric_x[:, :, :1], electric_z[:, :, :1]]), "gy")
    y_low = from_prev(
        jnp.stack([electric_x[:, :, -1:], electric_y[:, :, -1:], magnetic_z[:, :, -1:]]), "gy"
    )
    corner_ex = from_diagonal(electric_x[:, -1:, :1], ("gx", "gy"), 1, -1)
    corner_ey = from_diagonal(electric_y[:, :1, -1:], ("gx", "gy"), -1, 1)

    flags = jnp.stack([bottom, first_x, first_y]).astype(jnp.int32)
    rate_stack = jnp.stack([keep_rate, curl_rate, z_rate, stiffness])
    (magnetic_z_new, slope_zx, slope_zy, partial_x, partial_y, low_weight, high_weight,
     own) = make_sources(
        flags, electric, magnetic, rate_stack, x_high, x_low, y_high, y_low,
        corner_ex, corner_ey,
    )
    slab_count = lax.axis_size("gz")
    gathered = [own]
    for shift in range(1, slab_count):
        gathered.append(
            lax.ppermute(own, "gz", [(i, (i + shift) % slab_count) for i in range(slab_count)])
        )
    gathered = jnp.stack(gathered)
    slabs = []
    for index in range(slab_count):
        chosen = lax.dynamic_index_in_dim(
            gathered, (slab - index) % slab_count, axis=0, keepdims=False
        )
        slabs.append(chosen)
    zero_pair = jnp.zeros((2,) + partial_x.shape[1:], jnp.float32)
    below_all = [zero_pair] + [slabs[index][8:10] for index in range(slab_count - 1)]
    above_all = [slabs[index][10:12] for index in range(1, slab_count)] + [zero_pair]
    for index in range(slab_count):
        chosen = slabs[index]
        low_first, low_last, high_first, high_last = chosen[4], chosen[5], chosen[6], chosen[7]
        rows_first = (
            chosen[0:2] + below_all[index] * low_first[None] + above_all[index] * high_first[None]
        )
        rows_last = (
            chosen[2:4] + below_all[index] * low_last[None] + above_all[index] * high_last[None]
        )
        slabs[index] = (rows_first, rows_last, low_first, low_last, high_first, high_last)

    incoming_all = []
    factor_all = []
    offset_all = []
    coupling_all = []
    incoming = jnp.zeros((2,) + partial_x.shape[1:], jnp.float32)
    factor = jnp.zeros_like(low_weight[0])
    for index in range(slab_count):
        if index > 0:
            incoming, factor = outgoing, factor_out
        offset, coupling, outgoing, factor_out = advance(slabs[index], incoming, factor)
        incoming_all.append(incoming)
        factor_all.append(factor)
        offset_all.append(offset)
        coupling_all.append(coupling)
    following_all = [None] * slab_count
    leading_all = [None] * slab_count
    following = jnp.zeros((2,) + partial_x.shape[1:], jnp.float32)
    for index in reversed(range(slab_count)):
        if index < slab_count - 1:
            following = leading_all[index + 1]
        following_all[index] = following
        leading_all[index] = offset_all[index] + coupling_all[index][None] * following

    def pick(values):
        return lax.dynamic_index_in_dim(jnp.stack(values), slab, axis=0, keepdims=False)

    incoming = pick(incoming_all)
    factor = pick(factor_all)
    following = pick(following_all)
    leading = pick(leading_all)
    below = pick(below_all)
    above = pick(above_all)

    previous_last = incoming + factor[None] * leading + below
    following = following + above
    electric_x_new = (
        partial_x + previous_last[0][None] * low_weight + following[0][None] * high_weight
    )
    electric_y_new = (
        partial_y + previous_last[1][None] * low_weight + following[1][None] * high_weight
    )
    sum_x = electric_x + electric_x_new
    sum_y = electric_y + electric_y_new
    top_x = following[0]
    top_y = following[1]
    rise_x = jnp.concatenate([sum_x[1:], top_x[None]], axis=0) - sum_x
    rise_y = jnp.concatenate([sum_y[1:], top_y[None]], axis=0) - sum_y
    magnetic_y_new = magnetic_y - 0.5 * z_courant * rise_x + time_step * slope_zx
    magnetic_x_new = magnetic_x - time_step * slope_zy + 0.5 * z_courant * rise_y
    before_hy = from_prev(magnetic_y_new[:, -1:, :], "gx")
    before_hx = from_prev(magnetic_x_new[:, :, -1:], "gy")
    change_hy = magnetic_y_new - jnp.concatenate([before_hy, magnetic_y_new[:, :-1]], axis=1)
    change_hx = magnetic_x_new - jnp.concatenate([before_hx, magnetic_x_new[:, :, :-1]], axis=2)
    electric_z_new = keep_rate * electric_z + curl_rate * (change_hy - change_hx)
    return (
        jnp.stack([electric_x_new, electric_y_new, electric_z_new]),
        jnp.stack([magnetic_x_new, magnetic_y_new, magnetic_z_new]),
    )


def solution(mesh):
    return jax.shard_map(
        body,
        mesh=mesh,
        in_specs=(
            P(None, "gz", "gx", "gy"),
            P(None, "gz", "gx", "gy"),
            P("gz", "gx", "gy"),
            P("gz"),
            P(),
            P(),
        ),
        out_specs=(P(None, "gz", "gx", "gy"), P(None, "gz", "gx", "gy")),
        check_vma=False,
    )
```

```python
import jax
import jax.numpy as jnp
from jax import lax
from jax.sharding import PartitionSpec as P
from jax.experimental import pallas as pl
from jax.experimental.pallas import tpu as pltpu

time_step = 0.5
z_courant = 128.0


def from_prev(block, axis):
    count = lax.axis_size(axis)
    return lax.ppermute(block, axis, [(i, i + 1) for i in range(count - 1)])


def from_next(block, axis):
    count = lax.axis_size(axis)
    return lax.ppermute(block, axis, [(i + 1, i) for i in range(count - 1)])


def from_diagonal(block, axes, step_a, step_b):
    size_a = lax.axis_size(axes[0])
    size_b = lax.axis_size(axes[1])
    pairs = []
    for a in range(size_a):
        for b in range(size_b):
            src_a, src_b = a - step_a, b - step_b
            if 0 <= src_a < size_a and 0 <= src_b < size_b:
                pairs.append((src_a * size_b + src_b, a * size_b + b))
    return lax.ppermute(block, axes, pairs)


def lookup(table_values, layer_map, material):
    kind_count, entry_count = table_values.shape
    layer_hot = layer_map[:, None] == lax.broadcasted_iota(jnp.int32, (1, kind_count), 1)
    table_rows = jnp.sum(jnp.where(layer_hot[:, :, None], table_values[None], 0.0), axis=1)
    result = jnp.zeros(material.shape, jnp.float32)
    for entry_index in range(entry_count):
        result = result + jnp.where(
            material == entry_index, table_rows[:, entry_index][:, None, None], 0.0
        )
    return result


def rates(epsilon_cell, sigma_cell):
    half_loss = 0.25 * sigma_cell / epsilon_cell
    drive_rate = 1.0 / (1.0 + half_loss)
    keep_rate = (1.0 - half_loss) * drive_rate
    curl_rate = 0.5 * drive_rate / epsilon_cell
    z_rate = z_courant * drive_rate / epsilon_cell
    stiffness = 4096.0 * drive_rate / epsilon_cell
    return (keep_rate, curl_rate, z_rate, stiffness)


def thomas_kernel(
    stiff_ref, diag_ref, sx_ref, sy_ref, px_ref, py_ref, lw_ref, hw_ref, edge_ref, ur_ref
):
    depth = stiff_ref.shape[0]
    stiff = stiff_ref[0]
    inv = 1.0 / diag_ref[0]
    ur_ref[0] = -stiff * inv
    px_ref[0] = sx_ref[0] * inv
    py_ref[0] = sy_ref[0] * inv
    lw_ref[0] = inv

    def forward(z, carry):
        upper, value_x, value_y, value_low, unused = carry
        stiff = stiff_ref[z]
        inv = 1.0 / (diag_ref[z] + stiff * upper)
        upper = -stiff * inv
        value_x = (sx_ref[z] + stiff * value_x) * inv
        value_y = (sy_ref[z] + stiff * value_y) * inv
        value_low = (stiff * value_low) * inv
        ur_ref[z] = upper
        px_ref[z] = value_x
        py_ref[z] = value_y
        lw_ref[z] = value_low
        return upper, value_x, value_y, value_low, inv

    first = (ur_ref[0], px_ref[0], py_ref[0], lw_ref[0], inv)
    last_x, last_y, last_low, last_high = lax.fori_loop(1, depth, forward, first, unroll=True)[1:]
    low_scale = stiff_ref[0]
    high_scale = stiff_ref[depth - 1]
    lw_ref[depth - 1] = low_scale * last_low
    hw_ref[depth - 1] = high_scale * last_high

    def backward(step, carry):
        z = depth - 2 - step
        next_x, next_y, next_low, next_high = carry
        upper = ur_ref[z]
        next_x = px_ref[z] - upper * next_x
        next_y = py_ref[z] - upper * next_y
        next_low = lw_ref[z] - upper * next_low
        next_high = -upper * next_high
        px_ref[z] = next_x
        py_ref[z] = next_y
        lw_ref[z] = low_scale * next_low
        hw_ref[z] = high_scale * next_high
        return next_x, next_y, next_low, next_high

    lax.fori_loop(0, depth - 1, backward, (last_x, last_y, last_low, last_high), unroll=True)
    edge_ref[0] = px_ref[0]
    edge_ref[1] = py_ref[0]
    edge_ref[2] = px_ref[depth - 1]
    edge_ref[3] = py_ref[depth - 1]
    edge_ref[4] = lw_ref[0]
    edge_ref[5] = lw_ref[depth - 1]
    edge_ref[6] = hw_ref[0]
    edge_ref[7] = hw_ref[depth - 1]


def solve_slab(stiffness, diagonal, source_x, source_y):
    shape = jax.ShapeDtypeStruct(stiffness.shape, jnp.float32)
    edges = jax.ShapeDtypeStruct((8,) + stiffness.shape[1:], jnp.float32)
    return pl.pallas_call(
        thomas_kernel,
        out_shape=(shape, shape, shape, shape, edges),
        scratch_shapes=[pltpu.VMEM(stiffness.shape, jnp.float32)],
    )(stiffness, diagonal, source_x, source_y)


def source_kernel(
    flag_ref, e_ref, h_ref, rate_ref, xh_ref, xl_ref, yh_ref, yl_ref,
    cex_ref, cey_ref, hzn_ref, szx_ref, szy_ref, px_ref, py_ref, lw_ref, hw_ref, edge_ref,
    sx_ref, sy_ref, diag_ref, ur_ref,
):
    depth, rows, lanes = sx_ref.shape
    bottom = flag_ref[0] == 1
    first_x = flag_ref[1] == 1
    first_y = flag_ref[2] == 1
    sub = lax.broadcasted_iota(jnp.int32, (rows, lanes), 0)
    lane = lax.broadcasted_iota(jnp.int32, (rows, lanes), 1)

    def full(value):
        return jnp.broadcast_to(value, (rows, lanes))

    def next_x(tile, edge):
        return jnp.where(sub == rows - 1, full(edge), pltpu.roll(tile, rows - 1, 0))

    def prev_x(tile, edge):
        return jnp.where(sub == 0, full(edge), pltpu.roll(tile, 1, 0))

    def next_y(tile, edge):
        return jnp.where(lane == lanes - 1, full(edge), pltpu.roll(tile, lanes - 1, 1))

    def prev_y(tile, edge):
        return jnp.where(lane == 0, full(edge), pltpu.roll(tile, 1, 1))

    def row(z, below, above, first_row):
        ex, ey, ez = e_ref[0, z], e_ref[1, z], e_ref[2, z]
        hx, hy, hz = h_ref[0, z], h_ref[1, z], h_ref[2, z]
        keep, curl, zrate, stiff = rate_ref[0, z], rate_ref[1, z], rate_ref[2, z], rate_ref[3, z]
        ey_xh, ez_xh = full(xh_ref[0, z]), full(xh_ref[1, z])
        ex_xl, ey_xl, hz_xl = full(xl_ref[0, z]), full(xl_ref[1, z]), full(xl_ref[2, z])
        ex_yh, ez_yh = full(yh_ref[0, z]), full(yh_ref[1, z])
        ex_yl, ey_yl, hz_yl = full(yl_ref[0, z]), full(yl_ref[1, z]), full(yl_ref[2, z])
        corner_ex = full(cex_ref[z])
        corner_ey = full(cey_ref[z])
        hz_new = hz - time_step * ((next_x(ey, ey_xh) - ey) - (next_y(ex, ex_yh) - ex))
        ex_py = prev_y(ex, ex_yl)
        ey_py = prev_y(ey, ey_yl)
        hz_py = prev_y(hz, hz_yl)
        face_py = (next_x(ey_py, prev_y(ey_xh, corner_ey)) - ey_py) - (ex - ex_py)
        hz_new_py = hz_py - time_step * face_py
        hz_new_py = jnp.where(jnp.logical_and(first_y, lane == 0), 0.0, hz_new_py)
        ex_px = prev_x(ex, ex_xl)
        ey_px = prev_x(ey, ey_xl)
        hz_px = prev_x(hz, hz_xl)
        face_px = (ey - ey_px) - (next_y(ex_px, prev_x(ex_yh, corner_ex)) - ex_px)
        hz_new_px = hz_px - time_step * face_px
        hz_new_px = jnp.where(jnp.logical_and(first_x, sub == 0), 0.0, hz_new_px)
        slope_zx = next_x(ez, ez_xh) - ez
        slope_zy = next_y(ez, ez_yh) - ez
        ex_b, ey_b, hx_b, hy_b, slope_zx_b, slope_zy_b = below
        ex_a, ey_a = above
        rise_x = ex - ex_b
        rise_y = ey - ey_b
        diag_ref[z] = 1.0 + 2.0 * stiff
        if first_row:
            rise_x = jnp.where(bottom, 0.0, rise_x)
            rise_y = jnp.where(bottom, 0.0, rise_y)
            diag_ref[z] = jnp.where(bottom, 1.0 + stiff, 1.0 + 2.0 * stiff)
        quarter_z = 0.25 * zrate
        sx_ref[z] = (
            keep * ex
            + stiff * ((ex_a - ex) - rise_x)
            + curl * (hz_new - hz_new_py)
            - zrate * (hy - hy_b)
            - quarter_z * (slope_zx - slope_zx_b)
        )
        sy_ref[z] = (
            keep * ey
            + stiff * ((ey_a - ey) - rise_y)
            + zrate * (hx - hx_b)
            - quarter_z * (slope_zy - slope_zy_b)
            - curl * (hz_new - hz_new_px)
        )
        hzn_ref[z] = hz_new
        szx_ref[z] = slope_zx
        szy_ref[z] = slope_zy
        return (ex, ey, hx, hy, slope_zx, slope_zy)

    zero = jnp.zeros((rows, lanes), jnp.float32)
    below = row(0, (zero,) * 6, (e_ref[0, 1], e_ref[1, 1]), True)

    def middle(z, below):
        return row(z, below, (e_ref[0, z + 1], e_ref[1, z + 1]), False)

    below = lax.fori_loop(1, depth - 1, middle, below, unroll=True)
    row(depth - 1, below, (zero, zero), False)
    thomas_kernel(
        rate_ref.at[3], diag_ref, sx_ref, sy_ref, px_ref, py_ref, lw_ref, hw_ref, edge_ref, ur_ref
    )
    edge_ref[8] = e_ref[0, depth - 1] + (h_ref[1, depth - 1] + 0.25 * szx_ref[depth - 1]) / 32.0
    edge_ref[9] = e_ref[1, depth - 1] + (0.25 * szy_ref[depth - 1] - h_ref[0, depth - 1]) / 32.0
    edge_ref[10] = e_ref[0, 0]
    edge_ref[11] = e_ref[1, 0]


def make_sources(flags, electric, magnetic, rate_stack, x_high, x_low, y_high, y_low,
                 corner_ex, corner_ey):
    shape = jax.ShapeDtypeStruct(electric.shape[1:], jnp.float32)
    edges = jax.ShapeDtypeStruct((12,) + electric.shape[2:], jnp.float32)
    vmem = pl.BlockSpec(memory_space=pltpu.VMEM)
    smem = pl.BlockSpec(memory_space=pltpu.SMEM)
    return pl.pallas_call(
        source_kernel,
        out_shape=(shape,) * 7 + (edges,),
        in_specs=[smem] + [vmem] * 9,
        out_specs=(vmem,) * 8,
        scratch_shapes=[pltpu.VMEM(electric.shape[1:], jnp.float32)] * 4,
    )(flags, electric, magnetic, rate_stack, x_high, x_low, y_high, y_low,
      corner_ex, corner_ey)


def advance(pieces, incoming, factor):
    rows_first, rows_last, low_first, low_last, high_first, high_last = pieces
    denominator = 1.0 - low_first * factor
    offset = (rows_first + low_first[None] * incoming) / denominator[None]
    coupling = high_first / denominator
    outgoing = rows_last + low_last[None] * (incoming + factor[None] * offset)
    factor_out = low_last * factor * coupling + high_last
    return (offset, coupling, outgoing, factor_out)


def body(electric, magnetic, material, layer_map, permittivity, conductivity):
    epsilon_cell = lookup(permittivity, layer_map, material)
    sigma_cell = lookup(conductivity, layer_map, material)
    keep_rate, curl_rate, z_rate, stiffness = rates(epsilon_cell, sigma_cell)
    depth_rows, span_x, span_y = material.shape
    slab = lax.axis_index("gz")
    bottom = slab == 0
    first_x = lax.axis_index("gx") == 0
    first_y = lax.axis_index("gy") == 0
    electric_x, electric_y, electric_z = (electric[0], electric[1], electric[2])
    magnetic_x, magnetic_y, magnetic_z = (magnetic[0], magnetic[1], magnetic[2])

    x_high = from_next(jnp.stack([electric_y[:, :1], electric_z[:, :1]]), "gx")
    x_low = from_prev(
        jnp.stack([electric_x[:, -1:], electric_y[:, -1:], magnetic_z[:, -1:]]), "gx"
    )
    y_high = from_next(jnp.stack([electric_x[:, :, :1], electric_z[:, :, :1]]), "gy")
    y_low = from_prev(
        jnp.stack([electric_x[:, :, -1:], electric_y[:, :, -1:], magnetic_z[:, :, -1:]]), "gy"
    )
    corner_ex = from_diagonal(electric_x[:, -1:, :1], ("gx", "gy"), 1, -1)
    corner_ey = from_diagonal(electric_y[:, :1, -1:], ("gx", "gy"), -1, 1)

    flags = jnp.stack([bottom, first_x, first_y]).astype(jnp.int32)
    rate_stack = jnp.stack([keep_rate, curl_rate, z_rate, stiffness])
    (magnetic_z_new, slope_zx, slope_zy, partial_x, partial_y, low_weight, high_weight,
     own) = make_sources(
        flags, electric, magnetic, rate_stack, x_high, x_low, y_high, y_low,
        corner_ex, corner_ey,
    )
    slab_count = lax.axis_size("gz")
    gathered = [own]
    for shift in range(1, slab_count):
        gathered.append(
            lax.ppermute(own, "gz", [(i, (i + shift) % slab_count) for i in range(slab_count)])
        )
    gathered = jnp.stack(gathered)
    slabs = []
    for index in range(slab_count):
        chosen = lax.dynamic_index_in_dim(
            gathered, (slab - index) % slab_count, axis=0, keepdims=False
        )
        slabs.append(chosen)
    zero_pair = jnp.zeros((2,) + partial_x.shape[1:], jnp.float32)
    below_all = [zero_pair] + [slabs[index][8:10] for index in range(slab_count - 1)]
    above_all = [slabs[index][10:12] for index in range(1, slab_count)] + [zero_pair]
    for index in range(slab_count):
        chosen = slabs[index]
        low_first, low_last, high_first, high_last = chosen[4], chosen[5], chosen[6], chosen[7]
        rows_first = (
            chosen[0:2] + below_all[index] * low_first[None] + above_all[index] * high_first[None]
        )
        rows_last = (
            chosen[2:4] + below_all[index] * low_last[None] + above_all[index] * high_last[None]
        )
        slabs[index] = (rows_first, rows_last, low_first, low_last, high_first, high_last)

    incoming_all = []
    factor_all = []
    offset_all = []
    coupling_all = []
    incoming = jnp.zeros((2,) + partial_x.shape[1:], jnp.float32)
    factor = jnp.zeros_like(low_weight[0])
    for index in range(slab_count):
        if index > 0:
            incoming, factor = outgoing, factor_out
        offset, coupling, outgoing, factor_out = advance(slabs[index], incoming, factor)
        incoming_all.append(incoming)
        factor_all.append(factor)
        offset_all.append(offset)
        coupling_all.append(coupling)
    following_all = [None] * slab_count
    leading_all = [None] * slab_count
    following = jnp.zeros((2,) + partial_x.shape[1:], jnp.float32)
    for index in reversed(range(slab_count)):
        if index < slab_count - 1:
            following = leading_all[index + 1]
        following_all[index] = following
        leading_all[index] = offset_all[index] + coupling_all[index][None] * following

    def pick(values):
        return lax.dynamic_index_in_dim(jnp.stack(values), slab, axis=0, keepdims=False)

    incoming = pick(incoming_all)
    factor = pick(factor_all)
    following = pick(following_all)
    leading = pick(leading_all)
    below = pick(below_all)
    above = pick(above_all)

    previous_last = incoming + factor[None] * leading + below
    following = following + above
    def updated(sel):
        row_sel = sel[1:]
        new_x = (
            partial_x[sel]
            + previous_last[0][row_sel][None] * low_weight[sel]
            + following[0][row_sel][None] * high_weight[sel]
        )
        new_y = (
            partial_y[sel]
            + previous_last[1][row_sel][None] * low_weight[sel]
            + following[1][row_sel][None] * high_weight[sel]
        )
        sum_x = electric_x[sel] + new_x
        sum_y = electric_y[sel] + new_y
        rise_x = jnp.concatenate([sum_x[1:], following[0][row_sel][None]], axis=0) - sum_x
        rise_y = jnp.concatenate([sum_y[1:], following[1][row_sel][None]], axis=0) - sum_y
        new_hy = magnetic_y[sel] - 0.5 * z_courant * rise_x + time_step * slope_zx[sel]
        new_hx = magnetic_x[sel] - time_step * slope_zy[sel] + 0.5 * z_courant * rise_y
        return new_x, new_y, new_hx, new_hy

    every = slice(None)
    before_hy = from_prev(updated((every, slice(-1, None), every))[3], "gx")
    before_hx = from_prev(updated((every, every, slice(-1, None)))[2], "gy")
    electric_x_new, electric_y_new, magnetic_x_new, magnetic_y_new = updated((every,) * 3)
    change_hy = magnetic_y_new - jnp.concatenate([before_hy, magnetic_y_new[:, :-1]], axis=1)
    change_hx = magnetic_x_new - jnp.concatenate([before_hx, magnetic_x_new[:, :, :-1]], axis=2)
    electric_z_new = keep_rate * electric_z + curl_rate * (change_hy - change_hx)
    return (
        jnp.stack([electric_x_new, electric_y_new, electric_z_new]),
        jnp.stack([magnetic_x_new, magnetic_y_new, magnetic_z_new]),
    )


def solution(mesh):
    return jax.shard_map(
        body,
        mesh=mesh,
        in_specs=(
            P(None, "gz", "gx", "gy"),
            P(None, "gz", "gx", "gy"),
            P("gz", "gx", "gy"),
            P("gz"),
            P(),
            P(),
        ),
        out_specs=(P(None, "gz", "gx", "gy"), P(None, "gz", "gx", "gy")),
        check_vma=False,
    )
```

```python
import jax
import jax.numpy as jnp
from jax import lax
from jax.sharding import PartitionSpec as P
from jax.experimental import pallas as pl
from jax.experimental.pallas import tpu as pltpu

time_step = 0.5
z_courant = 128.0


def from_prev(block, axis):
    count = lax.axis_size(axis)
    return lax.ppermute(block, axis, [(i, i + 1) for i in range(count - 1)])


def from_next(block, axis):
    count = lax.axis_size(axis)
    return lax.ppermute(block, axis, [(i + 1, i) for i in range(count - 1)])


def from_diagonal(block, axes, step_a, step_b):
    size_a = lax.axis_size(axes[0])
    size_b = lax.axis_size(axes[1])
    pairs = []
    for a in range(size_a):
        for b in range(size_b):
            src_a, src_b = a - step_a, b - step_b
            if 0 <= src_a < size_a and 0 <= src_b < size_b:
                pairs.append((src_a * size_b + src_b, a * size_b + b))
    return lax.ppermute(block, axes, pairs)


def lookup(table_values, layer_map, material):
    kind_count, entry_count = table_values.shape
    layer_hot = layer_map[:, None] == lax.broadcasted_iota(jnp.int32, (1, kind_count), 1)
    table_rows = jnp.sum(jnp.where(layer_hot[:, :, None], table_values[None], 0.0), axis=1)
    result = jnp.zeros(material.shape, jnp.float32)
    for entry_index in range(entry_count):
        result = result + jnp.where(
            material == entry_index, table_rows[:, entry_index][:, None, None], 0.0
        )
    return result


def rates(epsilon_cell, sigma_cell):
    half_loss = 0.25 * sigma_cell / epsilon_cell
    drive_rate = 1.0 / (1.0 + half_loss)
    keep_rate = (1.0 - half_loss) * drive_rate
    curl_rate = 0.5 * drive_rate / epsilon_cell
    z_rate = z_courant * drive_rate / epsilon_cell
    stiffness = 4096.0 * drive_rate / epsilon_cell
    return (keep_rate, curl_rate, z_rate, stiffness)


def thomas_kernel(
    stiff_ref, diag_ref, sx_ref, sy_ref, px_ref, py_ref, lw_ref, hw_ref, edge_ref, ur_ref
):
    depth = stiff_ref.shape[0]
    stiff = stiff_ref[0]
    inv = 1.0 / diag_ref[0]
    ur_ref[0] = -stiff * inv
    px_ref[0] = sx_ref[0] * inv
    py_ref[0] = sy_ref[0] * inv
    lw_ref[0] = inv

    def forward(z, carry):
        upper, value_x, value_y, value_low, unused = carry
        stiff = stiff_ref[z]
        inv = 1.0 / (diag_ref[z] + stiff * upper)
        upper = -stiff * inv
        value_x = (sx_ref[z] + stiff * value_x) * inv
        value_y = (sy_ref[z] + stiff * value_y) * inv
        value_low = (stiff * value_low) * inv
        ur_ref[z] = upper
        px_ref[z] = value_x
        py_ref[z] = value_y
        lw_ref[z] = value_low
        return upper, value_x, value_y, value_low, inv

    first = (ur_ref[0], px_ref[0], py_ref[0], lw_ref[0], inv)
    last_x, last_y, last_low, last_high = lax.fori_loop(1, depth, forward, first, unroll=True)[1:]
    low_scale = stiff_ref[0]
    high_scale = stiff_ref[depth - 1]
    lw_ref[depth - 1] = low_scale * last_low
    hw_ref[depth - 1] = high_scale * last_high

    def backward(step, carry):
        z = depth - 2 - step
        next_x, next_y, next_low, next_high = carry
        upper = ur_ref[z]
        next_x = px_ref[z] - upper * next_x
        next_y = py_ref[z] - upper * next_y
        next_low = lw_ref[z] - upper * next_low
        next_high = -upper * next_high
        px_ref[z] = next_x
        py_ref[z] = next_y
        lw_ref[z] = low_scale * next_low
        hw_ref[z] = high_scale * next_high
        return next_x, next_y, next_low, next_high

    lax.fori_loop(0, depth - 1, backward, (last_x, last_y, last_low, last_high), unroll=True)
    edge_ref[0] = px_ref[0]
    edge_ref[1] = py_ref[0]
    edge_ref[2] = px_ref[depth - 1]
    edge_ref[3] = py_ref[depth - 1]
    edge_ref[4] = lw_ref[0]
    edge_ref[5] = lw_ref[depth - 1]
    edge_ref[6] = hw_ref[0]
    edge_ref[7] = hw_ref[depth - 1]


def solve_slab(stiffness, diagonal, source_x, source_y):
    shape = jax.ShapeDtypeStruct(stiffness.shape, jnp.float32)
    edges = jax.ShapeDtypeStruct((8,) + stiffness.shape[1:], jnp.float32)
    return pl.pallas_call(
        thomas_kernel,
        out_shape=(shape, shape, shape, shape, edges),
        scratch_shapes=[pltpu.VMEM(stiffness.shape, jnp.float32)],
    )(stiffness, diagonal, source_x, source_y)


def source_kernel(
    flag_ref, e_ref, h_ref, rate_ref, xh_ref, xl_ref, yh_ref, yl_ref,
    cex_ref, cey_ref, hzn_ref, szx_ref, szy_ref, px_ref, py_ref, lw_ref, hw_ref, edge_ref,
    sx_ref, sy_ref, diag_ref, ur_ref,
):
    depth, rows, lanes = sx_ref.shape
    bottom = flag_ref[0] == 1
    first_x = flag_ref[1] == 1
    first_y = flag_ref[2] == 1
    sub = lax.broadcasted_iota(jnp.int32, (rows, lanes), 0)
    lane = lax.broadcasted_iota(jnp.int32, (rows, lanes), 1)

    def full(value):
        return jnp.broadcast_to(value, (rows, lanes))

    def next_x(tile, edge):
        return jnp.where(sub == rows - 1, full(edge), pltpu.roll(tile, rows - 1, 0))

    def prev_x(tile, edge):
        return jnp.where(sub == 0, full(edge), pltpu.roll(tile, 1, 0))

    def next_y(tile, edge):
        return jnp.where(lane == lanes - 1, full(edge), pltpu.roll(tile, lanes - 1, 1))

    def prev_y(tile, edge):
        return jnp.where(lane == 0, full(edge), pltpu.roll(tile, 1, 1))

    def row(z, below, above, first_row):
        ex, ey, ez = e_ref[0, z], e_ref[1, z], e_ref[2, z]
        hx, hy, hz = h_ref[0, z], h_ref[1, z], h_ref[2, z]
        keep, curl, zrate, stiff = rate_ref[0, z], rate_ref[1, z], rate_ref[2, z], rate_ref[3, z]
        ey_xh, ez_xh = full(xh_ref[0, z]), full(xh_ref[1, z])
        ex_xl, ey_xl, hz_xl = full(xl_ref[0, z]), full(xl_ref[1, z]), full(xl_ref[2, z])
        ex_yh, ez_yh = full(yh_ref[0, z]), full(yh_ref[1, z])
        ex_yl, ey_yl, hz_yl = full(yl_ref[0, z]), full(yl_ref[1, z]), full(yl_ref[2, z])
        corner_ex = full(cex_ref[z])
        corner_ey = full(cey_ref[z])
        hz_new = hz - time_step * ((next_x(ey, ey_xh) - ey) - (next_y(ex, ex_yh) - ex))
        ex_py = prev_y(ex, ex_yl)
        ey_py = prev_y(ey, ey_yl)
        hz_py = prev_y(hz, hz_yl)
        face_py = (next_x(ey_py, prev_y(ey_xh, corner_ey)) - ey_py) - (ex - ex_py)
        hz_new_py = hz_py - time_step * face_py
        hz_new_py = jnp.where(jnp.logical_and(first_y, lane == 0), 0.0, hz_new_py)
        ex_px = prev_x(ex, ex_xl)
        ey_px = prev_x(ey, ey_xl)
        hz_px = prev_x(hz, hz_xl)
        face_px = (ey - ey_px) - (next_y(ex_px, prev_x(ex_yh, corner_ex)) - ex_px)
        hz_new_px = hz_px - time_step * face_px
        hz_new_px = jnp.where(jnp.logical_and(first_x, sub == 0), 0.0, hz_new_px)
        slope_zx = next_x(ez, ez_xh) - ez
        slope_zy = next_y(ez, ez_yh) - ez
        ex_b, ey_b, hx_b, hy_b, slope_zx_b, slope_zy_b = below
        ex_a, ey_a = above
        rise_x = ex - ex_b
        rise_y = ey - ey_b
        diag_ref[z] = 1.0 + 2.0 * stiff
        if first_row:
            rise_x = jnp.where(bottom, 0.0, rise_x)
            rise_y = jnp.where(bottom, 0.0, rise_y)
            diag_ref[z] = jnp.where(bottom, 1.0 + stiff, 1.0 + 2.0 * stiff)
        quarter_z = 0.25 * zrate
        sx_ref[z] = (
            keep * ex
            + stiff * ((ex_a - ex) - rise_x)
            + curl * (hz_new - hz_new_py)
            - zrate * (hy - hy_b)
            - quarter_z * (slope_zx - slope_zx_b)
        )
        sy_ref[z] = (
            keep * ey
            + stiff * ((ey_a - ey) - rise_y)
            + zrate * (hx - hx_b)
            - quarter_z * (slope_zy - slope_zy_b)
            - curl * (hz_new - hz_new_px)
        )
        hzn_ref[z] = hz_new
        szx_ref[z] = slope_zx
        szy_ref[z] = slope_zy
        return (ex, ey, hx, hy, slope_zx, slope_zy)

    zero = jnp.zeros((rows, lanes), jnp.float32)
    below = row(0, (zero,) * 6, (e_ref[0, 1], e_ref[1, 1]), True)

    def middle(z, below):
        return row(z, below, (e_ref[0, z + 1], e_ref[1, z + 1]), False)

    below = lax.fori_loop(1, depth - 1, middle, below, unroll=True)
    row(depth - 1, below, (zero, zero), False)
    thomas_kernel(
        rate_ref.at[3], diag_ref, sx_ref, sy_ref, px_ref, py_ref, lw_ref, hw_ref, edge_ref, ur_ref
    )
    edge_ref[8] = e_ref[0, depth - 1] + (h_ref[1, depth - 1] + 0.25 * szx_ref[depth - 1]) / 32.0
    edge_ref[9] = e_ref[1, depth - 1] + (0.25 * szy_ref[depth - 1] - h_ref[0, depth - 1]) / 32.0
    edge_ref[10] = e_ref[0, 0]
    edge_ref[11] = e_ref[1, 0]


def make_sources(flags, electric, magnetic, rate_stack, x_high, x_low, y_high, y_low,
                 corner_ex, corner_ey):
    shape = jax.ShapeDtypeStruct(electric.shape[1:], jnp.float32)
    edges = jax.ShapeDtypeStruct((12,) + electric.shape[2:], jnp.float32)
    vmem = pl.BlockSpec(memory_space=pltpu.VMEM)
    smem = pl.BlockSpec(memory_space=pltpu.SMEM)
    return pl.pallas_call(
        source_kernel,
        out_shape=(shape,) * 7 + (edges,),
        in_specs=[smem] + [vmem] * 9,
        out_specs=(vmem,) * 8,
        scratch_shapes=[pltpu.VMEM(electric.shape[1:], jnp.float32)] * 4,
    )(flags, electric, magnetic, rate_stack, x_high, x_low, y_high, y_low,
      corner_ex, corner_ey)


def advance(pieces, incoming, factor):
    rows_first, rows_last, low_first, low_last, high_first, high_last = pieces
    denominator = 1.0 - low_first * factor
    offset = (rows_first + low_first[None] * incoming) / denominator[None]
    coupling = high_first / denominator
    outgoing = rows_last + low_last[None] * (incoming + factor[None] * offset)
    factor_out = low_last * factor * coupling + high_last
    return (offset, coupling, outgoing, factor_out)


def body(electric, magnetic, material, layer_map, permittivity, conductivity):
    epsilon_cell = lookup(permittivity, layer_map, material)
    sigma_cell = lookup(conductivity, layer_map, material)
    keep_rate, curl_rate, z_rate, stiffness = rates(epsilon_cell, sigma_cell)
    depth_rows, span_x, span_y = material.shape
    slab = lax.axis_index("gz")
    bottom = slab == 0
    first_x = lax.axis_index("gx") == 0
    first_y = lax.axis_index("gy") == 0
    electric_x, electric_y, electric_z = (electric[0], electric[1], electric[2])
    magnetic_x, magnetic_y, magnetic_z = (magnetic[0], magnetic[1], magnetic[2])

    x_high = from_next(jnp.stack([electric_y[:, :1], electric_z[:, :1]]), "gx")
    x_low = from_prev(
        jnp.stack([electric_x[:, -1:], electric_y[:, -1:], magnetic_z[:, -1:]]), "gx"
    )
    y_high = from_next(jnp.stack([electric_x[:, :, :1], electric_z[:, :, :1]]), "gy")
    y_low = from_prev(
        jnp.stack([electric_x[:, :, -1:], electric_y[:, :, -1:], magnetic_z[:, :, -1:]]), "gy"
    )
    corner_ex = from_diagonal(electric_x[:, -1:, :1], ("gx", "gy"), 1, -1)
    corner_ey = from_diagonal(electric_y[:, :1, -1:], ("gx", "gy"), -1, 1)

    flags = jnp.stack([bottom, first_x, first_y]).astype(jnp.int32)
    rate_stack = jnp.stack([keep_rate, curl_rate, z_rate, stiffness])
    (magnetic_z_new, slope_zx, slope_zy, partial_x, partial_y, low_weight, high_weight,
     own) = make_sources(
        flags, electric, magnetic, rate_stack, x_high, x_low, y_high, y_low,
        corner_ex, corner_ey,
    )
    slab_count = lax.axis_size("gz")
    gathered = [own]
    for shift in range(1, slab_count):
        gathered.append(
            lax.ppermute(own, "gz", [(i, (i + shift) % slab_count) for i in range(slab_count)])
        )
    gathered = jnp.stack(gathered)
    slabs = []
    for index in range(slab_count):
        chosen = lax.dynamic_index_in_dim(
            gathered, (slab - index) % slab_count, axis=0, keepdims=False
        )
        slabs.append(chosen)
    zero_pair = jnp.zeros((2,) + partial_x.shape[1:], jnp.float32)
    below_all = [zero_pair] + [slabs[index][8:10] for index in range(slab_count - 1)]
    above_all = [slabs[index][10:12] for index in range(1, slab_count)] + [zero_pair]
    for index in range(slab_count):
        chosen = slabs[index]
        low_first, low_last, high_first, high_last = chosen[4], chosen[5], chosen[6], chosen[7]
        rows_first = (
            chosen[0:2] + below_all[index] * low_first[None] + above_all[index] * high_first[None]
        )
        rows_last = (
            chosen[2:4] + below_all[index] * low_last[None] + above_all[index] * high_last[None]
        )
        slabs[index] = (rows_first, rows_last, low_first, low_last, high_first, high_last)

    incoming_all = []
    factor_all = []
    offset_all = []
    coupling_all = []
    incoming = jnp.zeros((2,) + partial_x.shape[1:], jnp.float32)
    factor = jnp.zeros_like(low_weight[0])
    for index in range(slab_count):
        if index > 0:
            incoming, factor = outgoing, factor_out
        offset, coupling, outgoing, factor_out = advance(slabs[index], incoming, factor)
        incoming_all.append(incoming)
        factor_all.append(factor)
        offset_all.append(offset)
        coupling_all.append(coupling)
    following_all = [None] * slab_count
    leading_all = [None] * slab_count
    following = jnp.zeros((2,) + partial_x.shape[1:], jnp.float32)
    for index in reversed(range(slab_count)):
        if index < slab_count - 1:
            following = leading_all[index + 1]
        following_all[index] = following
        leading_all[index] = offset_all[index] + coupling_all[index][None] * following

    def pick(values):
        return lax.dynamic_index_in_dim(jnp.stack(values), slab, axis=0, keepdims=False)

    incoming = pick(incoming_all)
    factor = pick(factor_all)
    following = pick(following_all)
    leading = pick(leading_all)
    below = pick(below_all)
    above = pick(above_all)

    previous_last = incoming + factor[None] * leading + below
    following = following + above
    electric_x_new = (
        partial_x + previous_last[0][None] * low_weight + following[0][None] * high_weight
    )
    electric_y_new = (
        partial_y + previous_last[1][None] * low_weight + following[1][None] * high_weight
    )
    sum_x = electric_x + electric_x_new
    sum_y = electric_y + electric_y_new
    top_x = following[0]
    top_y = following[1]
    rise_x = jnp.concatenate([sum_x[1:], top_x[None]], axis=0) - sum_x
    rise_y = jnp.concatenate([sum_y[1:], top_y[None]], axis=0) - sum_y
    magnetic_y_new = magnetic_y - 0.5 * z_courant * rise_x + time_step * slope_zx
    magnetic_x_new = magnetic_x - time_step * slope_zy + 0.5 * z_courant * rise_y
    before_hy = from_prev(magnetic_y_new[:, -1:, :], "gx")
    before_hx = from_prev(magnetic_x_new[:, :, -1].reshape(-1), "gy").reshape(
        magnetic_x_new.shape[:2] + (1,)
    )
    change_hy = magnetic_y_new - jnp.concatenate([before_hy, magnetic_y_new[:, :-1]], axis=1)
    change_hx = magnetic_x_new - jnp.concatenate([before_hx, magnetic_x_new[:, :, :-1]], axis=2)
    electric_z_new = keep_rate * electric_z + curl_rate * (change_hy - change_hx)
    return (
        jnp.stack([electric_x_new, electric_y_new, electric_z_new]),
        jnp.stack([magnetic_x_new, magnetic_y_new, magnetic_z_new]),
    )


def solution(mesh):
    return jax.shard_map(
        body,
        mesh=mesh,
        in_specs=(
            P(None, "gz", "gx", "gy"),
            P(None, "gz", "gx", "gy"),
            P("gz", "gx", "gy"),
            P("gz"),
            P(),
            P(),
        ),
        out_specs=(P(None, "gz", "gx", "gy"), P(None, "gz", "gx", "gy")),
        check_vma=False,
    )
```

```python
import jax
import jax.numpy as jnp
from jax import lax
from jax.sharding import PartitionSpec as P
from jax.experimental import pallas as pl
from jax.experimental.pallas import tpu as pltpu

time_step = 0.5
z_courant = 128.0


def from_prev(block, axis):
    count = lax.axis_size(axis)
    return lax.ppermute(block, axis, [(i, i + 1) for i in range(count - 1)])


def from_next(block, axis):
    count = lax.axis_size(axis)
    return lax.ppermute(block, axis, [(i + 1, i) for i in range(count - 1)])


def from_diagonal(block, axes, step_a, step_b):
    size_a = lax.axis_size(axes[0])
    size_b = lax.axis_size(axes[1])
    pairs = []
    for a in range(size_a):
        for b in range(size_b):
            src_a, src_b = a - step_a, b - step_b
            if 0 <= src_a < size_a and 0 <= src_b < size_b:
                pairs.append((src_a * size_b + src_b, a * size_b + b))
    return lax.ppermute(block, axes, pairs)


def lookup(table_values, layer_map, material):
    kind_count, entry_count = table_values.shape
    layer_hot = layer_map[:, None] == lax.broadcasted_iota(jnp.int32, (1, kind_count), 1)
    table_rows = jnp.sum(jnp.where(layer_hot[:, :, None], table_values[None], 0.0), axis=1)
    result = jnp.zeros(material.shape, jnp.float32)
    for entry_index in range(entry_count):
        result = result + jnp.where(
            material == entry_index, table_rows[:, entry_index][:, None, None], 0.0
        )
    return result


def rates(epsilon_cell, sigma_cell):
    half_loss = 0.25 * sigma_cell / epsilon_cell
    drive_rate = 1.0 / (1.0 + half_loss)
    keep_rate = (1.0 - half_loss) * drive_rate
    curl_rate = 0.5 * drive_rate / epsilon_cell
    z_rate = z_courant * drive_rate / epsilon_cell
    stiffness = 4096.0 * drive_rate / epsilon_cell
    return (keep_rate, curl_rate, z_rate, stiffness)


def thomas_kernel(
    stiff_ref, diag_ref, sx_ref, sy_ref, px_ref, py_ref, lw_ref, hw_ref, edge_ref, ur_ref
):
    depth = stiff_ref.shape[0]
    stiff = stiff_ref[0]
    inv = 1.0 / diag_ref[0]
    ur_ref[0] = -stiff * inv
    px_ref[0] = sx_ref[0] * inv
    py_ref[0] = sy_ref[0] * inv
    lw_ref[0] = inv

    def forward(z, carry):
        upper, value_x, value_y, value_low, _ = carry
        stiff = stiff_ref[z]
        inv = 1.0 / (diag_ref[z] + stiff * upper)
        upper = -stiff * inv
        value_x = (sx_ref[z] + stiff * value_x) * inv
        value_y = (sy_ref[z] + stiff * value_y) * inv
        value_low = (stiff * value_low) * inv
        ur_ref[z] = upper
        px_ref[z] = value_x
        py_ref[z] = value_y
        lw_ref[z] = value_low
        return upper, value_x, value_y, value_low, inv

    first = (ur_ref[0], px_ref[0], py_ref[0], lw_ref[0], inv)
    last_x, last_y, last_low, last_high = lax.fori_loop(1, depth, forward, first, unroll=True)[1:]
    low_scale = stiff_ref[0]
    high_scale = stiff_ref[depth - 1]
    lw_ref[depth - 1] = low_scale * last_low
    hw_ref[depth - 1] = high_scale * last_high

    def backward(step, carry):
        z = depth - 2 - step
        next_x, next_y, next_low, next_high = carry
        upper = ur_ref[z]
        next_x = px_ref[z] - upper * next_x
        next_y = py_ref[z] - upper * next_y
        next_low = lw_ref[z] - upper * next_low
        next_high = -upper * next_high
        px_ref[z] = next_x
        py_ref[z] = next_y
        lw_ref[z] = low_scale * next_low
        hw_ref[z] = high_scale * next_high
        return next_x, next_y, next_low, next_high

    lax.fori_loop(0, depth - 1, backward, (last_x, last_y, last_low, last_high), unroll=True)
    edge_ref[0] = px_ref[0]
    edge_ref[1] = py_ref[0]
    edge_ref[2] = px_ref[depth - 1]
    edge_ref[3] = py_ref[depth - 1]
    edge_ref[4] = lw_ref[0]
    edge_ref[5] = lw_ref[depth - 1]
    edge_ref[6] = hw_ref[0]
    edge_ref[7] = hw_ref[depth - 1]


def source_kernel(
    flag_ref, e_ref, h_ref, rate_ref, xh_ref, xl_ref, yh_ref, yl_ref,
    cex_ref, cey_ref, hzn_ref, szx_ref, szy_ref, px_ref, py_ref, lw_ref, hw_ref, edge_ref,
    sx_ref, sy_ref, diag_ref, ur_ref,
):
    depth, rows, lanes = sx_ref.shape
    bottom = flag_ref[0] == 1
    first_x = flag_ref[1] == 1
    first_y = flag_ref[2] == 1
    sub = lax.broadcasted_iota(jnp.int32, (rows, lanes), 0)
    lane = lax.broadcasted_iota(jnp.int32, (rows, lanes), 1)

    def full(value):
        return jnp.broadcast_to(value, (rows, lanes))

    def next_x(tile, edge):
        return jnp.where(sub == rows - 1, full(edge), pltpu.roll(tile, rows - 1, 0))

    def prev_x(tile, edge):
        return jnp.where(sub == 0, full(edge), pltpu.roll(tile, 1, 0))

    def next_y(tile, edge):
        return jnp.where(lane == lanes - 1, full(edge), pltpu.roll(tile, lanes - 1, 1))

    def prev_y(tile, edge):
        return jnp.where(lane == 0, full(edge), pltpu.roll(tile, 1, 1))

    def row(z, below, above, first_row):
        ex, ey, ez = e_ref[0, z], e_ref[1, z], e_ref[2, z]
        hx, hy, hz = h_ref[0, z], h_ref[1, z], h_ref[2, z]
        keep, curl, zrate, stiff = rate_ref[0, z], rate_ref[1, z], rate_ref[2, z], rate_ref[3, z]
        ey_xh, ez_xh = full(xh_ref[0, z]), full(xh_ref[1, z])
        ex_xl, ey_xl, hz_xl = full(xl_ref[0, z]), full(xl_ref[1, z]), full(xl_ref[2, z])
        ex_yh, ez_yh = full(yh_ref[0, z]), full(yh_ref[1, z])
        ex_yl, ey_yl, hz_yl = full(yl_ref[0, z]), full(yl_ref[1, z]), full(yl_ref[2, z])
        corner_ex = full(cex_ref[z])
        corner_ey = full(cey_ref[z])
        hz_new = hz - time_step * ((next_x(ey, ey_xh) - ey) - (next_y(ex, ex_yh) - ex))
        ex_py = prev_y(ex, ex_yl)
        ey_py = prev_y(ey, ey_yl)
        hz_py = prev_y(hz, hz_yl)
        face_py = (next_x(ey_py, prev_y(ey_xh, corner_ey)) - ey_py) - (ex - ex_py)
        hz_new_py = hz_py - time_step * face_py
        hz_new_py = jnp.where(jnp.logical_and(first_y, lane == 0), 0.0, hz_new_py)
        ex_px = prev_x(ex, ex_xl)
        ey_px = prev_x(ey, ey_xl)
        hz_px = prev_x(hz, hz_xl)
        face_px = (ey - ey_px) - (next_y(ex_px, prev_x(ex_yh, corner_ex)) - ex_px)
        hz_new_px = hz_px - time_step * face_px
        hz_new_px = jnp.where(jnp.logical_and(first_x, sub == 0), 0.0, hz_new_px)
        slope_zx = next_x(ez, ez_xh) - ez
        slope_zy = next_y(ez, ez_yh) - ez
        ex_b, ey_b, hx_b, hy_b, slope_zx_b, slope_zy_b = below
        ex_a, ey_a = above
        rise_x = ex - ex_b
        rise_y = ey - ey_b
        diag_ref[z] = 1.0 + 2.0 * stiff
        if first_row:
            rise_x = jnp.where(bottom, 0.0, rise_x)
            rise_y = jnp.where(bottom, 0.0, rise_y)
            diag_ref[z] = jnp.where(bottom, 1.0 + stiff, 1.0 + 2.0 * stiff)
        quarter_z = 0.25 * zrate
        sx_ref[z] = (
            keep * ex
            + stiff * ((ex_a - ex) - rise_x)
            + curl * (hz_new - hz_new_py)
            - zrate * (hy - hy_b)
            - quarter_z * (slope_zx - slope_zx_b)
        )
        sy_ref[z] = (
            keep * ey
            + stiff * ((ey_a - ey) - rise_y)
            + zrate * (hx - hx_b)
            - quarter_z * (slope_zy - slope_zy_b)
            - curl * (hz_new - hz_new_px)
        )
        hzn_ref[z] = hz_new
        szx_ref[z] = slope_zx
        szy_ref[z] = slope_zy
        return (ex, ey, hx, hy, slope_zx, slope_zy)

    zero = jnp.zeros((rows, lanes), jnp.float32)
    below = row(0, (zero,) * 6, (e_ref[0, 1], e_ref[1, 1]), True)

    def middle(z, below):
        return row(z, below, (e_ref[0, z + 1], e_ref[1, z + 1]), False)

    below = lax.fori_loop(1, depth - 1, middle, below, unroll=True)
    row(depth - 1, below, (zero, zero), False)
    thomas_kernel(
        rate_ref.at[3], diag_ref, sx_ref, sy_ref, px_ref, py_ref, lw_ref, hw_ref, edge_ref, ur_ref
    )
    edge_ref[8] = e_ref[0, depth - 1] + (h_ref[1, depth - 1] + 0.25 * szx_ref[depth - 1]) / 32.0
    edge_ref[9] = e_ref[1, depth - 1] + (0.25 * szy_ref[depth - 1] - h_ref[0, depth - 1]) / 32.0
    edge_ref[10] = e_ref[0, 0]
    edge_ref[11] = e_ref[1, 0]


def make_sources(flags, electric, magnetic, rate_stack, x_high, x_low, y_high, y_low,
                 corner_ex, corner_ey):
    shape = jax.ShapeDtypeStruct(electric.shape[1:], jnp.float32)
    edges = jax.ShapeDtypeStruct((12,) + electric.shape[2:], jnp.float32)
    vmem = pl.BlockSpec(memory_space=pltpu.VMEM)
    smem = pl.BlockSpec(memory_space=pltpu.SMEM)
    return pl.pallas_call(
        source_kernel,
        out_shape=(shape,) * 7 + (edges,),
        in_specs=[smem] + [vmem] * 9,
        out_specs=(vmem,) * 8,
        scratch_shapes=[pltpu.VMEM(electric.shape[1:], jnp.float32)] * 4,
    )(flags, electric, magnetic, rate_stack, x_high, x_low, y_high, y_low,
      corner_ex, corner_ey)


def advance(pieces, incoming, factor):
    rows_first, rows_last, low_first, low_last, high_first, high_last = pieces
    denominator = 1.0 - low_first * factor
    offset = (rows_first + low_first[None] * incoming) / denominator[None]
    coupling = high_first / denominator
    outgoing = rows_last + low_last[None] * (incoming + factor[None] * offset)
    factor_out = low_last * factor * coupling + high_last
    return (offset, coupling, outgoing, factor_out)


def step_body(electric, magnetic, material, layer_map, permittivity, conductivity):
    epsilon_cell = lookup(permittivity, layer_map, material)
    sigma_cell = lookup(conductivity, layer_map, material)
    keep_rate, curl_rate, z_rate, stiffness = rates(epsilon_cell, sigma_cell)
    slab = lax.axis_index("gz")
    bottom = slab == 0
    first_x = lax.axis_index("gx") == 0
    first_y = lax.axis_index("gy") == 0
    electric_x, electric_y, electric_z = (electric[0], electric[1], electric[2])
    magnetic_x, magnetic_y, magnetic_z = (magnetic[0], magnetic[1], magnetic[2])

    corner_ex = from_diagonal(electric_x[:, -1:, :1], ("gx", "gy"), 1, -1)
    corner_ey = from_diagonal(electric_y[:, :1, -1:], ("gx", "gy"), -1, 1)
    x_high = from_next(jnp.stack([electric_y[:, :1], electric_z[:, :1]]), "gx")
    x_low = from_prev(jnp.stack([electric_x[:, -1:], electric_y[:, -1:], magnetic_z[:, -1:]]), "gx")
    y_high = from_next(jnp.stack([electric_x[:, :, :1], electric_z[:, :, :1]]), "gy")
    y_low = from_prev(
        jnp.stack([electric_x[:, :, -1:], electric_y[:, :, -1:], magnetic_z[:, :, -1:]]),
        "gy",
    )

    flags = jnp.stack([bottom, first_x, first_y]).astype(jnp.int32)
    rate_stack = jnp.stack([keep_rate, curl_rate, z_rate, stiffness])
    (magnetic_z_new, slope_zx, slope_zy, partial_x, partial_y, low_weight, high_weight,
     own) = make_sources(
        flags, electric, magnetic, rate_stack, x_high, x_low, y_high, y_low,
        corner_ex, corner_ey,
    )
    slab_count = lax.axis_size("gz")
    gathered = [own]
    for shift in range(1, slab_count):
        gathered.append(
            lax.ppermute(own, "gz", [(i, (i + shift) % slab_count) for i in range(slab_count)])
        )
    gathered = jnp.stack(gathered)
    slabs = []
    for index in range(slab_count):
        chosen = lax.dynamic_index_in_dim(
            gathered, (slab - index) % slab_count, axis=0, keepdims=False
        )
        slabs.append(chosen)
    zero_pair = jnp.zeros((2,) + partial_x.shape[1:], jnp.float32)
    below_all = [zero_pair] + [slabs[index][8:10] for index in range(slab_count - 1)]
    above_all = [slabs[index][10:12] for index in range(1, slab_count)] + [zero_pair]
    for index in range(slab_count):
        chosen = slabs[index]
        low_first, low_last, high_first, high_last = chosen[4], chosen[5], chosen[6], chosen[7]
        rows_first = (
            chosen[0:2] + below_all[index] * low_first[None] + above_all[index] * high_first[None]
        )
        rows_last = (
            chosen[2:4] + below_all[index] * low_last[None] + above_all[index] * high_last[None]
        )
        slabs[index] = (rows_first, rows_last, low_first, low_last, high_first, high_last)

    incoming_all = []
    factor_all = []
    offset_all = []
    coupling_all = []
    incoming = jnp.zeros((2,) + partial_x.shape[1:], jnp.float32)
    factor = jnp.zeros_like(low_weight[0])
    for index in range(slab_count):
        if index > 0:
            incoming, factor = outgoing, factor_out
        offset, coupling, outgoing, factor_out = advance(slabs[index], incoming, factor)
        incoming_all.append(incoming)
        factor_all.append(factor)
        offset_all.append(offset)
        coupling_all.append(coupling)
    following_all = [None] * slab_count
    leading_all = [None] * slab_count
    following = jnp.zeros((2,) + partial_x.shape[1:], jnp.float32)
    for index in reversed(range(slab_count)):
        if index < slab_count - 1:
            following = leading_all[index + 1]
        following_all[index] = following
        leading_all[index] = offset_all[index] + coupling_all[index][None] * following

    def pick(values):
        return lax.dynamic_index_in_dim(jnp.stack(values), slab, axis=0, keepdims=False)

    incoming = pick(incoming_all)
    factor = pick(factor_all)
    following = pick(following_all)
    leading = pick(leading_all)
    below = pick(below_all)
    above = pick(above_all)

    previous_last = incoming + factor[None] * leading + below
    following = following + above
    electric_x_new = (
        partial_x + previous_last[0][None] * low_weight + following[0][None] * high_weight
    )
    electric_y_new = (
        partial_y + previous_last[1][None] * low_weight + following[1][None] * high_weight
    )
    sum_x = electric_x + electric_x_new
    sum_y = electric_y + electric_y_new
    top_x = following[0]
    top_y = following[1]
    rise_x = jnp.concatenate([sum_x[1:], top_x[None]], axis=0) - sum_x
    rise_y = jnp.concatenate([sum_y[1:], top_y[None]], axis=0) - sum_y
    magnetic_y_new = magnetic_y - 0.5 * z_courant * rise_x + time_step * slope_zx
    magnetic_x_new = magnetic_x - time_step * slope_zy + 0.5 * z_courant * rise_y
    before_hy = from_prev(magnetic_y_new[:, -1:, :], "gx")
    before_hx = from_prev(magnetic_x_new[:, :, -1:], "gy")
    change_hy = magnetic_y_new - jnp.concatenate([before_hy, magnetic_y_new[:, :-1]], axis=1)
    change_hx = magnetic_x_new - jnp.concatenate([before_hx, magnetic_x_new[:, :, :-1]], axis=2)
    electric_z_new = keep_rate * electric_z + curl_rate * (change_hy - change_hx)
    return (
        jnp.stack([electric_x_new, electric_y_new, electric_z_new]),
        jnp.stack([magnetic_x_new, magnetic_y_new, magnetic_z_new]),
    )


def solution(mesh):
    return jax.shard_map(
        step_body,
        mesh=mesh,
        in_specs=(
            P(None, "gz", "gx", "gy"),
            P(None, "gz", "gx", "gy"),
            P("gz", "gx", "gy"),
            P("gz"),
            P(),
            P(),
        ),
        out_specs=(P(None, "gz", "gx", "gy"), P(None, "gz", "gx", "gy")),
        check_vma=False,
    )
```

```python
import jax
import jax.numpy as jnp
from jax import lax
from jax.sharding import PartitionSpec as P
from jax.experimental import pallas as pl
from jax.experimental.pallas import tpu as pltpu

time_step = 0.5
z_courant = 128.0


def from_prev(block, axis):
    count = lax.axis_size(axis)
    return lax.ppermute(block, axis, [(i, i + 1) for i in range(count - 1)])


def from_next(block, axis):
    count = lax.axis_size(axis)
    return lax.ppermute(block, axis, [(i + 1, i) for i in range(count - 1)])


def from_diagonal(block, axes, step_a, step_b):
    size_a = lax.axis_size(axes[0])
    size_b = lax.axis_size(axes[1])
    pairs = []
    for a in range(size_a):
        for b in range(size_b):
            src_a, src_b = a - step_a, b - step_b
            if 0 <= src_a < size_a and 0 <= src_b < size_b:
                pairs.append((src_a * size_b + src_b, a * size_b + b))
    return lax.ppermute(block, axes, pairs)


def lookup(table_values, layer_map, material):
    kind_count, entry_count = table_values.shape
    layer_hot = layer_map[:, None] == lax.broadcasted_iota(jnp.int32, (1, kind_count), 1)
    table_rows = jnp.sum(jnp.where(layer_hot[:, :, None], table_values[None], 0.0), axis=1)
    result = jnp.zeros(material.shape, jnp.float32)
    for entry_index in range(entry_count):
        result = result + jnp.where(
            material == entry_index, table_rows[:, entry_index][:, None, None], 0.0
        )
    return result


def rates(epsilon_cell, sigma_cell):
    half_loss = 0.25 * sigma_cell / epsilon_cell
    drive_rate = 1.0 / (1.0 + half_loss)
    keep_rate = (1.0 - half_loss) * drive_rate
    curl_rate = 0.5 * drive_rate / epsilon_cell
    z_rate = z_courant * drive_rate / epsilon_cell
    stiffness = 4096.0 * drive_rate / epsilon_cell
    return (keep_rate, curl_rate, z_rate, stiffness)


def thomas_kernel(
    stiff_ref, diag_ref, sx_ref, sy_ref, px_ref, py_ref, lw_ref, hw_ref, edge_ref, ur_ref
):
    depth = stiff_ref.shape[0]
    stiff = stiff_ref[0]
    inv = 1.0 / diag_ref[0]
    ur_ref[0] = -stiff * inv
    px_ref[0] = sx_ref[0] * inv
    py_ref[0] = sy_ref[0] * inv
    lw_ref[0] = inv

    def forward(z, carry):
        upper, value_x, value_y, value_low, unused = carry
        stiff = stiff_ref[z]
        inv = 1.0 / (diag_ref[z] + stiff * upper)
        upper = -stiff * inv
        value_x = (sx_ref[z] + stiff * value_x) * inv
        value_y = (sy_ref[z] + stiff * value_y) * inv
        value_low = (stiff * value_low) * inv
        ur_ref[z] = upper
        px_ref[z] = value_x
        py_ref[z] = value_y
        lw_ref[z] = value_low
        return upper, value_x, value_y, value_low, inv

    first = (ur_ref[0], px_ref[0], py_ref[0], lw_ref[0], inv)
    last_x, last_y, last_low, last_high = lax.fori_loop(1, depth, forward, first, unroll=True)[1:]
    low_scale = stiff_ref[0]
    high_scale = stiff_ref[depth - 1]
    lw_ref[depth - 1] = low_scale * last_low
    hw_ref[depth - 1] = high_scale * last_high

    def backward(step, carry):
        z = depth - 2 - step
        next_x, next_y, next_low, next_high = carry
        upper = ur_ref[z]
        next_x = px_ref[z] - upper * next_x
        next_y = py_ref[z] - upper * next_y
        next_low = lw_ref[z] - upper * next_low
        next_high = -upper * next_high
        px_ref[z] = next_x
        py_ref[z] = next_y
        lw_ref[z] = low_scale * next_low
        hw_ref[z] = high_scale * next_high
        return next_x, next_y, next_low, next_high

    lax.fori_loop(0, depth - 1, backward, (last_x, last_y, last_low, last_high), unroll=True)
    edge_ref[0] = px_ref[0]
    edge_ref[1] = py_ref[0]
    edge_ref[2] = px_ref[depth - 1]
    edge_ref[3] = py_ref[depth - 1]
    edge_ref[4] = lw_ref[0]
    edge_ref[5] = lw_ref[depth - 1]
    edge_ref[6] = hw_ref[0]
    edge_ref[7] = hw_ref[depth - 1]


def solve_slab(stiffness, diagonal, source_x, source_y):
    shape = jax.ShapeDtypeStruct(stiffness.shape, jnp.float32)
    edges = jax.ShapeDtypeStruct((8,) + stiffness.shape[1:], jnp.float32)
    return pl.pallas_call(
        thomas_kernel,
        out_shape=(shape, shape, shape, shape, edges),
        scratch_shapes=[pltpu.VMEM(stiffness.shape, jnp.float32)],
    )(stiffness, diagonal, source_x, source_y)


def source_kernel(
    flag_ref, e_ref, h_ref, rate_ref, xh_ref, xl_ref, yh_ref, yl_ref,
    cex_ref, cey_ref, hzn_ref, szx_ref, szy_ref, px_ref, py_ref, lw_ref, hw_ref, edge_ref,
    sx_ref, sy_ref, diag_ref, ur_ref,
):
    depth, rows, lanes = sx_ref.shape
    bottom = flag_ref[0] == 1
    first_x = flag_ref[1] == 1
    first_y = flag_ref[2] == 1
    sub = lax.broadcasted_iota(jnp.int32, (rows, lanes), 0)
    lane = lax.broadcasted_iota(jnp.int32, (rows, lanes), 1)

    def full(value):
        return jnp.broadcast_to(value, (rows, lanes))

    def next_x(tile, edge):
        return jnp.where(sub == rows - 1, full(edge), pltpu.roll(tile, rows - 1, 0))

    def prev_x(tile, edge):
        return jnp.where(sub == 0, full(edge), pltpu.roll(tile, 1, 0))

    def next_y(tile, edge):
        return jnp.where(lane == lanes - 1, full(edge), pltpu.roll(tile, lanes - 1, 1))

    def prev_y(tile, edge):
        return jnp.where(lane == 0, full(edge), pltpu.roll(tile, 1, 1))

    def row(z, below, above, first_row):
        ex, ey, ez = e_ref[0, z], e_ref[1, z], e_ref[2, z]
        hx, hy, hz = h_ref[0, z], h_ref[1, z], h_ref[2, z]
        keep, curl, zrate, stiff = rate_ref[0, z], rate_ref[1, z], rate_ref[2, z], rate_ref[3, z]
        ey_xh, ez_xh = full(xh_ref[0, z]), full(xh_ref[1, z])
        ex_xl, ey_xl, hz_xl = full(xl_ref[0, z]), full(xl_ref[1, z]), full(xl_ref[2, z])
        ex_yh, ez_yh = full(yh_ref[0, z]), full(yh_ref[1, z])
        ex_yl, ey_yl, hz_yl = full(yl_ref[0, z]), full(yl_ref[1, z]), full(yl_ref[2, z])
        corner_ex = full(cex_ref[z])
        corner_ey = full(cey_ref[z])
        hz_new = hz - time_step * ((next_x(ey, ey_xh) - ey) - (next_y(ex, ex_yh) - ex))
        ex_py = prev_y(ex, ex_yl)
        ey_py = prev_y(ey, ey_yl)
        hz_py = prev_y(hz, hz_yl)
        face_py = (next_x(ey_py, prev_y(ey_xh, corner_ey)) - ey_py) - (ex - ex_py)
        hz_new_py = hz_py - time_step * face_py
        hz_new_py = jnp.where(jnp.logical_and(first_y, lane == 0), 0.0, hz_new_py)
        ex_px = prev_x(ex, ex_xl)
        ey_px = prev_x(ey, ey_xl)
        hz_px = prev_x(hz, hz_xl)
        face_px = (ey - ey_px) - (next_y(ex_px, prev_x(ex_yh, corner_ex)) - ex_px)
        hz_new_px = hz_px - time_step * face_px
        hz_new_px = jnp.where(jnp.logical_and(first_x, sub == 0), 0.0, hz_new_px)
        slope_zx = next_x(ez, ez_xh) - ez
        slope_zy = next_y(ez, ez_yh) - ez
        ex_b, ey_b, hx_b, hy_b, slope_zx_b, slope_zy_b = below
        ex_a, ey_a = above
        rise_x = ex - ex_b
        rise_y = ey - ey_b
        diag_ref[z] = 1.0 + 2.0 * stiff
        if first_row:
            rise_x = jnp.where(bottom, 0.0, rise_x)
            rise_y = jnp.where(bottom, 0.0, rise_y)
            diag_ref[z] = jnp.where(bottom, 1.0 + stiff, 1.0 + 2.0 * stiff)
        quarter_z = 0.25 * zrate
        sx_ref[z] = (
            keep * ex
            + stiff * ((ex_a - ex) - rise_x)
            + curl * (hz_new - hz_new_py)
            - zrate * (hy - hy_b)
            - quarter_z * (slope_zx - slope_zx_b)
        )
        sy_ref[z] = (
            keep * ey
            + stiff * ((ey_a - ey) - rise_y)
            + zrate * (hx - hx_b)
            - quarter_z * (slope_zy - slope_zy_b)
            - curl * (hz_new - hz_new_px)
        )
        hzn_ref[z] = hz_new
        szx_ref[z] = slope_zx
        szy_ref[z] = slope_zy
        return (ex, ey, hx, hy, slope_zx, slope_zy)

    zero = jnp.zeros((rows, lanes), jnp.float32)
    below = row(0, (zero,) * 6, (e_ref[0, 1], e_ref[1, 1]), True)

    def middle(z, below):
        return row(z, below, (e_ref[0, z + 1], e_ref[1, z + 1]), False)

    below = lax.fori_loop(1, depth - 1, middle, below, unroll=True)
    row(depth - 1, below, (zero, zero), False)
    thomas_kernel(
        rate_ref.at[3], diag_ref, sx_ref, sy_ref, px_ref, py_ref, lw_ref, hw_ref, edge_ref, ur_ref
    )
    edge_ref[8] = e_ref[0, depth - 1] + (h_ref[1, depth - 1] + 0.25 * szx_ref[depth - 1]) / 32.0
    edge_ref[9] = e_ref[1, depth - 1] + (0.25 * szy_ref[depth - 1] - h_ref[0, depth - 1]) / 32.0
    edge_ref[10] = e_ref[0, 0]
    edge_ref[11] = e_ref[1, 0]


def make_sources(flags, electric, magnetic, rate_stack, x_high, x_low, y_high, y_low,
                 corner_ex, corner_ey):
    shape = jax.ShapeDtypeStruct(electric.shape[1:], jnp.float32)
    edges = jax.ShapeDtypeStruct((12,) + electric.shape[2:], jnp.float32)
    vmem = pl.BlockSpec(memory_space=pltpu.VMEM)
    smem = pl.BlockSpec(memory_space=pltpu.SMEM)
    return pl.pallas_call(
        source_kernel,
        out_shape=(shape,) * 7 + (edges,),
        in_specs=[smem] + [vmem] * 9,
        out_specs=(vmem,) * 8,
        scratch_shapes=[pltpu.VMEM(electric.shape[1:], jnp.float32)] * 4,
    )(flags, electric, magnetic, rate_stack, x_high, x_low, y_high, y_low,
      corner_ex, corner_ey)


def advance(pieces, incoming, factor):
    rows_first, rows_last, low_first, low_last, high_first, high_last = pieces
    denominator = 1.0 - low_first * factor
    offset = (rows_first + low_first[None] * incoming) / denominator[None]
    coupling = high_first / denominator
    outgoing = rows_last + low_last[None] * (incoming + factor[None] * offset)
    factor_out = low_last * factor * coupling + high_last
    return (offset, coupling, outgoing, factor_out)


def body(electric, magnetic, material, layer_map, permittivity, conductivity):
    epsilon_cell = lookup(permittivity, layer_map, material)
    sigma_cell = lookup(conductivity, layer_map, material)
    keep_rate, curl_rate, z_rate, stiffness = rates(epsilon_cell, sigma_cell)
    depth_rows, span_x, span_y = material.shape
    slab = lax.axis_index("gz")
    bottom = slab == 0
    first_x = lax.axis_index("gx") == 0
    first_y = lax.axis_index("gy") == 0
    electric_x, electric_y, electric_z = (electric[0], electric[1], electric[2])
    magnetic_x, magnetic_y, magnetic_z = (magnetic[0], magnetic[1], magnetic[2])

    x_high = from_next(jnp.stack([electric_y[:, :1], electric_z[:, :1]]), "gx")
    x_low = from_prev(
        jnp.stack([electric_x[:, -1:], electric_y[:, -1:], magnetic_z[:, -1:]]), "gx"
    )
    y_high = from_next(jnp.stack([electric_x[:, :, :1], electric_z[:, :, :1]]), "gy")
    y_low = from_prev(
        jnp.stack([electric_x[:, :, -1:], electric_y[:, :, -1:], magnetic_z[:, :, -1:]]), "gy"
    )
    corner_ex = from_diagonal(electric_x[:, -1:, :1], ("gx", "gy"), 1, -1)
    corner_ey = from_diagonal(electric_y[:, :1, -1:], ("gx", "gy"), -1, 1)

    flags = jnp.stack([bottom, first_x, first_y]).astype(jnp.int32)
    rate_stack = jnp.stack([keep_rate, curl_rate, z_rate, stiffness])
    (magnetic_z_new, slope_zx, slope_zy, partial_x, partial_y, low_weight, high_weight,
     own) = make_sources(
        flags, electric, magnetic, rate_stack, x_high, x_low, y_high, y_low,
        corner_ex, corner_ey,
    )
    slab_count = lax.axis_size("gz")
    gathered = [own]
    for shift in range(1, slab_count):
        gathered.append(
            lax.ppermute(own, "gz", [(i, (i + shift) % slab_count) for i in range(slab_count)])
        )
    gathered = jnp.stack(gathered)
    slabs = []
    for index in range(slab_count):
        chosen = lax.dynamic_index_in_dim(
            gathered, (slab - index) % slab_count, axis=0, keepdims=False
        )
        slabs.append(chosen)
    zero_pair = jnp.zeros((2,) + partial_x.shape[1:], jnp.float32)
    below_all = [zero_pair] + [slabs[index][8:10] for index in range(slab_count - 1)]
    above_all = [slabs[index][10:12] for index in range(1, slab_count)] + [zero_pair]
    for index in range(slab_count):
        chosen = slabs[index]
        low_first, low_last, high_first, high_last = chosen[4], chosen[5], chosen[6], chosen[7]
        rows_first = (
            chosen[0:2] + below_all[index] * low_first[None] + above_all[index] * high_first[None]
        )
        rows_last = (
            chosen[2:4] + below_all[index] * low_last[None] + above_all[index] * high_last[None]
        )
        slabs[index] = (rows_first, rows_last, low_first, low_last, high_first, high_last)

    incoming_all = []
    factor_all = []
    offset_all = []
    coupling_all = []
    incoming = jnp.zeros((2,) + partial_x.shape[1:], jnp.float32)
    factor = jnp.zeros_like(low_weight[0])
    for index in range(slab_count):
        if index > 0:
            incoming, factor = outgoing, factor_out
        offset, coupling, outgoing, factor_out = advance(slabs[index], incoming, factor)
        incoming_all.append(incoming)
        factor_all.append(factor)
        offset_all.append(offset)
        coupling_all.append(coupling)
    following_all = [None] * slab_count
    leading_all = [None] * slab_count
    following = jnp.zeros((2,) + partial_x.shape[1:], jnp.float32)
    for index in reversed(range(slab_count)):
        if index < slab_count - 1:
            following = leading_all[index + 1]
        following_all[index] = following
        leading_all[index] = offset_all[index] + coupling_all[index][None] * following

    def pick(values):
        return lax.dynamic_index_in_dim(jnp.stack(values), slab, axis=0, keepdims=False)

    incoming = pick(incoming_all)
    factor = pick(factor_all)
    following = pick(following_all)
    leading = pick(leading_all)
    below = pick(below_all)
    above = pick(above_all)

    previous_last = incoming + factor[None] * leading + below
    following = following + above
    electric_x_new = (
        partial_x + previous_last[0][None] * low_weight + following[0][None] * high_weight
    )
    electric_y_new = (
        partial_y + previous_last[1][None] * low_weight + following[1][None] * high_weight
    )
    sum_x = electric_x + electric_x_new
    sum_y = electric_y + electric_y_new
    top_x = following[0]
    top_y = following[1]
    rise_x = jnp.concatenate([sum_x[1:], top_x[None]], axis=0) - sum_x
    rise_y = jnp.concatenate([sum_y[1:], top_y[None]], axis=0) - sum_y
    magnetic_y_new = magnetic_y - 0.5 * z_courant * rise_x + time_step * slope_zx
    magnetic_x_new = magnetic_x - time_step * slope_zy + 0.5 * z_courant * rise_y
    before_hy = from_prev(magnetic_y_new[:, -1:, :], "gx")
    before_hx = from_prev(magnetic_x_new[:, :, -1:], "gy")
    change_hy = magnetic_y_new - jnp.concatenate([before_hy, magnetic_y_new[:, :-1]], axis=1)
    change_hx = magnetic_x_new - jnp.concatenate([before_hx, magnetic_x_new[:, :, :-1]], axis=2)
    electric_z_new = keep_rate * electric_z + curl_rate * (change_hy - change_hx)
    electric_next = jnp.stack([electric_x_new, electric_y_new, jnp.zeros_like(electric_z)])
    return (
        electric_next.at[2].set(electric_z_new),
        jnp.stack([magnetic_x_new, magnetic_y_new, magnetic_z_new]),
    )


def solution(mesh):
    return jax.shard_map(
        body,
        mesh=mesh,
        in_specs=(
            P(None, "gz", "gx", "gy"),
            P(None, "gz", "gx", "gy"),
            P("gz", "gx", "gy"),
            P("gz"),
            P(),
            P(),
        ),
        out_specs=(P(None, "gz", "gx", "gy"), P(None, "gz", "gx", "gy")),
        check_vma=False,
    )
```
